128 devices in a mesh: member: 8 (over y, core), lat: 16 (over x, z).
Axes of the slice: x: 4, y: 4, z: 4, core: 2. Of those that a mesh axis runs over, the one named last changes fastest.
Arguments:
- ensemble: float32 [640, 64, 1024], P('member', 'lat'), may hold values from -6 to 6
- obs_cell: int32 [128, 128], P(('member', 'lat')), may hold values from 0 to 511
- obs_value: float32 [128, 128], P(('member', 'lat')), may hold values from -8 to 8
- obs_var: float32 [128, 128], P(('member', 'lat')), may hold values from 0.5 to 8
- patch_rows: int32 [128, 2], P(('member', 'lat')), may hold values from 1 to 48, 64 in all within a row
Outputs:
- analysis: float32 [640, 64, 1024], P('member', 'lat')
The draws below stay inside these ranges and needn't reach their ends.
Inputs may be any that keep to these rules, and one draw needn't show every extreme that they name: `patch_rows`: each server's 2 patch lengths sum to 64.
All inputs are finite; a program needn't handle non-finite values. Where the reference program divides by a largest or mean magnitude, that divisor is 1e-20 or more.
Results may differ from the reference program's by a relative error of at most 0.0003.
Values sent between devices are 32-bit elements; how exact they have to be, the bound alone decides.
No kernel may reach another device: no remote copies, remote signals or barrier semaphores. Data moves between devices by JAX's collectives and lax.ppermute only.
A program may use at most 64 MiB of HBM per device.

```python
import math
import jax
import jax.numpy as jnp
import numpy as np
from jax import lax

K = 640
LON_DEV = 8
OBS_DEV = 128
PATCH_DEV = 2
NS_ITERS = 3
STEPS = 4
NLAT = 64
NLON = 1024
DEVICES = 128


def place_ends(drawn, own_key, low, top_value):
    longest = drawn.shape.index(max(drawn.shape))
    spots = []
    for shift in (0, 1):
        where = [jax.random.randint(jax.random.fold_in(own_key, axis), (), 0, length) for axis, length in enumerate(drawn.shape)]
        where[longest] = (where[longest] + shift) % drawn.shape[longest]
        spots.append(tuple(where))
    return drawn.at[spots[0]].set(low).at[spots[1]].set(top_value)


def steps_of(key, extent, shards, smallest, largest):
    level = 1.0
    for position, blocks in shards:
        draws = jax.random.uniform(jax.random.fold_in(jax.random.fold_in(key, 6), position), (blocks,), jnp.float32, smallest / len(shards), largest / len(shards))
        level = level * jnp.repeat(jnp.exp(draws), extent[position] // blocks).reshape((-1,) + (1,) * (len(extent) - 1 - position))
    return level


def profile(count, total, most, skew):
    portions = [(1 << 20) // math.isqrt(grade ** skew) + 1 for grade in range(2, count + 1)]
    rest, counts = total - most - (count - 1), [1] * (count - 1)
    while rest > 0:
        free = [i for i in range(count - 1) if counts[i] < most]
        pool, budget = sum([portions[i] for i in free]), rest
        for i in free:
            more = min(most - counts[i], max(1, budget * portions[i] // pool), rest)
            counts[i] = counts[i] + more
            rest = rest - more
    return np.array([most] + counts)


def ragged_sizes(own_key, amount, total, limit, skew):
    if amount == 2:
        one = jax.random.randint(own_key, (), max(1, total - limit), min(limit, total - 1) + 1)
        return jnp.stack([one, total - one])
    sizes = jnp.asarray(profile(amount, total, limit, skew), jnp.int32)
    twos = (amount - 1) // 2
    source_of, taker = sizes[1:1 + 2 * twos:2], sizes[2:2 + 2 * twos:2]
    slack = jnp.minimum(source_of - 1, limit - taker)
    shifted = jax.random.randint(jax.random.fold_in(own_key, 1), (twos,), 0, 1 << 20) % (slack + 1)
    sizes = sizes.at[1:1 + 2 * twos:2].set(source_of - shifted).at[2:2 + 2 * twos:2].set(taker + shifted)
    return sizes[jax.random.permutation(jax.random.fold_in(own_key, 2), amount)]


def gaussian(rng, shape, scale, limit, cuts=(), kind=jnp.bfloat16):
    values = jax.random.normal(rng, shape, jnp.float32) * scale
    if len(cuts) > 0:
        values = steps_of(rng, shape, cuts, -0.22, 0.18) * values
    return jnp.clip(values, min=-limit, max=limit).astype(kind)


def setup_inputs(seed: int = 0) -> dict:
    key_list = jax.random.split(jax.random.key(seed), 6)
    return {
        "ensemble": gaussian(key_list[0], (K, NLAT, NLON), 1.0, 6.0, ((0, 8), (1, 16)), jnp.float32),
        "obs_cell": place_ends(jax.random.randint(key_list[1], (DEVICES, OBS_DEV), 0, NLAT * LON_DEV), jax.random.fold_in(key_list[1], 1), 0, (NLAT * LON_DEV) - 1).astype(jnp.int32),
        "obs_value": gaussian(key_list[2], (DEVICES, OBS_DEV), 1.5, 8.0, ((0, 128),), jnp.float32),
        "obs_var": jnp.clip(jnp.exp(math.log(8.0) - 2.7725887 * jax.random.uniform(key_list[3], (DEVICES, OBS_DEV), jnp.float32) ** steps_of(key_list[3], (DEVICES, OBS_DEV), ((0, 128),), -0.2, 0.2)), 0.5, 8.0),
        "patch_rows": jax.vmap(lambda own: ragged_sizes(own, PATCH_DEV, NLAT, NLAT - NLAT // 4, 0))(jax.random.split(key_list[4], DEVICES)).reshape((DEVICES, PATCH_DEV)).astype(jnp.int32),
    }


lat_coeff = 0.4
lon_coeff = 0.05
advect_coeff = 0.1

def matmul(left, right):
    return jnp.dot(left, right, precision=lax.Precision.HIGHEST, preferred_element_type=jnp.float32)

def advance(padded):
    centre = padded[:, 1:-1]
    northern = padded[:, :-2]
    southern = padded[:, 2:]
    eastern = jnp.roll(centre, -1, axis=2)
    western = jnp.roll(centre, 1, axis=2)
    return centre + lat_coeff * (northern + southern - 2.0 * centre) + lon_coeff * (eastern + western - 2.0 * centre) - advect_coeff * centre * (eastern - western)

def observe(states, cell_index, values):
    observed = jnp.take(states, cell_index, axis=1)
    obs_mean = lax.optimization_barrier(jnp.mean(observed, axis=0))
    return (observed - obs_mean, values - obs_mean)

def localize(obs_rows, rel_cols, first_row, row_count, lat_scale, width_cols):
    lower = first_row.astype(jnp.float32)
    upper = lower + row_count.astype(jnp.float32) - 1.0
    lat_gap = jnp.maximum(jnp.maximum(lower - obs_rows, obs_rows - upper), 0.0) / lat_scale
    lon_gap = jnp.maximum(jnp.maximum(-rel_cols, rel_cols - (width_cols - 1.0)), 0.0) / width_cols
    return jnp.exp(-lat_gap * lat_gap - lon_gap * lon_gap)

def inverse_root(gram_matrix):
    bound = jnp.max(lax.optimization_barrier(jnp.sum(jnp.abs(gram_matrix), axis=1)))
    identity = jnp.eye(gram_matrix.shape[0], dtype=jnp.float32)
    iterate = gram_matrix / bound
    result = identity
    for turn_index in range(NS_ITERS):
        middle = 1.5 * identity - 0.5 * matmul(result, iterate)
        result = matmul(middle, result)
        if turn_index + 1 < NS_ITERS:
            iterate = matmul(iterate, middle)
    return result / jnp.sqrt(bound)

def analyse(states, spread, obs_meta, lengths, width_cols):
    members = states.shape[0]
    cell_total = states.shape[1]
    lat_total = cell_total // width_cols
    state_mean = lax.optimization_barrier(jnp.mean(states, axis=0))
    anomaly = states - state_mean
    starts = jnp.cumsum(lengths) - lengths
    cell_rows = jnp.arange(cell_total, dtype=jnp.int32) // width_cols
    identity = jnp.eye(members, dtype=jnp.float32)
    result = jnp.broadcast_to(state_mean, states.shape)
    for patch in range(lengths.shape[0]):
        weights = localize(obs_meta[2], obs_meta[3], starts[patch], lengths[patch], lat_total / 4.0, float(width_cols)) / obs_meta[1]
        weighted = spread * weights
        gram_matrix = (members - 1.0) * identity + matmul(weighted, spread.T)
        root = inverse_root(gram_matrix)
        drive = matmul(weighted, obs_meta[0])
        mean_weights = matmul(root, matmul(root, drive))
        transform = jnp.sqrt(members - 1.0) * root + mean_weights[:, None]
        update = matmul(transform.T, anomaly)
        cell_mask = (cell_rows >= starts[patch]) & (cell_rows < starts[patch] + lengths[patch])
        result = result + jnp.where(cell_mask[None, :], update, 0.0)
    return result

def reference(ensemble, obs_cell, obs_value, obs_var, patch_rows):
    fields = ensemble
    for _ in range(STEPS):
        fields = advance(jnp.pad(fields, ((0, 0), (1, 1), (0, 0))))
    servers = NLON // LON_DEV
    strips = fields.reshape(K, NLAT, servers, LON_DEV).transpose(2, 0, 1, 3).reshape(servers, K, NLAT * LON_DEV)

    def prepare(server):
        return observe(strips[server], obs_cell[server], obs_value[server])
    spreads, innovs = lax.map(prepare, jnp.arange(servers, dtype=jnp.int32))
    obs_rows = (obs_cell // LON_DEV).astype(jnp.float32)
    obs_cols = (obs_cell % LON_DEV).astype(jnp.float32)
    offsets = jnp.array([-1.0, 0.0, 1.0], jnp.float32)[:, None] * LON_DEV

    def solve(server):
        beside_all = jnp.stack([(server - 1) % servers, server, (server + 1) % servers]).astype(jnp.int32)
        near_spread = spreads[beside_all].transpose(1, 0, 2).reshape(K, 3 * OBS_DEV)
        obs_meta = jnp.stack([innovs[beside_all].reshape(-1), obs_var[beside_all].reshape(-1), obs_rows[beside_all].reshape(-1), (obs_cols[beside_all] + offsets).reshape(-1)])
        return analyse(strips[server], near_spread, obs_meta, patch_rows[server], LON_DEV)
    analysed = lax.map(solve, jnp.arange(servers, dtype=jnp.int32))
    return analysed.reshape(servers, K, NLAT, LON_DEV).transpose(1, 2, 0, 3).reshape(K, NLAT, NLON)
```

```python
import functools

import jax
import jax.numpy as jnp
import numpy as np
from jax import lax
from jax.experimental import pallas as pl
from jax.experimental.pallas import tpu as pltpu
from jax.sharding import PartitionSpec as P

BOTH = ("member", "lat")
K = 640
MEM = 80
NOBS = 384
CELLS = 512
F32 = jnp.float32
BF16 = jnp.bfloat16


def strip_places():
    columns = []
    for x in range(4):
        for y in range(4) if x % 2 == 0 else range(3, -1, -1):
            columns.append((x, y))
    places, z = [], 0
    for x, y in columns:
        for k in range(4):
            for core in range(2):
                places.append((y * 2 + core) * 16 + x * 4 + (z + k) % 4)
        z = (z + 3) % 4
    return places


PLACE = strip_places()


def lane_iota(rows=8):
    return lax.broadcasted_iota(jnp.int32, (rows, 128), 1)


def roll(value, shift):
    return pltpu.roll(value, shift % value.shape[-1], value.ndim - 1)


def block_transpose(values, size):
    values = list(values)
    count = len(values)
    lane = lane_iota()
    dist = 1
    while dist < count:
        low = (lane // (size * dist)) % 2 == 0
        for i in range(count):
            if i & dist:
                continue
            a, b = values[i], values[i + dist]
            values[i] = jnp.where(low, a, roll(b, size * dist))
            values[i + dist] = jnp.where(low, roll(a, -size * dist), b)
        dist *= 2
    return values


def pack_kernel(ens_ref, cell_ref, value_ref, var_ref, rows_ref, out_ref, meta_ref):
    meta_ref[...] = jnp.zeros_like(meta_ref)
    meta_ref[0:1, :] = cell_ref[...].astype(F32)
    meta_ref[1:2, :] = value_ref[...]
    meta_ref[2:3, :] = var_ref[...]
    meta_ref[3:4, :] = jnp.broadcast_to(rows_ref[0:1, 0:1].astype(F32), (1, 128))

    def body(i, carry):
        wide = []
        for h in range(2):
            for r in range(4):
                src = ens_ref[r, pl.ds(pl.multiple_of(h * 40 + i * 8, 8), 8), :]
                wide.append((roll(src, 4), roll(src, -4)))
        for g in range(8):
            for q in range(2):
                parts = [w[q][:, g * 128 : (g + 1) * 128] for w in wide]
                for w, part in enumerate(block_transpose(parts, 16)):
                    out_ref[PLACE[16 * g + 2 * w + q], pl.ds(pl.multiple_of(i * 8, 8), 8), :] = part
        return carry

    lax.fori_loop(0, 5, body, 0)


def forecast_kernel(recv_ref, meta_ref, x_ref, obs_ref):
    lane = lane_iota()

    def step(f):
        new = []
        for k in range(8):
            c = f[k]
            n = f[k - 1] if k else jnp.where(lane < 16, 0.0, roll(f[7], 16))
            s = f[k + 1] if k < 7 else jnp.where(lane >= 112, 0.0, roll(f[0], -16))
            e = roll(c, -1)
            w = roll(c, 1)
            t = 0.1 * c
            new.append(t + 0.4 * (n + s) + (0.05 - t) * e + (0.05 + t) * w)
        return new

    def body(index, carry):
        m, i = index // 5, index % 5
        rows = pl.ds(pl.multiple_of(i * 8, 8), 8)
        even = block_transpose([recv_ref[m * 16 + 2 * j, rows, :] for j in range(8)], 16)
        odd = block_transpose([recv_ref[m * 16 + 2 * j + 1, rows, :] for j in range(8)], 16)
        for h in range(2):
            f = even[4 * h : 4 * h + 4] + odd[4 * h : 4 * h + 4]
            for _ in range(4):
                f = step(f)
            dest = pl.ds(pl.multiple_of(m * 80 + h * 40 + i * 8, 8), 8)
            for r in range(4):
                x_ref[dest, r * 128 : (r + 1) * 128] = jnp.where(
                    lane % 16 < 8, roll(f[r], -4), roll(f[4 + r], 4)
                )
        return carry

    lax.fori_loop(0, 40, body, 0)
    cell = meta_ref[0:1, :].astype(jnp.int32)
    row = cell // 8
    place = (row % 4) * 128 + (row // 4) * 8 + cell % 8
    pick = jnp.where(
        lax.broadcasted_iota(jnp.int32, (CELLS, 128), 0) == place, 1.0, 0.0
    ).astype(BF16)

    def gather(i, carry):
        rows = pl.ds(pl.multiple_of(i * 128, 128), 128)
        x = x_ref[rows, :]
        x1 = x.astype(BF16)
        rest = x - x1.astype(F32)
        x2 = rest.astype(BF16)
        x3 = (rest - x2.astype(F32)).astype(BF16)
        total = jnp.dot(x1, pick, preferred_element_type=F32)
        total = total + jnp.dot(x2, pick, preferred_element_type=F32)
        obs_ref[rows, :] = total + jnp.dot(x3, pick, preferred_element_type=F32)
        return carry

    lax.fori_loop(0, 5, gather, 0)
    obs_ref[K : K + 8, :] = meta_ref[...]


def split(value):
    high = value.astype(BF16)
    return high, (value - high.astype(F32)).astype(BF16)


def left3(value):
    high, low = split(value)
    return jnp.concatenate([high, high, low], axis=1)


def right3(value):
    high, low = split(value)
    return jnp.concatenate([high, low, high], axis=0)


def mm(left, right):
    return jnp.dot(left, right, preferred_element_type=F32)


def server_kernel(
    x_ref, own_ref, before_ref, after_ref, out_ref, xa, y, yl3, yt3, xr3, p3, res, sums
):
    near = (before_ref, own_ref, after_ref)
    mean = jnp.sum(x_ref[...], axis=0, keepdims=True) * (1.0 / K)
    xa[...] = x_ref[...] - mean
    innov, var, orow, ocol = [], [], [], []
    for j, ref in enumerate(near):
        obs = ref[0:K, :]
        obs_mean = jnp.sum(obs, axis=0, keepdims=True) * (1.0 / K)
        y[:, j * 128 : (j + 1) * 128] = obs - obs_mean
        cell = ref[K : K + 1, :].astype(jnp.int32)
        innov.append(ref[K + 1 : K + 2, :] - obs_mean)
        var.append(ref[K + 2 : K + 3, :])
        orow.append((cell // 8).astype(F32))
        ocol.append((cell % 8).astype(F32) + 8.0 * (j - 1))
    innov, var, orow, ocol = (jnp.concatenate(v, axis=1) for v in (innov, var, orow, ocol))
    yv = y[...]
    yl3[...] = left3(yv)
    yt = yv.T
    yt_high, yt_low = split(yt)
    yt3[0:NOBS, :] = yt_high
    yt3[NOBS : 2 * NOBS, :] = yt_low
    yt3[2 * NOBS :, :] = yt_high
    ytl3 = jnp.concatenate([yt_high, yt_high, yt_low], axis=1)
    t_mat = mm(ytl3, right3(yv))
    xr3[...] = right3(xa[...])
    u_mat = mm(ytl3, xr3[...])

    first = own_ref[K + 3 : K + 4, 0:1]
    lane = lax.broadcasted_iota(jnp.int32, (1, CELLS), 1)
    cell_row = ((lane % 128) // 8 * 4 + lane // 128).astype(F32)
    eye = jnp.where(
        lax.broadcasted_iota(jnp.int32, (NOBS, NOBS), 0)
        == lax.broadcasted_iota(jnp.int32, (NOBS, NOBS), 1),
        1.0,
        0.0,
    )
    c_total = jnp.zeros((NOBS, CELLS), F32)
    coef = jnp.zeros((1, CELLS), F32)
    drow = jnp.zeros((1, CELLS), F32)
    for patch in range(2):
        lower = jnp.zeros_like(first) if patch == 0 else first
        upper = (first if patch == 0 else jnp.full_like(first, 64.0)) - 1.0
        gap_row = jnp.maximum(jnp.maximum(lower - orow, orow - upper), 0.0) * (1.0 / 16.0)
        gap_col = jnp.maximum(jnp.maximum(-ocol, ocol - 7.0), 0.0) * (1.0 / 8.0)
        g = jnp.exp(-gap_row * gap_row - gap_col * gap_col) / var
        sg = jnp.sqrt(g)
        both = jnp.concatenate([sg, sg * innov, jnp.zeros((6, NOBS), F32)], axis=0).T
        sg_col, sgd_col = both[:, 0:1], both[:, 1:2]
        p3[...] = left3(yv * g)
        sums[...] = jnp.zeros_like(sums)

        def gram(i, carry):
            rows = pl.ds(pl.multiple_of(i * 128, 128), 128)
            block = jnp.abs(mm(p3[rows, :], yt3[...]))
            sums[...] += jnp.sum(block.reshape(16, 8, K), axis=0)
            return carry

        lax.fori_loop(0, 5, gram, 0)
        bound = (K - 1.0) + jnp.max(
            jnp.sum(sums[...], axis=0, keepdims=True), axis=1, keepdims=True
        )
        inv = 1.0 / bound
        q0 = (K - 1.0) * inv
        a1 = 1.5 - 0.5 * q0
        m20 = 1.5 - 0.5 * q0 * a1 * a1
        z20 = a1 * m20
        z30 = z20 * (1.5 - 0.5 * q0 * z20 * z20)
        s = (sg_col * inv) * t_mat * sg
        s_left = left3(s)
        s2 = mm(s_left, right3(s))
        k2 = -0.5 * ((a1 * a1 - q0 * a1) * eye + (0.25 * q0 - a1) * s + 0.25 * s2)
        m2 = m20 * eye + mm(s_left, right3(k2))
        kz2 = a1 * k2 - 0.5 * m2
        z2 = z20 * eye + mm(s_left, right3(kz2))
        z2_left = left3(z2)
        inside = (cell_row >= lower) & (cell_row <= upper)
        spare = CELLS - 1 if patch == 0 else 0
        v = jnp.where(lane == spare, sgd_col, sg_col * u_mat)
        w1 = mm(z2_left, right3(v))
        w2 = mm(z2_left, right3(w1))
        tail = 1.5 * v - (0.5 * q0) * (w2 + z20 * w1 + (z20 * z20) * v)
        hv = mm(z2_left, right3(-0.5 * w2)) + mm(left3(kz2), right3(tail))
        h_col = hv[:, spare : spare + 1]
        z_row = jnp.sum(h_col * s, axis=0, keepdims=True)
        pair = jnp.concatenate([z_row, jnp.zeros((7, NOBS), F32)], axis=0).T
        u_col = z30 * sgd_col + pair[:, 0:1]
        su_row = jnp.sum(u_col * s, axis=0, keepdims=True)
        su_col = jnp.concatenate([su_row, jnp.zeros((7, NOBS), F32)], axis=0).T[:, 0:1]
        drift = (jnp.sum((z30 * u_col) * v + su_col * hv, axis=0, keepdims=True)) * inv
        scale = jnp.sqrt(q0)
        c_total = jnp.where(inside, (sg_col * (scale * inv)) * hv, c_total)
        coef = jnp.where(inside, scale * z30, coef)
        drow = jnp.where(inside, drift, drow)
    base = mean + drow
    c_right = right3(c_total)
    res[...] = base + coef * xa[...] + mm(yl3[...], c_right)

    def pack(m, carry):
        for k in range(3):
            parts = []
            for b in range(4):
                i = k * 4 + b
                for r in range(4):
                    if i < 10:
                        rows = pl.ds(pl.multiple_of(m * 80 + i * 8, 8), 8)
                        parts.append(res[rows, r * 128 : (r + 1) * 128])
                    else:
                        parts.append(jnp.zeros((8, 128), F32))
            for l, part in enumerate(block_transpose(parts, 8)):
                out_ref[m * 16 + l, k * 8 : (k + 1) * 8, :] = part
        return carry

    lax.fori_loop(0, 8, pack, 0)


def unpack_kernel(recv_ref, out_ref):
    for k in range(3):
        for g in range(8):
            parts = [recv_ref[PLACE[16 * g + t], k * 8 : (k + 1) * 8, :] for t in range(16)]
            parts = block_transpose(parts, 8)
            for b in range(4):
                i = k * 4 + b
                if i >= 10:
                    continue
                for r in range(4):
                    out_ref[r, i * 8 : (i + 1) * 8, g * 128 : (g + 1) * 128] = parts[4 * b + r]


def call(kernel, out_shape, *args, scratch=(), name=None):
    return pl.pallas_call(
        kernel,
        out_shape=out_shape,
        scratch_shapes=scratch,
        compiler_params=pltpu.CompilerParams(vmem_limit_bytes=56 * 1024 * 1024),
        name=name,
    )(*args)


def shaped(*shape, dtype=F32):
    return jax.ShapeDtypeStruct(shape, dtype)


def per_device(ensemble, obs_cell, obs_value, obs_var, patch_rows):
    chunks, meta = call(
        pack_kernel,
        (shaped(128, 40, 128), shaped(8, 128)),
        ensemble.transpose(1, 0, 2),
        obs_cell,
        obs_value,
        obs_var,
        patch_rows,
        name="pack",
    )
    meta = lax.ppermute(meta, BOTH, [(s, PLACE[s]) for s in range(128)])
    recv = lax.all_to_all(chunks, BOTH, split_axis=0, concat_axis=0, tiled=True)
    x, obs = call(
        forecast_kernel, (shaped(K, CELLS), shaped(K + 8, 128)), recv, meta, name="forecast"
    )
    up = [(PLACE[s], PLACE[(s + 1) % 128]) for s in range(128)]
    down = [(b, a) for a, b in up]
    before = lax.ppermute(obs, BOTH, up)
    after = lax.ppermute(obs, BOTH, down)
    back = call(
        server_kernel,
        shaped(128, 24, 128),
        x,
        obs,
        before,
        after,
        scratch=[
            pltpu.VMEM((K, CELLS), F32),
            pltpu.VMEM((K, NOBS), F32),
            pltpu.VMEM((K, 3 * NOBS), BF16),
            pltpu.VMEM((3 * NOBS, K), BF16),
            pltpu.VMEM((3 * K, CELLS), BF16),
            pltpu.VMEM((K, 3 * NOBS), BF16),
            pltpu.VMEM((K, CELLS), F32),
            pltpu.VMEM((8, K), F32),
        ],
        name="server",
    )
    back = lax.all_to_all(back, BOTH, split_axis=0, concat_axis=0, tiled=True)
    out = call(unpack_kernel, shaped(4, MEM, 1024), back, name="unpack")
    return out.transpose(1, 0, 2)


def solution(mesh):
    in_specs = (
        P("member", "lat", None),
        P(BOTH, None),
        P(BOTH, None),
        P(BOTH, None),
        P(BOTH, None),
    )
    return jax.shard_map(
        per_device,
        mesh=mesh,
        in_specs=in_specs,
        out_specs=P("member", "lat", None),
        check_vma=False,
    )
```

```python
import functools

import jax
import jax.numpy as jnp
import numpy as np
from jax import lax
from jax.experimental import pallas as pl
from jax.experimental.pallas import tpu as pltpu
from jax.sharding import PartitionSpec as P

BOTH = ("member", "lat")
K = 640
MEM = 80
NOBS = 384
CELLS = 512
F32 = jnp.float32
BF16 = jnp.bfloat16


def strip_places():
    columns = []
    for x in range(4):
        for y in range(4) if x % 2 == 0 else range(3, -1, -1):
            columns.append((x, y))
    places, z = [], 0
    for x, y in columns:
        for k in range(4):
            for core in range(2):
                places.append((y * 2 + core) * 16 + x * 4 + (z + k) % 4)
        z = (z + 3) % 4
    return places


PLACE = strip_places()


def lane_iota(rows=8):
    return lax.broadcasted_iota(jnp.int32, (rows, 128), 1)


def roll(value, shift):
    return pltpu.roll(value, shift % value.shape[-1], value.ndim - 1)


def block_transpose(values, size):
    values = list(values)
    count = len(values)
    lane = lane_iota()
    dist = 1
    while dist < count:
        low = (lane // (size * dist)) % 2 == 0
        for i in range(count):
            if i & dist:
                continue
            a, b = values[i], values[i + dist]
            values[i] = jnp.where(low, a, roll(b, size * dist))
            values[i + dist] = jnp.where(low, roll(a, -size * dist), b)
        dist *= 2
    return values


def pair_swap(a, b):
    low = lane_iota() < 64
    cross = roll(jnp.where(low, b, a), 64)
    return jnp.where(low, a, cross), jnp.where(low, cross, b)


def pack_kernel(ens_ref, cell_ref, value_ref, var_ref, rows_ref, out_ref, meta_ref, ab):
    meta_ref[...] = jnp.zeros_like(meta_ref)
    meta_ref[0:1, :] = cell_ref[...].astype(F32)
    meta_ref[1:2, :] = value_ref[...]
    meta_ref[2:3, :] = var_ref[...]
    meta_ref[3:4, :] = jnp.broadcast_to(rows_ref[0:1, 0:1].astype(F32), (1, 128))

    def shift(i, carry):
        rows = pl.ds(pl.multiple_of(i * 8, 8), 8)
        for r in range(4):
            src = ens_ref[r, rows, :]
            ab[r, rows, :] = roll(src, 4)
            ab[4 + r, rows, :] = roll(src, -4)
        return carry

    lax.fori_loop(0, 10, shift, 0, unroll=2)
    for g in range(8):
        cols = slice(g * 128, (g + 1) * 128)
        for b in range(5):
            if b < 4:
                block = jnp.concatenate([ab[2 * b, 0:64, cols], ab[2 * b + 1, 0:64, cols]], axis=0)
            else:
                block = jnp.concatenate([ab[j, 64:80, cols] for j in range(8)], axis=0)
            block = block.T
            for w in range(16):
                out_ref[PLACE[16 * g + w], 8 * b : 8 * b + 8, :] = block[8 * w : 8 * w + 8, :]


def forecast_kernel(recv_ref, meta_ref, x_ref, obs_ref, fa, fb):
    for buf in (fa, fb):
        buf[0] = jnp.zeros((16, K), F32)
        buf[65] = jnp.zeros((16, K), F32)

    def place(l, carry):
        for b in range(4):
            for k in range(4):
                outs = pair_swap(
                    recv_ref[2 * k * 16 + l, 8 * b : 8 * b + 8, :],
                    recv_ref[(2 * k + 1) * 16 + l, 8 * b : 8 * b + 8, :],
                )
                for j, out in enumerate(outs):
                    t, r = divmod(2 * b + j, 4)
                    fa[1 + 4 * l + r, 8 * t : 8 * t + 8, k * 128 : (k + 1) * 128] = out
        ends = block_transpose([recv_ref[m * 16 + l, 32:40, :] for m in range(8)], 16)
        for j, out in enumerate(ends):
            t, r = divmod(j, 4)
            fa[1 + 4 * l + r, 8 * t : 8 * t + 8, 512:640] = out
        return carry

    lax.fori_loop(0, 16, place, 0, unroll=2)

    def advance(src, row):
        c = src[row]
        n = src[row - 1]
        s = src[row + 1]
        e = pltpu.roll(c, 15, 0)
        w = pltpu.roll(c, 1, 0)
        t = 0.1 * c
        return t + 0.4 * (n + s) + (0.05 - t) * e + (0.05 + t) * w

    for src, dst in ((fa, fb), (fb, fa), (fa, fb)):

        def move(i, carry):
            dst[i + 1] = advance(src, i + 1)
            return carry

        lax.fori_loop(0, 64, move, 0, unroll=4)

    def last(i, carry):
        x_ref[pl.ds(pl.multiple_of(i * 8, 8), 8), :] = advance(fb, i + 1)[4:12, :]
        return carry

    lax.fori_loop(0, 64, last, 0, unroll=4)
    cell = jnp.concatenate([meta_ref[0:1, :], jnp.zeros((7, 128), F32)], axis=0).T[:, 0:1]
    pick = jnp.where(
        lax.broadcasted_iota(jnp.int32, (128, CELLS), 1) == cell.astype(jnp.int32), 1.0, 0.0
    ).astype(BF16)
    for j in range(5):
        cols = slice(j * 128, (j + 1) * 128)
        x = x_ref[:, cols]
        x1 = x.astype(BF16)
        rest = x - x1.astype(F32)
        x2 = rest.astype(BF16)
        x3 = (rest - x2.astype(F32)).astype(BF16)
        obs_ref[0:128, cols] = mm(pick, x1) + mm(pick, x2) + mm(pick, x3)
    obs_ref[128:136, :] = jnp.zeros((8, K), F32)
    obs_ref[128:136, 0:128] = meta_ref[...]


def split(value):
    high = value.astype(BF16)
    return high, (value - high.astype(F32)).astype(BF16)


def left3(value):
    high, low = split(value)
    return jnp.concatenate([high, high, low], axis=1)


def right3(value):
    high, low = split(value)
    return jnp.concatenate([high, low, high], axis=0)


def mm(left, right):
    return jnp.dot(left, right, preferred_element_type=F32)


def as_row(column):
    return jnp.broadcast_to(column, (column.shape[0], 128)).T[0:1, :]


def server_kernel(
    x_ref, own_ref, before_ref, after_ref, out_ref, xy3, y3, yt3, g3, res, sums
):
    mean = jnp.sum(x_ref[...], axis=1, keepdims=True) * (1.0 / K)
    xa = x_ref[...] - mean
    x_high, x_low = split(xa)
    xy3[NOBS:, 0:K] = x_high
    xy3[NOBS:, K : 2 * K] = x_high
    xy3[NOBS:, 2 * K :] = x_low
    innov, var, orow, ocol = [], [], [], []
    for j, ref in enumerate((before_ref, own_ref, after_ref)):
        obs = ref[0:128, :]
        obs_mean = jnp.sum(obs, axis=1, keepdims=True) * (1.0 / K)
        spread = obs - obs_mean
        high, low = split(spread)
        rows = slice(j * 128, (j + 1) * 128)
        xy3[rows, 0:K] = high
        xy3[rows, K : 2 * K] = high
        xy3[rows, 2 * K :] = low
        for n, part in enumerate((high, low, high)):
            yt3[n * NOBS + j * 128 : n * NOBS + (j + 1) * 128, :] = part
        y_high, y_low = split(spread.T)
        for n, part in enumerate((y_high, y_high, y_low)):
            y3[:, n * NOBS + j * 128 : n * NOBS + (j + 1) * 128] = part
        cell = ref[128:129, 0:128].astype(jnp.int32)
        innov.append(ref[129:130, 0:128] - as_row(obs_mean))
        var.append(ref[130:131, 0:128])
        orow.append((cell // 8).astype(F32))
        ocol.append((cell % 8).astype(F32) + 8.0 * (j - 1))
    innov, var, orow, ocol = (jnp.concatenate(v, axis=1) for v in (innov, var, orow, ocol))
    right = jnp.concatenate(
        [xy3[0:NOBS, 0:K], xy3[0:NOBS, 2 * K :], xy3[0:NOBS, 0:K]], axis=1
    )
    tu = lax.dot_general(
        xy3[...], right, (((1,), (1,)), ((), ())), preferred_element_type=F32
    )
    t_mat, u_mat = tu[0:NOBS], tu[NOBS:]

    first = own_ref[131:132, 0:1]
    eye = jnp.where(
        lax.broadcasted_iota(jnp.int32, (NOBS, NOBS), 0)
        == lax.broadcasted_iota(jnp.int32, (NOBS, NOBS), 1),
        1.0,
        0.0,
    )
    cell_row = (lax.broadcasted_iota(jnp.int32, (CELLS, 1), 0) // 8).astype(F32)
    is_first = cell_row < first
    parts = []
    for patch in range(2):
        lower = jnp.zeros_like(first) if patch == 0 else first
        upper = (first if patch == 0 else jnp.full_like(first, 64.0)) - 1.0
        gap_row = jnp.maximum(jnp.maximum(lower - orow, orow - upper), 0.0) * (1.0 / 16.0)
        gap_col = jnp.maximum(jnp.maximum(-ocol, ocol - 7.0), 0.0) * (1.0 / 8.0)
        g = jnp.exp(-gap_row * gap_row - gap_col * gap_col) / var
        sg = jnp.sqrt(g)
        sgd = sg * innov
        cols = jnp.concatenate([sg, sgd, g, jnp.zeros((5, NOBS), F32)], axis=0).T
        sg_col, sgd_col, g_col = cols[:, 0:1], cols[:, 1:2], cols[:, 2:3]
        scaled = (yt3[0:NOBS, :].astype(F32) + yt3[NOBS : 2 * NOBS, :].astype(F32)) * g_col
        g3[...] = right3(scaled)
        sums[...] = jnp.zeros_like(sums)

        def gram(i, carry):
            rows = pl.ds(pl.multiple_of(i * 128, 128), 128)
            block = jnp.abs(mm(y3[rows, :], g3[...]))
            sums[...] += jnp.sum(block.reshape(16, 8, K), axis=0)
            return carry

        lax.fori_loop(0, 5, gram, 0)
        bound = (K - 1.0) + jnp.max(
            jnp.sum(sums[...], axis=0, keepdims=True), axis=1, keepdims=True
        )
        inv = 1.0 / bound
        q0 = (K - 1.0) * inv
        a1 = 1.5 - 0.5 * q0
        m20 = 1.5 - 0.5 * q0 * a1 * a1
        z20 = a1 * m20
        z30 = z20 * (1.5 - 0.5 * q0 * z20 * z20)
        s = (sg_col * inv) * t_mat * sg
        s_left = left3(s)
        s2 = mm(s_left, right3(s))
        k2 = -0.5 * ((a1 * a1 - q0 * a1) * eye + (0.25 * q0 - a1) * s + 0.25 * s2)
        m2 = m20 * eye + mm(s_left, right3(k2))
        kz2 = a1 * k2 - 0.5 * m2
        z2 = z20 * eye + mm(s_left, right3(kz2))
        z2_right = right3(z2)
        v = jnp.concatenate(
            [u_mat[128 * patch : 128 * patch + 384] * sg, jnp.broadcast_to(sgd, (8, NOBS))],
            axis=0,
        )
        w1 = mm(left3(v), z2_right)
        w2 = mm(left3(w1), z2_right)
        tail = 1.5 * v - (0.5 * q0) * (w2 + z20 * w1 + (z20 * z20) * v)
        hv = mm(left3(-0.5 * w2), z2_right) + mm(left3(tail), right3(kz2))
        u_col = z30 * sgd_col + jnp.sum(hv[384:385, :] * s, axis=1, keepdims=True)
        su = jnp.sum(u_col * s, axis=0, keepdims=True)
        u = as_row(u_col)
        drift = inv * jnp.sum((z30 * u) * v[0:384] + su * hv[0:384], axis=1, keepdims=True)
        scale = jnp.sqrt(q0)
        parts.append((hv[0:384] * (sg * (scale * inv)), drift, scale * z30))
    (c0, d0, k0), (c1, d1, k1) = parts
    middle = is_first[128:384]
    c_total = jnp.concatenate(
        [c0[0:128], jnp.where(middle, c0[128:384], c1[0:256]), c1[256:384]], axis=0
    )
    drift = jnp.concatenate(
        [d0[0:128], jnp.where(middle, d0[128:384], d1[0:256]), d1[256:384]], axis=0
    )
    coef = jnp.where(is_first, k0, k1)
    res[...] = (coef * x_ref[...] + (mean * (1.0 - coef) + drift)) + mm(left3(c_total), yt3[...])

    def pack(l, carry):
        def block(r, k):
            rows = pl.ds(pl.multiple_of(l * 32 + r * 8, 8), 8)
            return res[rows, k * 128 : (k + 1) * 128]

        for half in range(2):
            for k in range(4):
                outs = pair_swap(block(2 * half, k), block(2 * half + 1, k))
                for j, out in enumerate(outs):
                    out_ref[(2 * k + j) * 16 + l, 8 * half : 8 * half + 8, :] = out
        ends = [block(r, 4) for r in range(4)]
        for j, out in enumerate(block_transpose(ends, 16)):
            out_ref[j * 16 + l, 16:24, :] = out
            out_ref[(4 + j) * 16 + l, 16:24, :] = roll(out, 64)
        return carry

    lax.fori_loop(0, 16, pack, 0, unroll=2)


def unpack_kernel(recv_ref, out_ref):
    for g in range(8):
        cols = slice(g * 128, (g + 1) * 128)
        for b in range(3):
            block = jnp.concatenate(
                [recv_ref[PLACE[16 * g + w], 8 * b : 8 * b + 8, :] for w in range(16)], axis=0
            ).T
            if b < 2:
                out_ref[2 * b, 0:64, cols] = block[0:64]
                out_ref[2 * b + 1, 0:64, cols] = block[64:128]
            else:
                for r in range(4):
                    out_ref[r, 64:80, cols] = block[16 * r : 16 * r + 16]


def call(kernel, out_shape, *args, scratch=(), name=None):
    return pl.pallas_call(
        kernel,
        out_shape=out_shape,
        scratch_shapes=scratch,
        compiler_params=pltpu.CompilerParams(vmem_limit_bytes=56 * 1024 * 1024),
        name=name,
    )(*args)


def shaped(*shape, dtype=F32):
    return jax.ShapeDtypeStruct(shape, dtype)


def per_device(ensemble, obs_cell, obs_value, obs_var, patch_rows):
    chunks, meta = call(
        pack_kernel,
        (shaped(128, 40, 128), shaped(8, 128)),
        ensemble.transpose(1, 0, 2),
        obs_cell,
        obs_value,
        obs_var,
        patch_rows,
        scratch=[pltpu.VMEM((8, MEM, 1024), F32)],
        name="pack",
    )
    meta = lax.ppermute(meta, BOTH, [(s, PLACE[s]) for s in range(128)])
    recv = lax.all_to_all(chunks, BOTH, split_axis=0, concat_axis=0, tiled=True)
    x, obs = call(
        forecast_kernel,
        (shaped(CELLS, K), shaped(136, K)),
        recv,
        meta,
        scratch=[pltpu.VMEM((66, 16, K), F32)] * 2,
        name="forecast",
    )
    up = [(PLACE[s], PLACE[(s + 1) % 128]) for s in range(128)]
    down = [(b, a) for a, b in up]
    before = lax.ppermute(obs, BOTH, up)
    after = lax.ppermute(obs, BOTH, down)
    back = call(
        server_kernel,
        shaped(128, 24, 128),
        x,
        obs,
        before,
        after,
        scratch=[
            pltpu.VMEM((NOBS + CELLS, 3 * K), BF16),
            pltpu.VMEM((K, 3 * NOBS), BF16),
            pltpu.VMEM((3 * NOBS, K), BF16),
            pltpu.VMEM((3 * NOBS, K), BF16),
            pltpu.VMEM((CELLS, K), F32),
            pltpu.VMEM((8, K), F32),
        ],
        name="server",
    )
    back = lax.all_to_all(back, BOTH, split_axis=0, concat_axis=0, tiled=True)
    out = call(unpack_kernel, shaped(4, MEM, 1024), back, name="unpack")
    return out.transpose(1, 0, 2)


def solution(mesh):
    in_specs = (
        P("member", "lat", None),
        P(BOTH, None),
        P(BOTH, None),
        P(BOTH, None),
        P(BOTH, None),
    )
    return jax.shard_map(
        per_device,
        mesh=mesh,
        in_specs=in_specs,
        out_specs=P("member", "lat", None),
        check_vma=False,
    )
```

```python
import functools

import jax
import jax.numpy as jnp
import numpy as np
from jax import lax
from jax.experimental import pallas as pl
from jax.experimental.pallas import tpu as pltpu
from jax.sharding import PartitionSpec as P

BOTH = ("member", "lat")
K = 640
MEM = 80
NOBS = 384
CELLS = 512
F32 = jnp.float32
BF16 = jnp.bfloat16


def strip_places():
    columns = []
    for x in range(4):
        for y in range(4) if x % 2 == 0 else range(3, -1, -1):
            columns.append((x, y))
    places, z = [], 0
    for x, y in columns:
        for k in range(4):
            for core in range(2):
                places.append((y * 2 + core) * 16 + x * 4 + (z + k) % 4)
        z = (z + 3) % 4
    return places


PLACE = strip_places()


def lane_iota(rows=8):
    return lax.broadcasted_iota(jnp.int32, (rows, 128), 1)


def roll(value, shift):
    return pltpu.roll(value, shift % value.shape[-1], value.ndim - 1)


def block_transpose(values, size):
    values = list(values)
    count = len(values)
    lane = lane_iota()
    dist = 1
    while dist < count:
        low = (lane // (size * dist)) % 2 == 0
        for i in range(count):
            if i & dist:
                continue
            a, b = values[i], values[i + dist]
            values[i] = jnp.where(low, a, roll(b, size * dist))
            values[i + dist] = jnp.where(low, roll(a, -size * dist), b)
        dist *= 2
    return values


def pair_swap(a, b):
    low = lane_iota() < 64
    cross = roll(jnp.where(low, b, a), 64)
    return jnp.where(low, a, cross), jnp.where(low, cross, b)


def pack_kernel(
    ens_hbm, cell_hbm, value_hbm, var_hbm, rows_hbm, out_hbm, meta_ref,
    ens, ab, stage, cell, value, var, rows_v, ens_sem, meta_sem, out_sem
):
    loads = [
        pltpu.make_async_copy(ens_hbm.at[8 * i : 8 * i + 8], ens.at[8 * i : 8 * i + 8], ens_sem.at[i])
        for i in range(10)
    ]
    smalls = [
        pltpu.make_async_copy(src, dst, meta_sem.at[i])
        for i, (src, dst) in enumerate(
            ((cell_hbm, cell), (value_hbm, value), (var_hbm, var), (rows_hbm, rows_v))
        )
    ]
    for copy in loads + smalls:
        copy.start()
    for i in range(10):
        loads[i].wait()
        rows = slice(8 * i, 8 * i + 8)
        for r in range(4):
            src = ens[rows, r, :]
            ab[r, rows, :] = roll(src, 4)
            ab[4 + r, rows, :] = roll(src, -4)
    stores = []
    for g in range(8):
        cols = slice(g * 128, (g + 1) * 128)
        for b in range(5):
            if b < 4:
                block = jnp.concatenate([ab[2 * b, 0:64, cols], ab[2 * b + 1, 0:64, cols]], axis=0)
            else:
                block = jnp.concatenate([ab[j, 64:80, cols] for j in range(8)], axis=0)
            block = block.T
            for w in range(16):
                stage[PLACE[16 * g + w], 8 * b : 8 * b + 8, :] = block[8 * w : 8 * w + 8, :]
        for base in sorted({PLACE[16 * g + w] // 4 * 4 for w in range(16)}):
            part = slice(base, base + 4)
            stores.append(
                pltpu.make_async_copy(stage.at[part], out_hbm.at[part], out_sem.at[base // 4])
            )
            stores[-1].start()
    for copy in smalls:
        copy.wait()
    meta_ref[...] = jnp.zeros_like(meta_ref)
    meta_ref[0:1, :] = cell[...].astype(F32)
    meta_ref[1:2, :] = value[...]
    meta_ref[2:3, :] = var[...]
    meta_ref[3:4, :] = jnp.broadcast_to(rows_v[0:1, 0:1].astype(F32), (1, 128))
    for copy in stores:
        copy.wait()


def forecast_kernel(recv_ref, meta_ref, x_ref, obs_ref, fa, fb):
    for buf in (fa, fb):
        buf[0] = jnp.zeros((16, K), F32)
        buf[65] = jnp.zeros((16, K), F32)

    def place(l, carry):
        for b in range(4):
            for k in range(4):
                outs = pair_swap(
                    recv_ref[2 * k * 16 + l, 8 * b : 8 * b + 8, :],
                    recv_ref[(2 * k + 1) * 16 + l, 8 * b : 8 * b + 8, :],
                )
                for j, out in enumerate(outs):
                    t, r = divmod(2 * b + j, 4)
                    fa[1 + 4 * l + r, 8 * t : 8 * t + 8, k * 128 : (k + 1) * 128] = out
        ends = block_transpose([recv_ref[m * 16 + l, 32:40, :] for m in range(8)], 16)
        for j, out in enumerate(ends):
            t, r = divmod(j, 4)
            fa[1 + 4 * l + r, 8 * t : 8 * t + 8, 512:640] = out
        return carry

    lax.fori_loop(0, 16, place, 0, unroll=2)

    def advance(src, row):
        c = src[row]
        n = src[row - 1]
        s = src[row + 1]
        e = pltpu.roll(c, 15, 0)
        w = pltpu.roll(c, 1, 0)
        t = 0.1 * c
        return t + 0.4 * (n + s) + (0.05 - t) * e + (0.05 + t) * w

    for src, dst in ((fa, fb), (fb, fa), (fa, fb)):

        def move(i, carry):
            dst[i + 1] = advance(src, i + 1)
            return carry

        lax.fori_loop(0, 64, move, 0, unroll=4)

    def last(i, carry):
        x_ref[pl.ds(pl.multiple_of(i * 8, 8), 8), :] = advance(fb, i + 1)[4:12, :]
        return carry

    lax.fori_loop(0, 64, last, 0, unroll=4)
    cell = jnp.concatenate([meta_ref[0:1, :], jnp.zeros((7, 128), F32)], axis=0).T[:, 0:1]
    pick = jnp.where(
        lax.broadcasted_iota(jnp.int32, (128, CELLS), 1) == cell.astype(jnp.int32), 1.0, 0.0
    ).astype(BF16)
    for j in range(5):
        cols = slice(j * 128, (j + 1) * 128)
        x = x_ref[:, cols]
        x1 = x.astype(BF16)
        rest = x - x1.astype(F32)
        x2 = rest.astype(BF16)
        x3 = (rest - x2.astype(F32)).astype(BF16)
        obs_ref[0:128, cols] = mm(pick, x1) + mm(pick, x2) + mm(pick, x3)
    obs_ref[128:136, :] = jnp.zeros((8, K), F32)
    obs_ref[128:136, 0:128] = meta_ref[...]


def split(value):
    high = value.astype(BF16)
    return high, (value - high.astype(F32)).astype(BF16)


def left3(value):
    high, low = split(value)
    return jnp.concatenate([high, high, low], axis=1)


def right3(value):
    high, low = split(value)
    return jnp.concatenate([high, low, high], axis=0)


def mm(left, right):
    return jnp.dot(left, right, preferred_element_type=F32)


def as_row(column):
    return jnp.broadcast_to(column, (column.shape[0], 128)).T[0:1, :]


def server_kernel(
    x_ref, own_ref, before_ref, after_ref, out_ref, xy3, y3, yt3, g3, res, sums
):
    mean = jnp.sum(x_ref[...], axis=1, keepdims=True) * (1.0 / K)
    xa = x_ref[...] - mean
    x_high, x_low = split(xa)
    xy3[NOBS:, 0:K] = x_high
    xy3[NOBS:, K : 2 * K] = x_high
    xy3[NOBS:, 2 * K :] = x_low
    innov, var, orow, ocol = [], [], [], []
    for j, ref in enumerate((before_ref, own_ref, after_ref)):
        obs = ref[0:128, :]
        obs_mean = jnp.sum(obs, axis=1, keepdims=True) * (1.0 / K)
        spread = obs - obs_mean
        high, low = split(spread)
        rows = slice(j * 128, (j + 1) * 128)
        xy3[rows, 0:K] = high
        xy3[rows, K : 2 * K] = high
        xy3[rows, 2 * K :] = low
        for n, part in enumerate((high, low, high)):
            yt3[n * NOBS + j * 128 : n * NOBS + (j + 1) * 128, :] = part
        y_high, y_low = split(spread.T)
        for n, part in enumerate((y_high, y_high, y_low)):
            y3[:, n * NOBS + j * 128 : n * NOBS + (j + 1) * 128] = part
        cell = ref[128:129, 0:128].astype(jnp.int32)
        innov.append(ref[129:130, 0:128] - as_row(obs_mean))
        var.append(ref[130:131, 0:128])
        orow.append((cell // 8).astype(F32))
        ocol.append((cell % 8).astype(F32) + 8.0 * (j - 1))
    innov, var, orow, ocol = (jnp.concatenate(v, axis=1) for v in (innov, var, orow, ocol))
    right = jnp.concatenate(
        [xy3[0:NOBS, 0:K], xy3[0:NOBS, 2 * K :], xy3[0:NOBS, 0:K]], axis=1
    )
    tu = lax.dot_general(
        xy3[...], right, (((1,), (1,)), ((), ())), preferred_element_type=F32
    )
    t_mat, u_mat = tu[0:NOBS], tu[NOBS:]

    first = own_ref[131:132, 0:1]
    eye = jnp.where(
        lax.broadcasted_iota(jnp.int32, (NOBS, NOBS), 0)
        == lax.broadcasted_iota(jnp.int32, (NOBS, NOBS), 1),
        1.0,
        0.0,
    )
    cell_row = (lax.broadcasted_iota(jnp.int32, (CELLS, 1), 0) // 8).astype(F32)
    is_first = cell_row < first
    parts = []
    for patch in range(2):
        lower = jnp.zeros_like(first) if patch == 0 else first
        upper = (first if patch == 0 else jnp.full_like(first, 64.0)) - 1.0
        gap_row = jnp.maximum(jnp.maximum(lower - orow, orow - upper), 0.0) * (1.0 / 16.0)
        gap_col = jnp.maximum(jnp.maximum(-ocol, ocol - 7.0), 0.0) * (1.0 / 8.0)
        g = jnp.exp(-gap_row * gap_row - gap_col * gap_col) / var
        sg = jnp.sqrt(g)
        sgd = sg * innov
        cols = jnp.concatenate([sg, sgd, g, jnp.zeros((5, NOBS), F32)], axis=0).T
        sg_col, sgd_col, g_col = cols[:, 0:1], cols[:, 1:2], cols[:, 2:3]
        scaled = (yt3[0:NOBS, :].astype(F32) + yt3[NOBS : 2 * NOBS, :].astype(F32)) * g_col
        g3[...] = right3(scaled)
        sums[...] = jnp.zeros_like(sums)

        def gram(i, carry):
            rows = pl.ds(pl.multiple_of(i * 128, 128), 128)
            block = jnp.abs(mm(y3[rows, :], g3[...]))
            sums[...] += jnp.sum(block.reshape(16, 8, K), axis=0)
            return carry

        lax.fori_loop(0, 5, gram, 0)
        bound = (K - 1.0) + jnp.max(
            jnp.sum(sums[...], axis=0, keepdims=True), axis=1, keepdims=True
        )
        inv = 1.0 / bound
        q0 = (K - 1.0) * inv
        a1 = 1.5 - 0.5 * q0
        m20 = 1.5 - 0.5 * q0 * a1 * a1
        z20 = a1 * m20
        z30 = z20 * (1.5 - 0.5 * q0 * z20 * z20)
        s = (sg_col * inv) * t_mat * sg
        s_left = left3(s)
        s2 = mm(s_left, right3(s))
        k2 = -0.5 * ((a1 * a1 - q0 * a1) * eye + (0.25 * q0 - a1) * s + 0.25 * s2)
        m2 = m20 * eye + mm(s_left, right3(k2))
        kz2 = a1 * k2 - 0.5 * m2
        z2 = z20 * eye + mm(s_left, right3(kz2))
        z2_right = right3(z2)
        v = jnp.concatenate(
            [u_mat[128 * patch : 128 * patch + 384] * sg, jnp.broadcast_to(sgd, (8, NOBS))],
            axis=0,
        )
        w1 = mm(left3(v), z2_right)
        w2 = mm(left3(w1), z2_right)
        tail = 1.5 * v - (0.5 * q0) * (w2 + z20 * w1 + (z20 * z20) * v)
        hv = mm(left3(-0.5 * w2), z2_right) + mm(left3(tail), right3(kz2))
        u_col = z30 * sgd_col + jnp.sum(hv[384:385, :] * s, axis=1, keepdims=True)
        su = jnp.sum(u_col * s, axis=0, keepdims=True)
        u = as_row(u_col)
        drift = inv * jnp.sum((z30 * u) * v[0:384] + su * hv[0:384], axis=1, keepdims=True)
        scale = jnp.sqrt(q0)
        parts.append((hv[0:384] * (sg * (scale * inv)), drift, scale * z30))
    (c0, d0, k0), (c1, d1, k1) = parts
    middle = is_first[128:384]
    c_total = jnp.concatenate(
        [c0[0:128], jnp.where(middle, c0[128:384], c1[0:256]), c1[256:384]], axis=0
    )
    drift = jnp.concatenate(
        [d0[0:128], jnp.where(middle, d0[128:384], d1[0:256]), d1[256:384]], axis=0
    )
    coef = jnp.where(is_first, k0, k1)
    res[...] = (coef * x_ref[...] + (mean * (1.0 - coef) + drift)) + mm(left3(c_total), yt3[...])

    low = lane_iota() < 64

    def pack(l, carry):
        def block(r, k):
            rows = pl.ds(pl.multiple_of(l * 32 + r * 8, 8), 8)
            return res[rows, k * 128 : (k + 1) * 128]

        for half in range(2):
            for k in range(4):
                outs = pair_swap(block(2 * half, k), block(2 * half + 1, k))
                for j, out in enumerate(outs):
                    dest = (2 * k + j) * 16 + l
                    out_ref[dest, 2 * half : 2 * half + 2, :, :] = out.reshape(2, 4, 128)
        ends = [block(r, 4) for r in range(4)]
        for j, out in enumerate(block_transpose(ends, 16)):
            turned = roll(out, 64)
            first_half = jnp.where(low, out, pltpu.roll(turned, 4, 0))
            second_half = jnp.where(low, turned, pltpu.roll(out, 4, 0))
            out_ref[j * 16 + l, 4, :, :] = first_half[0:4]
            out_ref[(4 + j) * 16 + l, 4, :, :] = second_half[0:4]
        return carry

    lax.fori_loop(0, 16, pack, 0, unroll=2)


def unpack_kernel(recv_ref, out_ref):
    for g in range(8):
        cols = slice(g * 128, (g + 1) * 128)
        for b in range(3):
            parts = []
            for w in range(16):
                src = PLACE[16 * g + w]
                if b < 2:
                    parts.append(recv_ref[src, 2 * b : 2 * b + 2, :, :].reshape(8, 128))
                else:
                    part = recv_ref[src, 4, :, :]
                    parts.append(jnp.concatenate([part, roll(part, 64)], axis=0))
            block = jnp.concatenate(parts, axis=0).T
            if b < 2:
                out_ref[0:64, 2 * b, cols] = block[0:64]
                out_ref[0:64, 2 * b + 1, cols] = block[64:128]
            else:
                for r in range(4):
                    out_ref[64:80, r, cols] = block[16 * r : 16 * r + 16]


WHOLE = pl.BlockSpec(memory_space=pltpu.VMEM)
THERE = pl.BlockSpec(memory_space=pltpu.HBM)


def call(kernel, out_shape, *args, scratch=(), name=None, vmem=16, ins=None, outs=None, cost=None):
    return pl.pallas_call(
        kernel,
        out_shape=out_shape,
        in_specs=ins or [WHOLE] * len(args),
        out_specs=outs or jax.tree.map(lambda _: WHOLE, out_shape),
        scratch_shapes=scratch,
        compiler_params=pltpu.CompilerParams(vmem_limit_bytes=vmem * 1024 * 1024),
        cost_estimate=cost,
        name=name,
    )(*args)


def shaped(*shape, dtype=F32):
    return jax.ShapeDtypeStruct(shape, dtype)


def per_device(ensemble, obs_cell, obs_value, obs_var, patch_rows):
    chunks, meta = call(
        pack_kernel,
        (shaped(128, 40, 128), shaped(8, 128)),
        ensemble,
        obs_cell,
        obs_value,
        obs_var,
        patch_rows,
        scratch=[
            pltpu.VMEM((MEM, 4, 1024), F32),
            pltpu.VMEM((8, MEM, 1024), F32),
            pltpu.VMEM((128, 40, 128), F32),
            pltpu.VMEM((1, 128), jnp.int32),
            pltpu.VMEM((1, 128), F32),
            pltpu.VMEM((1, 128), F32),
            pltpu.VMEM((1, 2), jnp.int32),
            pltpu.SemaphoreType.DMA((10,)),
            pltpu.SemaphoreType.DMA((4,)),
            pltpu.SemaphoreType.DMA((32,)),
        ],
        ins=[THERE] * 5,
        outs=(THERE, WHOLE),
        name="pack",
        vmem=58,
    )
    meta = lax.ppermute(meta, BOTH, [(s, PLACE[s]) for s in range(128)])
    recv = lax.all_to_all(chunks, BOTH, split_axis=0, concat_axis=0, tiled=True)
    x, obs = call(
        forecast_kernel,
        (shaped(CELLS, K), shaped(136, K)),
        recv,
        meta,
        scratch=[pltpu.VMEM((66, 16, K), F32)] * 2,
        name="forecast",
        vmem=12,
    )
    up = [(PLACE[s], PLACE[(s + 1) % 128]) for s in range(128)]
    down = [(b, a) for a, b in up]
    before = lax.ppermute(obs, BOTH, up)
    after = lax.ppermute(obs, BOTH, down)
    back = call(
        server_kernel,
        shaped(128, 5, 4, 128),
        x,
        obs,
        before,
        after,
        scratch=[
            pltpu.VMEM((NOBS + CELLS, 3 * K), BF16),
            pltpu.VMEM((K, 3 * NOBS), BF16),
            pltpu.VMEM((3 * NOBS, K), BF16),
            pltpu.VMEM((3 * NOBS, K), BF16),
            pltpu.VMEM((CELLS, K), F32),
            pltpu.VMEM((8, K), F32),
        ],
        name="server",
        vmem=28,
    )
    back = lax.all_to_all(back, BOTH, split_axis=0, concat_axis=0, tiled=True)
    return call(unpack_kernel, shaped(MEM, 4, 1024), back, name="unpack", vmem=6)


def solution(mesh):
    in_specs = (
        P("member", "lat", None),
        P(BOTH, None),
        P(BOTH, None),
        P(BOTH, None),
        P(BOTH, None),
    )
    return jax.shard_map(
        per_device,
        mesh=mesh,
        in_specs=in_specs,
        out_specs=P("member", "lat", None),
        check_vma=False,
    )
```

```python
import functools

import jax
import jax.numpy as jnp
import numpy as np
from jax import lax
from jax.experimental import pallas as pl
from jax.experimental.pallas import tpu as pltpu
from jax.sharding import PartitionSpec as P

BOTH = ("member", "lat")
K = 640
MEM = 80
NOBS = 384
CELLS = 512
F32 = jnp.float32
BF16 = jnp.bfloat16


def strip_places():
    columns = []
    for x in range(4):
        for y in range(4) if x % 2 == 0 else range(3, -1, -1):
            columns.append((x, y))
    places, z = [], 0
    for x, y in columns:
        for k in range(4):
            for core in range(2):
                places.append((y * 2 + core) * 16 + x * 4 + (z + k) % 4)
        z = (z + 3) % 4
    return places


PLACE = strip_places()


def lane_iota(rows=8):
    return lax.broadcasted_iota(jnp.int32, (rows, 128), 1)


def roll(value, shift):
    return pltpu.roll(value, shift % value.shape[-1], value.ndim - 1)


def block_transpose(values, size):
    values = list(values)
    count = len(values)
    lane = lane_iota()
    dist = 1
    while dist < count:
        low = (lane // (size * dist)) % 2 == 0
        for i in range(count):
            if i & dist:
                continue
            a, b = values[i], values[i + dist]
            values[i] = jnp.where(low, a, roll(b, size * dist))
            values[i + dist] = jnp.where(low, roll(a, -size * dist), b)
        dist *= 2
    return values


def pair_swap(a, b):
    low = lane_iota() < 64
    cross = roll(jnp.where(low, b, a), 64)
    return jnp.where(low, a, cross), jnp.where(low, cross, b)


def pack_kernel(
    ens_hbm, cell_hbm, value_hbm, var_hbm, rows_hbm, out_hbm, meta_ref,
    ens, ab, stage, cell, value, var, rows_v, ens_sem, meta_sem, out_sem
):
    loads = [
        pltpu.make_async_copy(ens_hbm.at[8 * i : 8 * i + 8], ens.at[8 * i : 8 * i + 8], ens_sem.at[i])
        for i in range(10)
    ]
    smalls = [
        pltpu.make_async_copy(src, dst, meta_sem.at[i])
        for i, (src, dst) in enumerate(
            ((cell_hbm, cell), (value_hbm, value), (var_hbm, var), (rows_hbm, rows_v))
        )
    ]
    for copy in loads + smalls:
        copy.start()
    for i in range(10):
        loads[i].wait()
        rows = slice(8 * i, 8 * i + 8)
        for r in range(4):
            src = ens[rows, r, :]
            ab[r, rows, :] = roll(src, 4)
            ab[4 + r, rows, :] = roll(src, -4)
    stores = []
    for g in range(8):
        cols = slice(g * 128, (g + 1) * 128)
        for b in range(5):
            if b < 4:
                block = jnp.concatenate([ab[2 * b, 0:64, cols], ab[2 * b + 1, 0:64, cols]], axis=0)
            else:
                block = jnp.concatenate([ab[j, 64:80, cols] for j in range(8)], axis=0)
            block = block.T
            for w in range(16):
                stage[PLACE[16 * g + w], 8 * b : 8 * b + 8, :] = block[8 * w : 8 * w + 8, :]
        for base in sorted({PLACE[16 * g + w] // 4 * 4 for w in range(16)}):
            part = slice(base, base + 4)
            stores.append(
                pltpu.make_async_copy(stage.at[part], out_hbm.at[part], out_sem.at[base // 4])
            )
            stores[-1].start()
    for copy in smalls:
        copy.wait()
    meta_ref[...] = jnp.zeros_like(meta_ref)
    meta_ref[0:1, :] = cell[...].astype(F32)
    meta_ref[1:2, :] = value[...]
    meta_ref[2:3, :] = var[...]
    meta_ref[3:4, :] = jnp.broadcast_to(rows_v[0:1, 0:1].astype(F32), (1, 128))
    for copy in stores:
        copy.wait()


def forecast_kernel(recv_ref, meta_ref, x_ref, obs_ref, fa, fb):
    for buf in (fa, fb):
        buf[0] = jnp.zeros((16, K), F32)
        buf[65] = jnp.zeros((16, K), F32)

    def place(l, carry):
        for b in range(4):
            for k in range(4):
                outs = pair_swap(
                    recv_ref[2 * k * 16 + l, 8 * b : 8 * b + 8, :],
                    recv_ref[(2 * k + 1) * 16 + l, 8 * b : 8 * b + 8, :],
                )
                for j, out in enumerate(outs):
                    t, r = divmod(2 * b + j, 4)
                    fa[1 + 4 * l + r, 8 * t : 8 * t + 8, k * 128 : (k + 1) * 128] = out
        ends = block_transpose([recv_ref[m * 16 + l, 32:40, :] for m in range(8)], 16)
        for j, out in enumerate(ends):
            t, r = divmod(j, 4)
            fa[1 + 4 * l + r, 8 * t : 8 * t + 8, 512:640] = out
        return carry

    lax.fori_loop(0, 16, place, 0, unroll=4)

    def advance(src, row):
        c = src[row]
        n = src[row - 1]
        s = src[row + 1]
        e = pltpu.roll(c, 15, 0)
        w = pltpu.roll(c, 1, 0)
        t = 0.1 * c
        return t + 0.4 * (n + s) + (0.05 - t) * e + (0.05 + t) * w

    for src, dst in ((fa, fb), (fb, fa), (fa, fb)):

        def move(i, carry):
            dst[i + 1] = advance(src, i + 1)
            return carry

        lax.fori_loop(0, 64, move, 0, unroll=8)

    def last(i, carry):
        x_ref[pl.ds(pl.multiple_of(i * 8, 8), 8), :] = advance(fb, i + 1)[4:12, :]
        return carry

    lax.fori_loop(0, 64, last, 0, unroll=8)
    cell = jnp.concatenate([meta_ref[0:1, :], jnp.zeros((7, 128), F32)], axis=0).T[:, 0:1]
    pick = jnp.where(
        lax.broadcasted_iota(jnp.int32, (128, CELLS), 1) == cell.astype(jnp.int32), 1.0, 0.0
    ).astype(BF16)
    for j in range(5):
        cols = slice(j * 128, (j + 1) * 128)
        x = x_ref[:, cols]
        x1 = x.astype(BF16)
        rest = x - x1.astype(F32)
        x2 = rest.astype(BF16)
        x3 = (rest - x2.astype(F32)).astype(BF16)
        obs_ref[0:128, cols] = mm(pick, x1) + mm(pick, x2) + mm(pick, x3)
    obs_ref[128:136, :] = jnp.zeros((8, K), F32)
    obs_ref[128:136, 0:128] = meta_ref[...]


def split(value):
    high = value.astype(BF16)
    return high, (value - high.astype(F32)).astype(BF16)


def left3(value):
    high, low = split(value)
    return jnp.concatenate([high, high, low], axis=1)


def right3(value):
    high, low = split(value)
    return jnp.concatenate([high, low, high], axis=0)


def mm(left, right):
    return jnp.dot(left, right, preferred_element_type=F32)


def as_row(column):
    return jnp.broadcast_to(column, (column.shape[0], 128)).T[0:1, :]


def prepare_kernel(x_ref, own_ref, x3_ref, own3_ref, y_ref, tu_ref, mean_ref):
    mean = jnp.sum(x_ref[...], axis=1, keepdims=True) * (1.0 / K)
    mean_ref[...] = mean
    high, low = split(x_ref[...] - mean)
    x3_ref[:, 0:K] = high
    x3_ref[:, K : 2 * K] = high
    x3_ref[:, 2 * K :] = low
    obs = own_ref[0:128, :]
    spread = obs - jnp.sum(obs, axis=1, keepdims=True) * (1.0 / K)
    high, low = split(spread)
    own3_ref[:, 0:K] = high
    own3_ref[:, K : 2 * K] = high
    own3_ref[:, 2 * K :] = low
    y_ref[...] = spread.T.astype(BF16)
    right = jnp.concatenate([high, low, high], axis=1)
    tu_ref[0:128, :] = mm_nt(own3_ref[...], right)
    tu_ref[128:, :] = mm_nt(x3_ref[...], right)


def mm_nt(left, right):
    return lax.dot_general(left, right, (((1,), (1,)), ((), ())), preferred_element_type=F32)


def server_kernel(
    x_ref, own_ref, x3_ref, own3_ref, y_ref, tu_ref, mean_ref, before_ref, after_ref, out_ref,
    near3, yr, y2, yt3, g2, u_ref, c_ref, d_ref, res
):
    innov, var, orow, ocol = [], [], [], []
    yt3[0:128, :] = own3_ref[:, 0:K]
    yt3[NOBS : NOBS + 128, :] = own3_ref[:, 2 * K :]
    yt3[2 * NOBS : 2 * NOBS + 128, :] = own3_ref[:, 0:K]
    y2[:, 0:128] = y_ref[...]
    y2[:, NOBS : NOBS + 128] = y_ref[...]
    for j, ref in enumerate((own_ref, before_ref, after_ref)):
        obs = ref[0:128, :]
        obs_mean = jnp.sum(obs, axis=1, keepdims=True) * (1.0 / K)
        if j:
            spread = obs - obs_mean
            high, low = split(spread)
            rows = slice((j - 1) * 128, j * 128)
            for n, (left, right) in enumerate(((high, high), (high, low), (low, high))):
                near3[rows, n * K : (n + 1) * K] = left
                yr[rows, n * K : (n + 1) * K] = right
                yt3[n * NOBS + j * 128 : n * NOBS + (j + 1) * 128, :] = right
            turned = spread.T.astype(BF16)
            y2[:, j * 128 : (j + 1) * 128] = turned
            y2[:, NOBS + j * 128 : NOBS + (j + 1) * 128] = turned
        cell = ref[128:129, 0:128].astype(jnp.int32)
        innov.append(ref[129:130, 0:128] - as_row(obs_mean))
        var.append(ref[130:131, 0:128])
        orow.append((cell // 8).astype(F32))
        ocol.append((cell % 8).astype(F32) + (0.0, -8.0, 8.0)[j])
    innov, var, orow, ocol = (jnp.concatenate(v, axis=1) for v in (innov, var, orow, ocol))

    first = own_ref[131:132, 0:1]
    swap = first > 32.0
    swap_scalar = jnp.max(first) > 32.0
    eye128 = lax.broadcasted_iota(jnp.int32, (128, 128), 0) == lax.broadcasted_iota(
        jnp.int32, (128, 128), 1
    )
    eye = jnp.where(
        lax.broadcasted_iota(jnp.int32, (NOBS, NOBS), 0)
        == lax.broadcasted_iota(jnp.int32, (NOBS, NOBS), 1),
        1.0,
        0.0,
    )
    both = range(2)
    zero, full = jnp.zeros_like(first), jnp.full_like(first, 64.0)
    lower = [jnp.where(swap, first, zero), jnp.where(swap, zero, first)]
    upper = [jnp.where(swap, full, first) - 1.0, jnp.where(swap, first, full) - 1.0]
    sg, sgd, sg_col, sgd_col, diag = [], [], [], [], []
    yt = yt3[0:NOBS, :].astype(F32) + yt3[NOBS : 2 * NOBS, :].astype(F32)
    for p in both:
        gap_row = jnp.maximum(jnp.maximum(lower[p] - orow, orow - upper[p]), 0.0) * (1.0 / 16.0)
        gap_col = jnp.maximum(jnp.maximum(-ocol, ocol - 7.0), 0.0) * (1.0 / 8.0)
        g = jnp.exp(-gap_row * gap_row - gap_col * gap_col) / var
        sg.append(jnp.sqrt(g))
        sgd.append(sg[p] * innov)
        cols = jnp.concatenate([sg[p], sgd[p], g, jnp.zeros((5, NOBS), F32)], axis=0).T
        sg_col.append(cols[:, 0:1])
        sgd_col.append(cols[:, 1:2])
        scaled = yt * cols[:, 2:3]
        diag.append(jnp.sum(scaled * yt, axis=0, keepdims=True))
        high, low = split(scaled)
        g2[0:NOBS, p * K : (p + 1) * K] = high
        g2[NOBS:, p * K : (p + 1) * K] = low

    tu = mm_nt(near3[...], yr[...])
    cross = mm_nt(own3_ref[...], yr[...])
    t_mat = jnp.concatenate(
        [
            jnp.concatenate([tu_ref[0:128, :], cross], axis=1),
            jnp.concatenate([cross.T, tu], axis=1),
        ],
        axis=0,
    )
    u_ref[:, 0:128] = tu_ref[128:, :]
    u_ref[:, 128:] = mm_nt(x3_ref[...], yr[...])

    sums = []
    for n in range(5):
        block = jnp.abs(mm(y2[...], g2[:, n * 256 : (n + 1) * 256]))
        for half in range(2):
            own = (2 * n + half) % 5
            part = block[:, half * 128 : (half + 1) * 128]
            rows = [part[i * 128 : (i + 1) * 128] for i in range(5)]
            rows[own] = jnp.where(eye128, 0.0, rows[own])
            total = (rows[0] + rows[1]) + (rows[2] + rows[3]) + rows[4]
            sums.append(jnp.sum(total, axis=0, keepdims=True))
    inv, q0, a1, m20, z20, z30 = [], [], [], [], [], []
    for p in both:
        total = jnp.concatenate(sums[5 * p : 5 * p + 5], axis=1) + diag[p]
        bound = (K - 1.0) + jnp.max(total, axis=1, keepdims=True)
        inv.append(1.0 / bound)
        q0.append((K - 1.0) * inv[p])
        a1.append(1.5 - 0.5 * q0[p])
        m20.append(1.5 - 0.5 * q0[p] * a1[p] * a1[p])
        z20.append(a1[p] * m20[p])
        z30.append(z20[p] * (1.5 - 0.5 * q0[p] * z20[p] * z20[p]))
    s = [(sg_col[p] * inv[p]) * t_mat * sg[p] for p in both]
    s_left = [left3(s[p]) for p in both]
    s2 = [mm(s_left[p], right3(s[p])) for p in both]
    k2 = [
        -0.5
        * (
            (a1[p] * a1[p] - q0[p] * a1[p]) * eye
            + (0.25 * q0[p] - a1[p]) * s[p]
            + 0.25 * s2[p]
        )
        for p in both
    ]
    m2 = [m20[p] * eye + mm(s_left[p], right3(k2[p])) for p in both]
    kz2 = [a1[p] * k2[p] - 0.5 * m2[p] for p in both]
    z2 = [z20[p] * eye + mm(s_left[p], right3(kz2[p])) for p in both]
    z2_right = [right3(z2[p]) for p in both]
    size = (256, 384)
    start = [
        pl.multiple_of(jnp.where(swap_scalar, 256, 0), 128),
        pl.multiple_of(jnp.where(swap_scalar, 0, 128), 128),
    ]
    v = [
        jnp.concatenate(
            [u_ref[pl.ds(start[p], size[p]), :] * sg[p], jnp.broadcast_to(sgd[p], (8, NOBS))],
            axis=0,
        )
        for p in both
    ]
    w1 = [mm(left3(v[p]), z2_right[p]) for p in both]
    w2 = [mm(left3(w1[p]), z2_right[p]) for p in both]
    tail = [
        1.5 * v[p] - (0.5 * q0[p]) * (w2[p] + z20[p] * w1[p] + (z20[p] * z20[p]) * v[p])
        for p in both
    ]
    hv = [
        mm(
            jnp.concatenate([left3(-0.5 * w2[p]), left3(tail[p])], axis=1),
            jnp.concatenate([z2_right[p], right3(kz2[p])], axis=0),
        )
        for p in both
    ]
    scale = [jnp.sqrt(q0[p]) for p in both]
    for p in (1, 0):
        n = size[p]
        rows = pl.ds(start[p], n)
        u_col = z30[p] * sgd_col[p] + jnp.sum(hv[p][n : n + 1] * s[p], axis=1, keepdims=True)
        su = jnp.sum(u_col * s[p], axis=0, keepdims=True)
        u = as_row(u_col)
        drift = inv[p] * jnp.sum(
            (z30[p] * u) * v[p][0:n] + su * hv[p][0:n], axis=1, keepdims=True
        )
        part = hv[p][0:n] * (sg[p] * (scale[p] * inv[p]))
        if p == 0:
            cell_row = (
                (lax.broadcasted_iota(jnp.int32, (n, 1), 0) + start[p]) // 8
            ).astype(F32)
            inside = (cell_row >= lower[0]) & (cell_row <= upper[0])
            part = jnp.where(inside, part, c_ref[rows, :])
            drift = jnp.where(inside, drift, d_ref[rows, :])
        c_ref[rows, :] = part
        d_ref[rows, :] = drift
    cell_row = (lax.broadcasted_iota(jnp.int32, (CELLS, 1), 0) // 8).astype(F32)
    inside = (cell_row >= lower[0]) & (cell_row <= upper[0])
    coef = jnp.where(inside, scale[0] * z30[0], scale[1] * z30[1])
    base = mean_ref[...] * (1.0 - coef) + d_ref[...]
    low = lane_iota() < 64
    for i in range(4):
        rows = slice(i * 128, (i + 1) * 128)
        res[rows, :] = (
            coef[rows] * x_ref[rows, :] + base[rows] + mm(left3(c_ref[rows, :]), yt3[...])
        )
        for l in range(4 * i, 4 * i + 4):

            def block(r, k):
                return res[32 * l + 8 * r : 32 * l + 8 * r + 8, k * 128 : (k + 1) * 128]

            for half in range(2):
                for k in range(4):
                    outs = pair_swap(block(2 * half, k), block(2 * half + 1, k))
                    for j, out in enumerate(outs):
                        dest = (2 * k + j) * 16 + l
                        out_ref[dest, 2 * half : 2 * half + 2, :, :] = out.reshape(2, 4, 128)
            ends = [block(r, 4) for r in range(4)]
            for j, out in enumerate(block_transpose(ends, 16)):
                turned = roll(out, 64)
                first_half = jnp.where(low, out, pltpu.roll(turned, 4, 0))
                second_half = jnp.where(low, turned, pltpu.roll(out, 4, 0))
                out_ref[j * 16 + l, 4, :, :] = first_half[0:4]
                out_ref[(4 + j) * 16 + l, 4, :, :] = second_half[0:4]


def unpack_kernel(recv_ref, out_ref):
    for g in range(8):
        cols = slice(g * 128, (g + 1) * 128)
        for b in range(3):
            parts = []
            for w in range(16):
                src = PLACE[16 * g + w]
                if b < 2:
                    parts.append(recv_ref[src, 2 * b : 2 * b + 2, :, :].reshape(8, 128))
                else:
                    part = recv_ref[src, 4, :, :]
                    parts.append(jnp.concatenate([part, roll(part, 64)], axis=0))
            block = jnp.concatenate(parts, axis=0).T
            if b < 2:
                out_ref[0:64, 2 * b, cols] = block[0:64]
                out_ref[0:64, 2 * b + 1, cols] = block[64:128]
            else:
                for r in range(4):
                    out_ref[64:80, r, cols] = block[16 * r : 16 * r + 16]


WHOLE = pl.BlockSpec(memory_space=pltpu.VMEM)
THERE = pl.BlockSpec(memory_space=pltpu.HBM)


def call(kernel, out_shape, *args, scratch=(), name=None, vmem=16, ins=None, outs=None, cost=None):
    return pl.pallas_call(
        kernel,
        out_shape=out_shape,
        in_specs=ins or [WHOLE] * len(args),
        out_specs=outs or jax.tree.map(lambda _: WHOLE, out_shape),
        scratch_shapes=scratch,
        compiler_params=pltpu.CompilerParams(vmem_limit_bytes=vmem * 1024 * 1024),
        cost_estimate=cost,
        name=name,
    )(*args)


def shaped(*shape, dtype=F32):
    return jax.ShapeDtypeStruct(shape, dtype)


def per_device(ensemble, obs_cell, obs_value, obs_var, patch_rows):
    chunks, meta = call(
        pack_kernel,
        (shaped(128, 40, 128), shaped(8, 128)),
        ensemble,
        obs_cell,
        obs_value,
        obs_var,
        patch_rows,
        scratch=[
            pltpu.VMEM((MEM, 4, 1024), F32),
            pltpu.VMEM((8, MEM, 1024), F32),
            pltpu.VMEM((128, 40, 128), F32),
            pltpu.VMEM((1, 128), jnp.int32),
            pltpu.VMEM((1, 128), F32),
            pltpu.VMEM((1, 128), F32),
            pltpu.VMEM((1, 2), jnp.int32),
            pltpu.SemaphoreType.DMA((10,)),
            pltpu.SemaphoreType.DMA((4,)),
            pltpu.SemaphoreType.DMA((32,)),
        ],
        ins=[THERE] * 5,
        outs=(THERE, WHOLE),
        name="pack",
        vmem=58,
    )
    meta = lax.ppermute(meta, BOTH, [(s, PLACE[s]) for s in range(128)])
    recv = lax.all_to_all(chunks, BOTH, split_axis=0, concat_axis=0, tiled=True)
    x, obs = call(
        forecast_kernel,
        (shaped(CELLS, K), shaped(136, K)),
        recv,
        meta,
        scratch=[pltpu.VMEM((66, 16, K), F32)] * 2,
        name="forecast",
        vmem=12,
    )
    up = [(PLACE[s], PLACE[(s + 1) % 128]) for s in range(128)]
    down = [(b, a) for a, b in up]
    before = lax.ppermute(obs, BOTH, up)
    after = lax.ppermute(obs, BOTH, down)
    own = call(
        prepare_kernel,
        (
            shaped(CELLS, 3 * K, dtype=BF16),
            shaped(128, 3 * K, dtype=BF16),
            shaped(K, 128, dtype=BF16),
            shaped(128 + CELLS, 128),
            shaped(CELLS, 1),
        ),
        x,
        obs,
        name="prepare",
        vmem=6,
        cost=pl.CostEstimate(flops=2 * K * K * 128 * 3, bytes_accessed=8 << 20, transcendentals=0),
    )
    back = call(
        server_kernel,
        shaped(128, 5, 4, 128),
        x,
        obs,
        *own,
        before,
        after,
        scratch=[
            pltpu.VMEM((256, 3 * K), BF16),
            pltpu.VMEM((256, 3 * K), BF16),
            pltpu.VMEM((K, 2 * NOBS), BF16),
            pltpu.VMEM((3 * NOBS, K), BF16),
            pltpu.VMEM((2 * NOBS, 2 * K), BF16),
            pltpu.VMEM((CELLS, NOBS), F32),
            pltpu.VMEM((CELLS, NOBS), F32),
            pltpu.VMEM((CELLS, 1), F32),
            pltpu.VMEM((CELLS, K), F32),
        ],
        name="server",
        vmem=32,
    )
    back = lax.all_to_all(back, BOTH, split_axis=0, concat_axis=0, tiled=True)
    return call(unpack_kernel, shaped(MEM, 4, 1024), back, name="unpack", vmem=6)


def solution(mesh):
    in_specs = (
        P("member", "lat", None),
        P(BOTH, None),
        P(BOTH, None),
        P(BOTH, None),
        P(BOTH, None),
    )
    return jax.shard_map(
        per_device,
        mesh=mesh,
        in_specs=in_specs,
        out_specs=P("member", "lat", None),
        check_vma=False,
    )
```

```python
import functools

import jax
import jax.numpy as jnp
import numpy as np
from jax import lax
from jax.experimental import pallas as pl
from jax.experimental.pallas import tpu as pltpu
from jax.sharding import Mesh
from jax.sharding import PartitionSpec as P

ALL = ("y", "core", "lat")
CHIPS = ("y", "lat")
K = 640
MEM = 80
NOBS = 384
CELLS = 512
F32 = jnp.float32
BF16 = jnp.bfloat16


def strip_places():
    columns = []
    for x in range(4):
        for y in range(4) if x % 2 == 0 else range(3, -1, -1):
            columns.append((x, y))
    places, z = [], 0
    for x, y in columns:
        for k in range(4):
            for core in range(2):
                places.append((y * 2 + core) * 16 + x * 4 + (z + k) % 4)
        z = (z + 3) % 4
    return places


PLACE = strip_places()
CHIP = [PLACE[2 * j] // 32 * 16 + PLACE[2 * j] % 16 for j in range(64)]


def lane_iota(rows=8):
    return lax.broadcasted_iota(jnp.int32, (rows, 128), 1)


def roll(value, shift):
    return pltpu.roll(value, shift % value.shape[-1], value.ndim - 1)


def block_transpose(values, size):
    values = list(values)
    count = len(values)
    lane = lane_iota()
    dist = 1
    while dist < count:
        low = (lane // (size * dist)) % 2 == 0
        for i in range(count):
            if i & dist:
                continue
            a, b = values[i], values[i + dist]
            values[i] = jnp.where(low, a, roll(b, size * dist))
            values[i + dist] = jnp.where(low, roll(a, -size * dist), b)
        dist *= 2
    return values


def pair_swap(a, b):
    low = lane_iota() < 64
    cross = roll(jnp.where(low, b, a), 64)
    return jnp.where(low, a, cross), jnp.where(low, cross, b)


def pack_kernel(
    ens_hbm, cell_hbm, value_hbm, var_hbm, rows_hbm, out_hbm,
    ens, moved, stage, cell, value, var, rows_v, ens_sem, meta_sem, out_sem
):
    loads = [
        pltpu.make_async_copy(ens_hbm.at[8 * i : 8 * i + 8], ens.at[8 * i : 8 * i + 8], ens_sem.at[i])
        for i in range(10)
    ]
    smalls = [
        pltpu.make_async_copy(src, dst, meta_sem.at[i])
        for i, (src, dst) in enumerate(
            ((cell_hbm, cell), (value_hbm, value), (var_hbm, var), (rows_hbm, rows_v))
        )
    ]
    for copy in loads + smalls:
        copy.start()
    for i in range(10):
        loads[i].wait()
        rows = slice(8 * i, 8 * i + 8)
        for r in range(4):
            moved[r, rows, :] = roll(ens[rows, r, :], 4)
    for copy in smalls:
        copy.wait()
    meta = jnp.concatenate(
        [
            cell[...].astype(F32),
            value[...],
            var[...],
            jnp.broadcast_to(rows_v[0:1, 0:1].astype(F32), (1, 128)),
        ],
        axis=0,
    )
    for chip in range(64):
        stage[chip, 15, :, :] = meta
    stores = []

    def send(column):
        base = min(CHIP[4 * column : 4 * column + 4])
        part = slice(base, base + 4)
        stores.append(
            pltpu.make_async_copy(stage.at[part], out_hbm.at[part], out_sem.at[column])
        )
        stores[-1].start()

    low = lane_iota() < 64

    def put(j, t, pair):
        for h in range(2):
            tile = 4 * t + 2 * h
            stage[CHIP[j % 64], tile : tile + 2, :, :] = pair[h].reshape(2, 4, 128)

    for g in range(8):
        cols = slice(g * 128, (g + 1) * 128)
        main = [
            jnp.concatenate([moved[2 * h, 0:64, cols], moved[2 * h + 1, 0:64, cols]], axis=0).T
            for h in range(2)
        ]
        tails = jnp.concatenate([moved[r, 64:80, cols] for r in range(4)] * 2, axis=0).T
        for w in range(16):
            rows = slice(8 * w, 8 * w + 8)
            pair = [main[0][rows], main[1][rows]]
            tail = tails[rows]
            j = 8 * g + w // 2
            if w % 2 == 0:
                put(j - 1, 2, pair)
                put(j, 0, pair)
                both = jnp.where(low, tail, pltpu.roll(tail, 4, 0))
                stage[CHIP[(j - 1) % 64], 14, :, :] = both[0:4]
            else:
                put(j, 1, pair)
                both = jnp.where(low, tails[8 * w - 8 : 8 * w], tail)
                stage[CHIP[j], 12:14, :, :] = both.reshape(2, 4, 128)
            if w % 8 == 0 and j > 0:
                send(j // 4 - 1)
    send(15)
    for copy in stores:
        copy.wait()


def chip_pair():
    y, lat = lax.axis_index("y"), lax.axis_index("lat")
    x, z = lat // 4, lat % 4
    column = x * 4 + jnp.where(x % 2 == 0, y, 3 - y)
    return 4 * column + (z + column) % 4


def place_kernel(recv_ref, own_ref, send_ref):
    def run(core):
        def put(row, t, cols, value):
            if t in (core, core + 1):
                at = 8 * (t - core)
                own_ref[row, at : at + 8, cols] = value
            other = 1 - core
            if t in (other, other + 1):
                at = 8 * (t - other)
                send_ref[row, at : at + 8, cols] = value

        def place(l, carry):
            def vreg(y, tile):
                return recv_ref[y * 16 + l, tile : tile + 2, :, :].reshape(8, 128)

            for t in range(3):
                for h in range(2):
                    for k in range(2):
                        tile = 4 * t + 2 * h
                        outs = pair_swap(vreg(2 * k, tile), vreg(2 * k + 1, tile))
                        for j, out in enumerate(outs):
                            put(4 * l + 2 * h + j, t, slice(128 * k, 128 * k + 128), out)
            last = slice(256, 384)
            outs = block_transpose([vreg(y, 12) for y in range(4)], 16)
            for r, out in enumerate(outs):
                turned = roll(out, 64)
                put(4 * l + r, 0, last, turned if core else out)
                put(4 * l + r, 1, last, out if core else turned)
            ends = []
            for y in range(4):
                part = recv_ref[y * 16 + l, 14, :, :]
                ends.append(jnp.concatenate([part, roll(part, 64)], axis=0))
            for r, out in enumerate(block_transpose(ends, 16)):
                put(4 * l + r, 2, last, roll(out, 64) if core else out)
            return carry

        lax.fori_loop(0, 16, place, 0, unroll=4)
        for ref, strip in (
            (own_ref, 2 * chip_pair() + core),
            (send_ref, 2 * chip_pair() + 1 - core),
        ):
            ref[64, 0:4, 0:128] = recv_ref[strip // 32 * 16 + strip % 16, 15, :, :]

    core = lax.axis_index("core")
    for value in range(2):
        pl.when(core == value)(functools.partial(run, value))


def advance(src, row, cols):
    c = src[row, :, cols]
    n = src[row - 1, :, cols]
    s = src[row + 1, :, cols]
    e = pltpu.roll(c, 15, 0)
    w = pltpu.roll(c, 1, 0)
    t = 0.1 * c
    return t + 0.4 * (n + s) + (0.05 - t) * e + (0.05 + t) * w


def march(first, fa, fb, finish):
    every = slice(None)
    for buf in (fa, fb):
        buf[0] = jnp.zeros(buf.shape[1:], F32)
        buf[65] = jnp.zeros(buf.shape[1:], F32)

    def load(i, carry):
        fa[i + 1] = first(i)
        return carry

    lax.fori_loop(0, 64, load, 0, unroll=8)
    for src, dst in ((fa, fb), (fb, fa), (fa, fb)):

        def move(i, carry):
            dst[i + 1] = advance(src, i + 1, every)
            return carry

        lax.fori_loop(0, 64, move, 0, unroll=8)

    def last(i, carry):
        finish(i, advance(fb, i + 1, every)[4:12, :])
        return carry

    lax.fori_loop(0, 64, last, 0, unroll=8)


def forecast_own_kernel(own_ref, x_ref, fa, fb):
    def finish(i, value):
        x_ref[pl.ds(pl.multiple_of(i * 8, 8), 8), :] = value

    march(lambda i: own_ref[i, :, 0:256], fa, fb, finish)


def forecast_kernel(own_ref, other_ref, part_ref, x_ref, obs_ref, fa, fb):
    core = lax.axis_index("core")
    low_core = core == 0
    low = lax.broadcasted_iota(jnp.int32, (16, 128), 1) < 64
    own_low = jnp.where(low_core, 1, 0)
    pick_own = low == (jnp.broadcast_to(own_low, (16, 128)) > 0)

    def first(i):
        ends = jnp.where(pick_own, own_ref[i, :, 256:384], other_ref[i, :, 256:384])
        return jnp.concatenate([other_ref[i, :, 0:256], ends], axis=1)

    def finish(i, value):
        rows = pl.ds(pl.multiple_of(i * 8, 8), 8)
        x_ref[rows, pl.ds(pl.multiple_of((1 - core) * 256, 128), 256)] = value[:, 0:256]
        x_ref[rows, pl.ds(pl.multiple_of(core * 256, 128), 256)] = part_ref[rows, :]
        x_ref[rows, 512:640] = value[:, 256:384]

    march(first, fa, fb, finish)
    here = jnp.broadcast_to(jnp.where((chip_pair() // 8) % 2 == core, 1, 0), (4, 128)) > 0
    meta = jnp.where(here, own_ref[64, 0:4, 0:128], other_ref[64, 0:4, 0:128])
    meta = jnp.concatenate([meta, jnp.zeros((4, 128), F32)], axis=0)
    cell = meta.T[:, 0:1]
    pick = jnp.where(
        lax.broadcasted_iota(jnp.int32, (128, CELLS), 1) == cell.astype(jnp.int32), 1.0, 0.0
    ).astype(BF16)
    for j in range(5):
        cols = slice(j * 128, (j + 1) * 128)
        x = x_ref[:, cols]
        x1 = x.astype(BF16)
        rest = x - x1.astype(F32)
        x2 = rest.astype(BF16)
        x3 = (rest - x2.astype(F32)).astype(BF16)
        obs_ref[0:128, cols] = mm(pick, x1) + mm(pick, x2) + mm(pick, x3)
    obs_ref[128:136, :] = jnp.zeros((8, K), F32)
    obs_ref[128:136, 0:128] = meta


def split(value):
    high = value.astype(BF16)
    return high, (value - high.astype(F32)).astype(BF16)


def left3(value):
    high, low = split(value)
    return jnp.concatenate([high, high, low], axis=1)


def right3(value):
    high, low = split(value)
    return jnp.concatenate([high, low, high], axis=0)


def mm(left, right):
    return jnp.dot(left, right, preferred_element_type=F32)


def as_row(column):
    return jnp.broadcast_to(column, (column.shape[0], 128)).T[0:1, :]


def prepare_kernel(x_ref, own_ref, x3_ref, own3_ref, y_ref, tu_ref, mean_ref):
    mean = jnp.sum(x_ref[...], axis=1, keepdims=True) * (1.0 / K)
    mean_ref[...] = mean
    high, low = split(x_ref[...] - mean)
    x3_ref[:, 0:K] = high
    x3_ref[:, K : 2 * K] = high
    x3_ref[:, 2 * K :] = low
    obs = own_ref[0:128, :]
    spread = obs - jnp.sum(obs, axis=1, keepdims=True) * (1.0 / K)
    high, low = split(spread)
    own3_ref[:, 0:K] = high
    own3_ref[:, K : 2 * K] = high
    own3_ref[:, 2 * K :] = low
    y_ref[...] = spread.T.astype(BF16)
    right = jnp.concatenate([high, low, high], axis=1)
    tu_ref[0:128, :] = mm_nt(own3_ref[...], right)
    tu_ref[128:, :] = mm_nt(x3_ref[...], right)


def mm_nt(left, right):
    return lax.dot_general(left, right, (((1,), (1,)), ((), ())), preferred_element_type=F32)


def server_kernel(
    x_ref, own_ref, x3_ref, own3_ref, y_ref, tu_ref, mean_ref, before_ref, after_ref, out_ref,
    near3, yr, y2, yt3, g2, u_ref, c_ref, d_ref, res
):
    innov, var, orow, ocol = [], [], [], []
    yt3[0:128, :] = own3_ref[:, 0:K]
    yt3[NOBS : NOBS + 128, :] = own3_ref[:, 2 * K :]
    yt3[2 * NOBS : 2 * NOBS + 128, :] = own3_ref[:, 0:K]
    y2[:, 0:128] = y_ref[...]
    y2[:, NOBS : NOBS + 128] = y_ref[...]
    for j, ref in enumerate((own_ref, before_ref, after_ref)):
        obs = ref[0:128, :]
        obs_mean = jnp.sum(obs, axis=1, keepdims=True) * (1.0 / K)
        if j:
            spread = obs - obs_mean
            high, low = split(spread)
            rows = slice((j - 1) * 128, j * 128)
            for n, (left, right) in enumerate(((high, high), (high, low), (low, high))):
                near3[rows, n * K : (n + 1) * K] = left
                yr[rows, n * K : (n + 1) * K] = right
                yt3[n * NOBS + j * 128 : n * NOBS + (j + 1) * 128, :] = right
            turned = spread.T.astype(BF16)
            y2[:, j * 128 : (j + 1) * 128] = turned
            y2[:, NOBS + j * 128 : NOBS + (j + 1) * 128] = turned
        cell = ref[128:129, 0:128].astype(jnp.int32)
        innov.append(ref[129:130, 0:128] - as_row(obs_mean))
        var.append(ref[130:131, 0:128])
        orow.append((cell // 8).astype(F32))
        ocol.append((cell % 8).astype(F32) + (0.0, -8.0, 8.0)[j])
    innov, var, orow, ocol = (jnp.concatenate(v, axis=1) for v in (innov, var, orow, ocol))

    first = own_ref[131:132, 0:1]
    swap = first > 32.0
    swap_scalar = jnp.max(first) > 32.0
    eye128 = lax.broadcasted_iota(jnp.int32, (128, 128), 0) == lax.broadcasted_iota(
        jnp.int32, (128, 128), 1
    )
    eye = jnp.where(
        lax.broadcasted_iota(jnp.int32, (NOBS, NOBS), 0)
        == lax.broadcasted_iota(jnp.int32, (NOBS, NOBS), 1),
        1.0,
        0.0,
    )
    both = range(2)
    zero, full = jnp.zeros_like(first), jnp.full_like(first, 64.0)
    lower = [jnp.where(swap, first, zero), jnp.where(swap, zero, first)]
    upper = [jnp.where(swap, full, first) - 1.0, jnp.where(swap, first, full) - 1.0]
    sg, sgd, sg_col, sgd_col, diag = [], [], [], [], []
    yt = yt3[0:NOBS, :].astype(F32) + yt3[NOBS : 2 * NOBS, :].astype(F32)
    for p in both:
        gap_row = jnp.maximum(jnp.maximum(lower[p] - orow, orow - upper[p]), 0.0) * (1.0 / 16.0)
        gap_col = jnp.maximum(jnp.maximum(-ocol, ocol - 7.0), 0.0) * (1.0 / 8.0)
        g = jnp.exp(-gap_row * gap_row - gap_col * gap_col) / var
        sg.append(jnp.sqrt(g))
        sgd.append(sg[p] * innov)
        cols = jnp.concatenate([sg[p], sgd[p], g, jnp.zeros((5, NOBS), F32)], axis=0).T
        sg_col.append(cols[:, 0:1])
        sgd_col.append(cols[:, 1:2])
        scaled = yt * cols[:, 2:3]
        diag.append(jnp.sum(scaled * yt, axis=0, keepdims=True))
        high, low = split(scaled)
        g2[0:NOBS, p * K : (p + 1) * K] = high
        g2[NOBS:, p * K : (p + 1) * K] = low

    tu = mm_nt(near3[...], yr[...])
    cross = mm_nt(own3_ref[...], yr[...])
    t_mat = jnp.concatenate(
        [
            jnp.concatenate([tu_ref[0:128, :], cross], axis=1),
            jnp.concatenate([cross.T, tu], axis=1),
        ],
        axis=0,
    )
    u_ref[:, 0:128] = tu_ref[128:, :]
    u_ref[:, 128:] = mm_nt(x3_ref[...], yr[...])

    sums = []
    for n in range(5):
        block = jnp.abs(mm(y2[...], g2[:, n * 256 : (n + 1) * 256]))
        for half in range(2):
            own = (2 * n + half) % 5
            part = block[:, half * 128 : (half + 1) * 128]
            rows = [part[i * 128 : (i + 1) * 128] for i in range(5)]
            rows[own] = jnp.where(eye128, 0.0, rows[own])
            total = (rows[0] + rows[1]) + (rows[2] + rows[3]) + rows[4]
            sums.append(jnp.sum(total, axis=0, keepdims=True))
    inv, q0, a1, m20, z20, z30 = [], [], [], [], [], []
    for p in both:
        total = jnp.concatenate(sums[5 * p : 5 * p + 5], axis=1) + diag[p]
        bound = (K - 1.0) + jnp.max(total, axis=1, keepdims=True)
        inv.append(1.0 / bound)
        q0.append((K - 1.0) * inv[p])
        a1.append(1.5 - 0.5 * q0[p])
        m20.append(1.5 - 0.5 * q0[p] * a1[p] * a1[p])
        z20.append(a1[p] * m20[p])
        z30.append(z20[p] * (1.5 - 0.5 * q0[p] * z20[p] * z20[p]))
    s = [(sg_col[p] * inv[p]) * t_mat * sg[p] for p in both]
    s_left = [left3(s[p]) for p in both]
    s2 = [mm(s_left[p], right3(s[p])) for p in both]
    k2 = [
        -0.5
        * (
            (a1[p] * a1[p] - q0[p] * a1[p]) * eye
            + (0.25 * q0[p] - a1[p]) * s[p]
            + 0.25 * s2[p]
        )
        for p in both
    ]
    m2 = [m20[p] * eye + mm(s_left[p], right3(k2[p])) for p in both]
    kz2 = [a1[p] * k2[p] - 0.5 * m2[p] for p in both]
    z2 = [z20[p] * eye + mm(s_left[p], right3(kz2[p])) for p in both]
    z2_right = [right3(z2[p]) for p in both]
    size = (256, 384)
    start = [
        pl.multiple_of(jnp.where(swap_scalar, 256, 0), 128),
        pl.multiple_of(jnp.where(swap_scalar, 0, 128), 128),
    ]
    v = [
        jnp.concatenate(
            [u_ref[pl.ds(start[p], size[p]), :] * sg[p], jnp.broadcast_to(sgd[p], (8, NOBS))],
            axis=0,
        )
        for p in both
    ]
    w1 = [mm(left3(v[p]), z2_right[p]) for p in both]
    w2 = [mm(left3(w1[p]), z2_right[p]) for p in both]
    tail = [
        1.5 * v[p] - (0.5 * q0[p]) * (w2[p] + z20[p] * w1[p] + (z20[p] * z20[p]) * v[p])
        for p in both
    ]
    hv = [
        mm(
            jnp.concatenate([left3(-0.5 * w2[p]), left3(tail[p])], axis=1),
            jnp.concatenate([z2_right[p], right3(kz2[p])], axis=0),
        )
        for p in both
    ]
    scale = [jnp.sqrt(q0[p]) for p in both]
    for p in (1, 0):
        n = size[p]
        rows = pl.ds(start[p], n)
        u_col = z30[p] * sgd_col[p] + jnp.sum(hv[p][n : n + 1] * s[p], axis=1, keepdims=True)
        su = jnp.sum(u_col * s[p], axis=0, keepdims=True)
        u = as_row(u_col)
        drift = inv[p] * jnp.sum(
            (z30[p] * u) * v[p][0:n] + su * hv[p][0:n], axis=1, keepdims=True
        )
        part = hv[p][0:n] * (sg[p] * (scale[p] * inv[p]))
        if p == 0:
            cell_row = (
                (lax.broadcasted_iota(jnp.int32, (n, 1), 0) + start[p]) // 8
            ).astype(F32)
            inside = (cell_row >= lower[0]) & (cell_row <= upper[0])
            part = jnp.where(inside, part, c_ref[rows, :])
            drift = jnp.where(inside, drift, d_ref[rows, :])
        c_ref[rows, :] = part
        d_ref[rows, :] = drift
    cell_row = (lax.broadcasted_iota(jnp.int32, (CELLS, 1), 0) // 8).astype(F32)
    inside = (cell_row >= lower[0]) & (cell_row <= upper[0])
    coef = jnp.where(inside, scale[0] * z30[0], scale[1] * z30[1])
    base = mean_ref[...] * (1.0 - coef) + d_ref[...]
    low = lane_iota() < 64
    for i in range(4):
        rows = slice(i * 128, (i + 1) * 128)
        res[rows, :] = (
            coef[rows] * x_ref[rows, :] + base[rows] + mm(left3(c_ref[rows, :]), yt3[...])
        )
        for l in range(4 * i, 4 * i + 4):

            def block(r, k):
                return res[32 * l + 8 * r : 32 * l + 8 * r + 8, k * 128 : (k + 1) * 128]

            for half in range(2):
                for k in range(4):
                    outs = pair_swap(block(2 * half, k), block(2 * half + 1, k))
                    for j, out in enumerate(outs):
                        dest = (2 * (2 * (k % 2) + j) + k // 2) * 16 + l
                        out_ref[dest, 2 * half : 2 * half + 2, :, :] = out.reshape(2, 4, 128)
            ends = [block(r, 4) for r in range(4)]
            for j, out in enumerate(block_transpose(ends, 16)):
                turned = roll(out, 64)
                first_half = jnp.where(low, out, pltpu.roll(turned, 4, 0))
                second_half = jnp.where(low, turned, pltpu.roll(out, 4, 0))
                out_ref[2 * j * 16 + l, 4, :, :] = first_half[0:4]
                out_ref[(2 * j + 1) * 16 + l, 4, :, :] = second_half[0:4]


def unpack_kernel(recv_ref, out_ref):
    for g in range(8):
        cols = slice(g * 128, (g + 1) * 128)
        for b in range(3):
            parts = []
            for w in range(16):
                src = PLACE[16 * g + w]
                if b < 2:
                    parts.append(recv_ref[src, 2 * b : 2 * b + 2, :, :].reshape(8, 128))
                else:
                    part = recv_ref[src, 4, :, :]
                    parts.append(jnp.concatenate([part, roll(part, 64)], axis=0))
            block = jnp.concatenate(parts, axis=0).T
            if b < 2:
                out_ref[0:64, 2 * b, cols] = block[0:64]
                out_ref[0:64, 2 * b + 1, cols] = block[64:128]
            else:
                for r in range(4):
                    out_ref[64:80, r, cols] = block[16 * r : 16 * r + 16]


WHOLE = pl.BlockSpec(memory_space=pltpu.VMEM)
THERE = pl.BlockSpec(memory_space=pltpu.HBM)


def call(kernel, out_shape, *args, scratch=(), name=None, vmem=16, ins=None, outs=None, cost=None):
    return pl.pallas_call(
        kernel,
        out_shape=out_shape,
        in_specs=ins or [WHOLE] * len(args),
        out_specs=outs or jax.tree.map(lambda _: WHOLE, out_shape),
        scratch_shapes=scratch,
        compiler_params=pltpu.CompilerParams(vmem_limit_bytes=vmem * 1024 * 1024),
        cost_estimate=cost,
        name=name,
    )(*args)


def shaped(*shape, dtype=F32):
    return jax.ShapeDtypeStruct(shape, dtype)


def per_device(ensemble, obs_cell, obs_value, obs_var, patch_rows):
    chunks = call(
        pack_kernel,
        shaped(64, 16, 4, 128),
        ensemble,
        obs_cell,
        obs_value,
        obs_var,
        patch_rows,
        scratch=[
            pltpu.VMEM((MEM, 4, 1024), F32),
            pltpu.VMEM((4, MEM, 1024), F32),
            pltpu.VMEM((64, 16, 4, 128), F32),
            pltpu.VMEM((1, 128), jnp.int32),
            pltpu.VMEM((1, 128), F32),
            pltpu.VMEM((1, 128), F32),
            pltpu.VMEM((1, 2), jnp.int32),
            pltpu.SemaphoreType.DMA((10,)),
            pltpu.SemaphoreType.DMA((4,)),
            pltpu.SemaphoreType.DMA((16,)),
        ],
        ins=[THERE] * 5,
        outs=THERE,
        name="pack",
        vmem=58,
    )
    recv = lax.all_to_all(chunks, CHIPS, split_axis=0, concat_axis=0, tiled=True)
    own, other = call(
        place_kernel, (shaped(65, 16, 384), shaped(65, 16, 384)), recv, name="place", vmem=4
    )
    other = lax.ppermute(other, "core", [(0, 1), (1, 0)])
    part = call(
        forecast_own_kernel,
        shaped(CELLS, 256),
        own,
        scratch=[pltpu.VMEM((66, 16, 256), F32)] * 2,
        name="forecast_own",
        vmem=6,
        cost=pl.CostEstimate(flops=8 << 20, bytes_accessed=8 << 20, transcendentals=0),
    )
    x, obs = call(
        forecast_kernel,
        (shaped(CELLS, K), shaped(136, K)),
        own,
        other,
        part,
        scratch=[pltpu.VMEM((66, 16, 384), F32)] * 2,
        name="forecast",
        vmem=10,
    )
    up = [(PLACE[s], PLACE[(s + 1) % 128]) for s in range(128)]
    down = [(b, a) for a, b in up]
    before = lax.ppermute(obs, ALL, up)
    after = lax.ppermute(obs, ALL, down)
    own = call(
        prepare_kernel,
        (
            shaped(CELLS, 3 * K, dtype=BF16),
            shaped(128, 3 * K, dtype=BF16),
            shaped(K, 128, dtype=BF16),
            shaped(128 + CELLS, 128),
            shaped(CELLS, 1),
        ),
        x,
        obs,
        name="prepare",
        vmem=6,
        cost=pl.CostEstimate(flops=2 * K * K * 128 * 3, bytes_accessed=8 << 20, transcendentals=0),
    )
    back = call(
        server_kernel,
        shaped(128, 5, 4, 128),
        x,
        obs,
        *own,
        before,
        after,
        scratch=[
            pltpu.VMEM((256, 3 * K), BF16),
            pltpu.VMEM((256, 3 * K), BF16),
            pltpu.VMEM((K, 2 * NOBS), BF16),
            pltpu.VMEM((3 * NOBS, K), BF16),
            pltpu.VMEM((2 * NOBS, 2 * K), BF16),
            pltpu.VMEM((CELLS, NOBS), F32),
            pltpu.VMEM((CELLS, NOBS), F32),
            pltpu.VMEM((CELLS, 1), F32),
            pltpu.VMEM((CELLS, K), F32),
        ],
        name="server",
        vmem=32,
    )
    back = lax.all_to_all(back, ALL, split_axis=0, concat_axis=0, tiled=True)
    return call(unpack_kernel, shaped(MEM, 4, 1024), back, name="unpack", vmem=6)


def solution(mesh):
    split_mesh = Mesh(mesh.devices.reshape(4, 2, 16), ALL)
    in_specs = (P(("y", "core"), "lat", None),) + (P(ALL, None),) * 4
    return jax.shard_map(
        per_device,
        mesh=split_mesh,
        in_specs=in_specs,
        out_specs=P(("y", "core"), "lat", None),
        check_vma=False,
    )
```

```python
import functools

import jax
import jax.numpy as jnp
import numpy as np
from jax import lax
from jax.experimental import pallas as pl
from jax.experimental.pallas import tpu as pltpu
from jax.sharding import Mesh
from jax.sharding import PartitionSpec as P

ALL = ("y", "core", "lat")
CHIPS = ("y", "lat")
K = 640
MEM = 80
NOBS = 384
CELLS = 512
F32 = jnp.float32
BF16 = jnp.bfloat16


def strip_places():
    columns = []
    for x in range(4):
        for y in range(4) if x % 2 == 0 else range(3, -1, -1):
            columns.append((x, y))
    places, z = [], 0
    for x, y in columns:
        for k in range(4):
            for core in range(2):
                places.append((y * 2 + core) * 16 + x * 4 + (z + k) % 4)
        z = (z + 3) % 4
    return places


PLACE = strip_places()
CHIP = [PLACE[2 * j] // 32 * 16 + PLACE[2 * j] % 16 for j in range(64)]


def lane_iota(rows=8):
    return lax.broadcasted_iota(jnp.int32, (rows, 128), 1)


def roll(value, shift):
    return pltpu.roll(value, shift % value.shape[-1], value.ndim - 1)


def block_transpose(values, size):
    values = list(values)
    count = len(values)
    lane = lane_iota()
    dist = 1
    while dist < count:
        low = (lane // (size * dist)) % 2 == 0
        for i in range(count):
            if i & dist:
                continue
            a, b = values[i], values[i + dist]
            values[i] = jnp.where(low, a, roll(b, size * dist))
            values[i + dist] = jnp.where(low, roll(a, -size * dist), b)
        dist *= 2
    return values


def pair_swap(a, b):
    low = lane_iota() < 64
    cross = roll(jnp.where(low, b, a), 64)
    return jnp.where(low, a, cross), jnp.where(low, cross, b)


def pack_kernel(
    ens_hbm, cell_hbm, value_hbm, var_hbm, rows_hbm, out_hbm,
    ens, moved, stage, cell, value, var, rows_v, ens_sem, meta_sem, out_sem
):
    loads = [
        pltpu.make_async_copy(ens_hbm.at[8 * i : 8 * i + 8], ens.at[8 * i : 8 * i + 8], ens_sem.at[i])
        for i in range(10)
    ]
    smalls = [
        pltpu.make_async_copy(src, dst, meta_sem.at[i])
        for i, (src, dst) in enumerate(
            ((cell_hbm, cell), (value_hbm, value), (var_hbm, var), (rows_hbm, rows_v))
        )
    ]
    for copy in loads + smalls:
        copy.start()
    for i in range(10):
        loads[i].wait()
        rows = slice(8 * i, 8 * i + 8)
        for r in range(4):
            moved[r, rows, :] = roll(ens[rows, r, :], 4)
    for copy in smalls:
        copy.wait()
    meta = jnp.concatenate(
        [
            cell[...].astype(F32),
            value[...],
            var[...],
            jnp.broadcast_to(rows_v[0:1, 0:1].astype(F32), (1, 128)),
        ],
        axis=0,
    )
    for chip in range(64):
        stage[chip, 15, :, :] = meta
    stores = []

    def send(column):
        base = min(CHIP[4 * column : 4 * column + 4])
        part = slice(base, base + 4)
        stores.append(
            pltpu.make_async_copy(stage.at[part], out_hbm.at[part], out_sem.at[column])
        )
        stores[-1].start()

    low = lane_iota() < 64

    def put(j, t, pair):
        for h in range(2):
            tile = 4 * t + 2 * h
            stage[CHIP[j % 64], tile : tile + 2, :, :] = pair[h].reshape(2, 4, 128)

    for g in range(8):
        cols = slice(g * 128, (g + 1) * 128)
        main = [
            jnp.concatenate([moved[2 * h, 0:64, cols], moved[2 * h + 1, 0:64, cols]], axis=0).T
            for h in range(2)
        ]
        tails = jnp.concatenate([moved[r, 64:80, cols] for r in range(4)] * 2, axis=0).T
        for w in range(16):
            rows = slice(8 * w, 8 * w + 8)
            pair = [main[0][rows], main[1][rows]]
            tail = tails[rows]
            j = 8 * g + w // 2
            if w % 2 == 0:
                put(j - 1, 2, pair)
                put(j, 0, pair)
                both = jnp.where(low, tail, pltpu.roll(tail, 4, 0))
                stage[CHIP[(j - 1) % 64], 14, :, :] = both[0:4]
            else:
                put(j, 1, pair)
                both = jnp.where(low, tails[8 * w - 8 : 8 * w], tail)
                stage[CHIP[j], 12:14, :, :] = both.reshape(2, 4, 128)
            if w % 8 == 0 and j > 0:
                send(j // 4 - 1)
    send(15)
    for copy in stores:
        copy.wait()


def chip_pair():
    y, lat = lax.axis_index("y"), lax.axis_index("lat")
    x, z = lat // 4, lat % 4
    column = x * 4 + jnp.where(x % 2 == 0, y, 3 - y)
    return 4 * column + (z + column) % 4


def place_kernel(recv_ref, own_ref, send_ref):
    def run(core):
        def put(row, t, cols, value):
            if t in (core, core + 1):
                at = 8 * (t - core)
                own_ref[row, at : at + 8, cols] = value
            other = 1 - core
            if t in (other, other + 1):
                at = 8 * (t - other)
                send_ref[row, at : at + 8, cols] = value

        def place(l, carry):
            def vreg(y, tile):
                return recv_ref[y * 16 + l, tile : tile + 2, :, :].reshape(8, 128)

            for t in range(3):
                for h in range(2):
                    for k in range(2):
                        tile = 4 * t + 2 * h
                        outs = pair_swap(vreg(2 * k, tile), vreg(2 * k + 1, tile))
                        for j, out in enumerate(outs):
                            put(4 * l + 2 * h + j, t, slice(128 * k, 128 * k + 128), out)
            last = slice(256, 384)
            outs = block_transpose([vreg(y, 12) for y in range(4)], 16)
            for r, out in enumerate(outs):
                turned = roll(out, 64)
                put(4 * l + r, 0, last, turned if core else out)
                put(4 * l + r, 1, last, out if core else turned)
            ends = []
            for y in range(4):
                part = recv_ref[y * 16 + l, 14, :, :]
                ends.append(jnp.concatenate([part, roll(part, 64)], axis=0))
            for r, out in enumerate(block_transpose(ends, 16)):
                put(4 * l + r, 2, last, roll(out, 64) if core else out)
            return carry

        lax.fori_loop(0, 16, place, 0, unroll=4)
        for ref, strip in (
            (own_ref, 2 * chip_pair() + core),
            (send_ref, 2 * chip_pair() + 1 - core),
        ):
            ref[64, 0:4, 0:128] = recv_ref[strip // 32 * 16 + strip % 16, 15, :, :]

    core = lax.axis_index("core")
    for value in range(2):
        pl.when(core == value)(functools.partial(run, value))


def advance(src, row, cols):
    c = src[row, :, cols]
    n = src[row - 1, :, cols]
    s = src[row + 1, :, cols]
    e = pltpu.roll(c, 15, 0)
    w = pltpu.roll(c, 1, 0)
    t = 0.1 * c
    return t + 0.4 * (n + s) + (0.05 - t) * e + (0.05 + t) * w


def march(first, fa, fb, finish):
    every = slice(None)
    for buf in (fa, fb):
        buf[0] = jnp.zeros(buf.shape[1:], F32)
        buf[65] = jnp.zeros(buf.shape[1:], F32)

    def load(i, carry):
        fa[i + 1] = first(i)
        return carry

    lax.fori_loop(0, 64, load, 0, unroll=8)
    for src, dst in ((fa, fb), (fb, fa), (fa, fb)):

        def move(i, carry):
            dst[i + 1] = advance(src, i + 1, every)
            return carry

        lax.fori_loop(0, 64, move, 0, unroll=8)

    def last(i, carry):
        finish(i, advance(fb, i + 1, every)[4:12, :])
        return carry

    lax.fori_loop(0, 64, last, 0, unroll=8)


def forecast_own_kernel(own_ref, x_ref, fa, fb):
    def finish(i, value):
        x_ref[pl.ds(pl.multiple_of(i * 8, 8), 8), :] = value

    march(lambda i: own_ref[i, :, 0:256], fa, fb, finish)


def forecast_kernel(own_ref, other_ref, part_ref, x_ref, obs_ref, fa, fb):
    core = lax.axis_index("core")
    low_core = core == 0
    low = lax.broadcasted_iota(jnp.int32, (16, 128), 1) < 64
    own_low = jnp.where(low_core, 1, 0)
    pick_own = low == (jnp.broadcast_to(own_low, (16, 128)) > 0)

    def first(i):
        ends = jnp.where(pick_own, own_ref[i, :, 256:384], other_ref[i, :, 256:384])
        return jnp.concatenate([other_ref[i, :, 0:256], ends], axis=1)

    def finish(i, value):
        rows = pl.ds(pl.multiple_of(i * 8, 8), 8)
        x_ref[rows, pl.ds(pl.multiple_of((1 - core) * 256, 128), 256)] = value[:, 0:256]
        x_ref[rows, pl.ds(pl.multiple_of(core * 256, 128), 256)] = part_ref[rows, :]
        x_ref[rows, 512:640] = value[:, 256:384]

    march(first, fa, fb, finish)
    here = jnp.broadcast_to(jnp.where((chip_pair() // 8) % 2 == core, 1, 0), (4, 128)) > 0
    meta = jnp.where(here, own_ref[64, 0:4, 0:128], other_ref[64, 0:4, 0:128])
    meta = jnp.concatenate([meta, jnp.zeros((4, 128), F32)], axis=0)
    cell = meta.T[:, 0:1]
    pick = jnp.where(
        lax.broadcasted_iota(jnp.int32, (128, CELLS), 1) == cell.astype(jnp.int32), 1.0, 0.0
    ).astype(BF16)
    for j in range(5):
        cols = slice(j * 128, (j + 1) * 128)
        x = x_ref[:, cols]
        x1 = x.astype(BF16)
        rest = x - x1.astype(F32)
        x2 = rest.astype(BF16)
        x3 = (rest - x2.astype(F32)).astype(BF16)
        obs_ref[0:128, cols] = mm(pick, x1) + mm(pick, x2) + mm(pick, x3)
    obs_ref[128:136, :] = jnp.zeros((8, K), F32)
    obs_ref[128:136, 0:128] = meta


def split(value):
    high = value.astype(BF16)
    return high, (value - high.astype(F32)).astype(BF16)


def left3(value):
    high, low = split(value)
    return jnp.concatenate([high, high, low], axis=1)


def right3(value):
    high, low = split(value)
    return jnp.concatenate([high, low, high], axis=0)


def mm(left, right):
    return jnp.dot(left, right, preferred_element_type=F32)


def as_row(column):
    return jnp.broadcast_to(column, (column.shape[0], 128)).T[0:1, :]


def prepare_kernel(x_ref, own_ref, x3_ref, own3_ref, y_ref, tu_ref, mean_ref):
    mean = jnp.sum(x_ref[...], axis=1, keepdims=True) * (1.0 / K)
    mean_ref[...] = mean
    high, low = split(x_ref[...] - mean)
    x3_ref[:, 0:K] = high
    x3_ref[:, K : 2 * K] = high
    x3_ref[:, 2 * K :] = low
    obs = own_ref[0:128, :]
    spread = obs - jnp.sum(obs, axis=1, keepdims=True) * (1.0 / K)
    high, low = split(spread)
    own3_ref[:, 0:K] = high
    own3_ref[:, K : 2 * K] = high
    own3_ref[:, 2 * K :] = low
    y_ref[...] = spread.T.astype(BF16)
    right = jnp.concatenate([high, low, high], axis=1)
    tu_ref[0:128, :] = mm_nt(own3_ref[...], right)
    tu_ref[128:, :] = mm_nt(x3_ref[...], right)


def beside_kernel(obs_ref, x3_ref, own3_ref, near3_ref, y_ref, tu_ref):
    obs = obs_ref[0:128, :]
    spread = obs - jnp.sum(obs, axis=1, keepdims=True) * (1.0 / K)
    high, low = split(spread)
    near3_ref[:, 0:K] = high
    near3_ref[:, K : 2 * K] = high
    near3_ref[:, 2 * K :] = low
    y_ref[...] = spread.T.astype(BF16)
    right = jnp.concatenate([high, low, high], axis=1)
    tu_ref[0:128, :] = mm_nt(own3_ref[...], right)
    tu_ref[128:256, :] = mm_nt(near3_ref[...], right)
    tu_ref[256:, :] = mm_nt(x3_ref[...], right)


def mm_nt(left, right):
    return lax.dot_general(left, right, (((1,), (1,)), ((), ())), preferred_element_type=F32)


def server_kernel(
    x_ref, own_ref, x3_ref, own3_ref, y_ref, tu_ref, mean_ref,
    near_ref, near3_ref, ny_ref, ntu_ref, far_ref, out_ref,
    far3, y2, yt3, g2, u_ref, c_ref, d_ref, res
):
    innov, var, orow, ocol = [], [], [], []
    side = jnp.where(lax.axis_index("core") == 0, 8.0, -8.0)
    for j, (ref, three, turned) in enumerate(
        ((own_ref, own3_ref, y_ref), (near_ref, near3_ref, ny_ref), (far_ref, None, None))
    ):
        obs = ref[0:128, :]
        obs_mean = jnp.sum(obs, axis=1, keepdims=True) * (1.0 / K)
        if three is None:
            spread = obs - obs_mean
            high, low = split(spread)
            far3[:, 0:K] = high
            far3[:, K : 2 * K] = high
            far3[:, 2 * K :] = low
            far_right = jnp.concatenate([high, low, high], axis=1)
            turned = spread.T.astype(BF16)
        else:
            high, low, turned = three[:, 0:K], three[:, 2 * K :], turned[...]
        for n, part in enumerate((high, low, high)):
            yt3[n * NOBS + j * 128 : n * NOBS + (j + 1) * 128, :] = part
        y2[:, j * 128 : (j + 1) * 128] = turned
        y2[:, NOBS + j * 128 : NOBS + (j + 1) * 128] = turned
        cell = ref[128:129, 0:128].astype(jnp.int32)
        innov.append(ref[129:130, 0:128] - as_row(obs_mean))
        var.append(ref[130:131, 0:128])
        orow.append((cell // 8).astype(F32))
        ocol.append((cell % 8).astype(F32) + (0.0, side, -side)[j])
    innov, var, orow, ocol = (jnp.concatenate(v, axis=1) for v in (innov, var, orow, ocol))

    first = own_ref[131:132, 0:1]
    swap = first > 32.0
    swap_scalar = jnp.max(first) > 32.0
    eye128 = lax.broadcasted_iota(jnp.int32, (128, 128), 0) == lax.broadcasted_iota(
        jnp.int32, (128, 128), 1
    )
    eye = jnp.where(
        lax.broadcasted_iota(jnp.int32, (NOBS, NOBS), 0)
        == lax.broadcasted_iota(jnp.int32, (NOBS, NOBS), 1),
        1.0,
        0.0,
    )
    both = range(2)
    zero, full = jnp.zeros_like(first), jnp.full_like(first, 64.0)
    lower = [jnp.where(swap, first, zero), jnp.where(swap, zero, first)]
    upper = [jnp.where(swap, full, first) - 1.0, jnp.where(swap, first, full) - 1.0]
    sg, sgd, sg_col, sgd_col, diag = [], [], [], [], []
    yt = yt3[0:NOBS, :].astype(F32) + yt3[NOBS : 2 * NOBS, :].astype(F32)
    for p in both:
        gap_row = jnp.maximum(jnp.maximum(lower[p] - orow, orow - upper[p]), 0.0) * (1.0 / 16.0)
        gap_col = jnp.maximum(jnp.maximum(-ocol, ocol - 7.0), 0.0) * (1.0 / 8.0)
        g = jnp.exp(-gap_row * gap_row - gap_col * gap_col) / var
        sg.append(jnp.sqrt(g))
        sgd.append(sg[p] * innov)
        cols = jnp.concatenate([sg[p], sgd[p], g, jnp.zeros((5, NOBS), F32)], axis=0).T
        sg_col.append(cols[:, 0:1])
        sgd_col.append(cols[:, 1:2])
        scaled = yt * cols[:, 2:3]
        diag.append(jnp.sum(scaled * yt, axis=0, keepdims=True))
        high, low = split(scaled)
        g2[0:NOBS, p * K : (p + 1) * K] = high
        g2[NOBS:, p * K : (p + 1) * K] = low

    t_own, t_near, t_far = (mm_nt(far_right, ref[...]) for ref in (own3_ref, near3_ref, far3))
    cross = ntu_ref[0:128, :]
    t_mat = jnp.concatenate(
        [
            jnp.concatenate([tu_ref[0:128, :], cross, t_own.T], axis=1),
            jnp.concatenate([cross.T, ntu_ref[128:256, :], t_near.T], axis=1),
            jnp.concatenate([t_own, t_near, t_far], axis=1),
        ],
        axis=0,
    )
    u_ref[:, 0:128] = tu_ref[128:, :]
    u_ref[:, 128:256] = ntu_ref[256:, :]
    u_ref[:, 256:384] = mm_nt(far_right, x3_ref[...]).T

    sums = []
    for n in range(5):
        block = jnp.abs(mm(y2[...], g2[:, n * 256 : (n + 1) * 256]))
        for half in range(2):
            own = (2 * n + half) % 5
            part = block[:, half * 128 : (half + 1) * 128]
            rows = [part[i * 128 : (i + 1) * 128] for i in range(5)]
            rows[own] = jnp.where(eye128, 0.0, rows[own])
            total = (rows[0] + rows[1]) + (rows[2] + rows[3]) + rows[4]
            sums.append(jnp.sum(total, axis=0, keepdims=True))
    inv, q0, a1, m20, z20, z30 = [], [], [], [], [], []
    for p in both:
        total = jnp.concatenate(sums[5 * p : 5 * p + 5], axis=1) + diag[p]
        bound = (K - 1.0) + jnp.max(total, axis=1, keepdims=True)
        inv.append(1.0 / bound)
        q0.append((K - 1.0) * inv[p])
        a1.append(1.5 - 0.5 * q0[p])
        m20.append(1.5 - 0.5 * q0[p] * a1[p] * a1[p])
        z20.append(a1[p] * m20[p])
        z30.append(z20[p] * (1.5 - 0.5 * q0[p] * z20[p] * z20[p]))
    s = [(sg_col[p] * inv[p]) * t_mat * sg[p] for p in both]
    s_right = [right3(s[p]) for p in both]
    s2 = [mm(left3(s[p]), s_right[p]) for p in both]
    s34 = [mm(left3(s2[p]), jnp.concatenate([s_right[p], right3(s2[p])], axis=1)) for p in both]
    kz2, z2 = [], []
    for p in both:
        s3, s4 = s34[p][:, 0:NOBS], s34[p][:, NOBS:]
        e0 = -0.5 * (a1[p] * a1[p] - q0[p] * a1[p])
        e1 = -0.5 * (0.25 * q0[p] - a1[p])
        c0 = a1[p] * e0 - 0.5 * m20[p]
        c1 = a1[p] * e1 - 0.5 * e0
        c2 = -0.125 * a1[p] - 0.5 * e1
        kz2.append(c0 * eye + c1 * s[p] + c2 * s2[p] + 0.0625 * s3)
        z2.append(z20[p] * eye + c0 * s[p] + c1 * s2[p] + c2 * s3 + 0.0625 * s4)
    z2_right = [right3(z2[p]) for p in both]
    size = (256, 384)
    start = [
        pl.multiple_of(jnp.where(swap_scalar, 256, 0), 128),
        pl.multiple_of(jnp.where(swap_scalar, 0, 128), 128),
    ]
    v = [
        jnp.concatenate(
            [u_ref[pl.ds(start[p], size[p]), :] * sg[p], jnp.broadcast_to(sgd[p], (8, NOBS))],
            axis=0,
        )
        for p in both
    ]
    w1 = [
        mm(
            left3(v[p]),
            jnp.concatenate([right3(z2[p] + q0[p] * kz2[p]), right3(kz2[p])], axis=1),
        )
        for p in both
    ]
    kv = [w1[p][:, NOBS:] for p in both]
    w2 = [mm(left3(w1[p][:, 0:NOBS]), z2_right[p]) for p in both]
    w3 = [mm(left3(w2[p] + (q0[p] * z20[p]) * kv[p]), z2_right[p]) for p in both]
    hv = [(1.5 - 0.5 * q0[p] * z20[p] * z20[p]) * kv[p] - 0.5 * w3[p] for p in both]
    scale = [jnp.sqrt(q0[p]) for p in both]
    for p in (1, 0):
        n = size[p]
        rows = pl.ds(start[p], n)
        u_col = z30[p] * sgd_col[p] + jnp.sum(hv[p][n : n + 1] * s[p], axis=1, keepdims=True)
        su = jnp.sum(u_col * s[p], axis=0, keepdims=True)
        u = as_row(u_col)
        drift = inv[p] * jnp.sum(
            (z30[p] * u) * v[p][0:n] + su * hv[p][0:n], axis=1, keepdims=True
        )
        part = hv[p][0:n] * (sg[p] * (scale[p] * inv[p]))
        if p == 0:
            cell_row = (
                (lax.broadcasted_iota(jnp.int32, (n, 1), 0) + start[p]) // 8
            ).astype(F32)
            inside = (cell_row >= lower[0]) & (cell_row <= upper[0])
            part = jnp.where(inside, part, c_ref[rows, :])
            drift = jnp.where(inside, drift, d_ref[rows, :])
        c_ref[rows, :] = part
        d_ref[rows, :] = drift
    cell_row = (lax.broadcasted_iota(jnp.int32, (CELLS, 1), 0) // 8).astype(F32)
    inside = (cell_row >= lower[0]) & (cell_row <= upper[0])
    coef = jnp.where(inside, scale[0] * z30[0], scale[1] * z30[1])
    base = mean_ref[...] * (1.0 - coef) + d_ref[...]
    low = lane_iota() < 64
    for i in range(4):
        rows = slice(i * 128, (i + 1) * 128)
        res[rows, :] = (
            coef[rows] * x_ref[rows, :] + base[rows] + mm(left3(c_ref[rows, :]), yt3[...])
        )
        for l in range(4 * i, 4 * i + 4):

            def block(r, k):
                return res[32 * l + 8 * r : 32 * l + 8 * r + 8, k * 128 : (k + 1) * 128]

            for half in range(2):
                for k in range(4):
                    outs = pair_swap(block(2 * half, k), block(2 * half + 1, k))
                    for j, out in enumerate(outs):
                        dest = (2 * (2 * (k % 2) + j) + k // 2) * 16 + l
                        out_ref[dest, 2 * half : 2 * half + 2, :, :] = out.reshape(2, 4, 128)
            ends = [block(r, 4) for r in range(4)]
            for j, out in enumerate(block_transpose(ends, 16)):
                turned = roll(out, 64)
                first_half = jnp.where(low, out, pltpu.roll(turned, 4, 0))
                second_half = jnp.where(low, turned, pltpu.roll(out, 4, 0))
                out_ref[2 * j * 16 + l, 4, :, :] = first_half[0:4]
                out_ref[(2 * j + 1) * 16 + l, 4, :, :] = second_half[0:4]


def unpack_kernel(recv_ref, out_ref):
    for g in range(8):
        cols = slice(g * 128, (g + 1) * 128)
        for b in range(3):
            parts = []
            for w in range(16):
                src = PLACE[16 * g + w]
                if b < 2:
                    parts.append(recv_ref[src, 2 * b : 2 * b + 2, :, :].reshape(8, 128))
                else:
                    part = recv_ref[src, 4, :, :]
                    parts.append(jnp.concatenate([part, roll(part, 64)], axis=0))
            block = jnp.concatenate(parts, axis=0).T
            if b < 2:
                out_ref[0:64, 2 * b, cols] = block[0:64]
                out_ref[0:64, 2 * b + 1, cols] = block[64:128]
            else:
                for r in range(4):
                    out_ref[64:80, r, cols] = block[16 * r : 16 * r + 16]


WHOLE = pl.BlockSpec(memory_space=pltpu.VMEM)
THERE = pl.BlockSpec(memory_space=pltpu.HBM)


def call(kernel, out_shape, *args, scratch=(), name=None, vmem=16, ins=None, outs=None, cost=None):
    return pl.pallas_call(
        kernel,
        out_shape=out_shape,
        in_specs=ins or [WHOLE] * len(args),
        out_specs=outs or jax.tree.map(lambda _: WHOLE, out_shape),
        scratch_shapes=scratch,
        compiler_params=pltpu.CompilerParams(vmem_limit_bytes=vmem * 1024 * 1024),
        cost_estimate=cost,
        name=name,
    )(*args)


def shaped(*shape, dtype=F32):
    return jax.ShapeDtypeStruct(shape, dtype)


def per_device(ensemble, obs_cell, obs_value, obs_var, patch_rows):
    chunks = call(
        pack_kernel,
        shaped(64, 16, 4, 128),
        ensemble,
        obs_cell,
        obs_value,
        obs_var,
        patch_rows,
        scratch=[
            pltpu.VMEM((MEM, 4, 1024), F32),
            pltpu.VMEM((4, MEM, 1024), F32),
            pltpu.VMEM((64, 16, 4, 128), F32),
            pltpu.VMEM((1, 128), jnp.int32),
            pltpu.VMEM((1, 128), F32),
            pltpu.VMEM((1, 128), F32),
            pltpu.VMEM((1, 2), jnp.int32),
            pltpu.SemaphoreType.DMA((10,)),
            pltpu.SemaphoreType.DMA((4,)),
            pltpu.SemaphoreType.DMA((16,)),
        ],
        ins=[THERE] * 5,
        outs=THERE,
        name="pack",
        vmem=58,
    )
    recv = lax.all_to_all(chunks, CHIPS, split_axis=0, concat_axis=0, tiled=True)
    own, other = call(
        place_kernel, (shaped(65, 16, 384), shaped(65, 16, 384)), recv, name="place", vmem=4
    )
    other = lax.ppermute(other, "core", [(0, 1), (1, 0)])
    part = call(
        forecast_own_kernel,
        shaped(CELLS, 256),
        own,
        scratch=[pltpu.VMEM((66, 16, 256), F32)] * 2,
        name="forecast_own",
        vmem=6,
        cost=pl.CostEstimate(flops=8 << 20, bytes_accessed=8 << 20, transcendentals=0),
    )
    x, obs = call(
        forecast_kernel,
        (shaped(CELLS, K), shaped(136, K)),
        own,
        other,
        part,
        scratch=[pltpu.VMEM((66, 16, 384), F32)] * 2,
        name="forecast",
        vmem=10,
    )
    far_pairs = [(PLACE[s], PLACE[(s + 1) % 128]) for s in range(1, 128, 2)]
    far = lax.ppermute(obs, ALL, far_pairs + [(b, a) for a, b in far_pairs])
    near = lax.ppermute(obs, "core", [(0, 1), (1, 0)])
    own = call(
        prepare_kernel,
        (
            shaped(CELLS, 3 * K, dtype=BF16),
            shaped(128, 3 * K, dtype=BF16),
            shaped(K, 128, dtype=BF16),
            shaped(128 + CELLS, 128),
            shaped(CELLS, 1),
        ),
        x,
        obs,
        name="prepare",
        vmem=6,
        cost=pl.CostEstimate(flops=2 * K * K * 128 * 3, bytes_accessed=8 << 20, transcendentals=0),
    )
    beside = call(
        beside_kernel,
        (
            shaped(128, 3 * K, dtype=BF16),
            shaped(K, 128, dtype=BF16),
            shaped(256 + CELLS, 128),
        ),
        near,
        *own[0:2],
        name="beside",
        vmem=6,
        cost=pl.CostEstimate(flops=2 * K * K * 128 * 3, bytes_accessed=8 << 20, transcendentals=0),
    )
    back = call(
        server_kernel,
        shaped(128, 5, 4, 128),
        x,
        obs,
        *own,
        near,
        *beside,
        far,
        scratch=[
            pltpu.VMEM((128, 3 * K), BF16),
            pltpu.VMEM((K, 2 * NOBS), BF16),
            pltpu.VMEM((3 * NOBS, K), BF16),
            pltpu.VMEM((2 * NOBS, 2 * K), BF16),
            pltpu.VMEM((CELLS, NOBS), F32),
            pltpu.VMEM((CELLS, NOBS), F32),
            pltpu.VMEM((CELLS, 1), F32),
            pltpu.VMEM((CELLS, K), F32),
        ],
        name="server",
        vmem=32,
    )
    back = lax.all_to_all(back, ALL, split_axis=0, concat_axis=0, tiled=True)
    return call(unpack_kernel, shaped(MEM, 4, 1024), back, name="unpack", vmem=6)


def solution(mesh):
    split_mesh = Mesh(mesh.devices.reshape(4, 2, 16), ALL)
    in_specs = (P(("y", "core"), "lat", None),) + (P(ALL, None),) * 4
    return jax.shard_map(
        per_device,
        mesh=split_mesh,
        in_specs=in_specs,
        out_specs=P(("y", "core"), "lat", None),
        check_vma=False,
    )
```

```python
import functools

import jax
import jax.numpy as jnp
import numpy as np
from jax import lax
from jax.experimental import pallas as pl
from jax.experimental.pallas import tpu as pltpu
from jax.sharding import Mesh
from jax.sharding import PartitionSpec as P

ALL = ("y", "core", "lat")
CHIPS = ("y", "lat")
K = 640
MEM = 80
NOBS = 384
CELLS = 512
F32 = jnp.float32
BF16 = jnp.bfloat16


def strip_places():
    columns = []
    for x in range(4):
        for y in range(4) if x % 2 == 0 else range(3, -1, -1):
            columns.append((x, y))
    places, z = [], 0
    for x, y in columns:
        for k in range(4):
            for core in range(2):
                places.append((y * 2 + core) * 16 + x * 4 + (z + k) % 4)
        z = (z + 3) % 4
    return places


PLACE = strip_places()
CHIP = [PLACE[2 * j] // 32 * 16 + PLACE[2 * j] % 16 for j in range(64)]


def lane_iota(rows=8):
    return lax.broadcasted_iota(jnp.int32, (rows, 128), 1)


def roll(value, shift):
    return pltpu.roll(value, shift % value.shape[-1], value.ndim - 1)


def block_transpose(values, size):
    values = list(values)
    count = len(values)
    lane = lane_iota()
    dist = 1
    while dist < count:
        low = (lane // (size * dist)) % 2 == 0
        for i in range(count):
            if i & dist:
                continue
            a, b = values[i], values[i + dist]
            values[i] = jnp.where(low, a, roll(b, size * dist))
            values[i + dist] = jnp.where(low, roll(a, -size * dist), b)
        dist *= 2
    return values


def pair_swap(a, b):
    low = lane_iota() < 64
    cross = roll(jnp.where(low, b, a), 64)
    return jnp.where(low, a, cross), jnp.where(low, cross, b)


def pack_kernel(
    ens_hbm, cell_hbm, value_hbm, var_hbm, rows_hbm, out_hbm,
    ens, moved, stage, cell, value, var, rows_v, ens_sem, meta_sem, out_sem
):
    loads = [
        pltpu.make_async_copy(ens_hbm.at[8 * i : 8 * i + 8], ens.at[8 * i : 8 * i + 8], ens_sem.at[i])
        for i in range(10)
    ]
    smalls = [
        pltpu.make_async_copy(src, dst, meta_sem.at[i])
        for i, (src, dst) in enumerate(
            ((cell_hbm, cell), (value_hbm, value), (var_hbm, var), (rows_hbm, rows_v))
        )
    ]
    for copy in loads + smalls:
        copy.start()
    for i in range(10):
        loads[i].wait()
        rows = slice(8 * i, 8 * i + 8)
        for r in range(4):
            moved[r, rows, :] = roll(ens[rows, r, :], 4)
    for copy in smalls:
        copy.wait()
    meta = jnp.concatenate(
        [
            cell[...].astype(F32),
            value[...],
            var[...],
            jnp.broadcast_to(rows_v[0:1, 0:1].astype(F32), (1, 128)),
        ],
        axis=0,
    )
    for chip in range(64):
        stage[chip, 15, :, :] = meta
    stores = []

    def send(column):
        base = min(CHIP[4 * column : 4 * column + 4])
        part = slice(base, base + 4)
        stores.append(
            pltpu.make_async_copy(stage.at[part], out_hbm.at[part], out_sem.at[column])
        )
        stores[-1].start()

    low = lane_iota() < 64

    def put(j, t, pair):
        for h in range(2):
            tile = 4 * t + 2 * h
            stage[CHIP[j % 64], tile : tile + 2, :, :] = pair[h].reshape(2, 4, 128)

    for g in range(8):
        cols = slice(g * 128, (g + 1) * 128)
        main = [
            jnp.concatenate([moved[2 * h, 0:64, cols], moved[2 * h + 1, 0:64, cols]], axis=0).T
            for h in range(2)
        ]
        tails = jnp.concatenate([moved[r, 64:80, cols] for r in range(4)] * 2, axis=0).T
        for w in range(16):
            rows = slice(8 * w, 8 * w + 8)
            pair = [main[0][rows], main[1][rows]]
            tail = tails[rows]
            j = 8 * g + w // 2
            if w % 2 == 0:
                put(j - 1, 2, pair)
                put(j, 0, pair)
                both = jnp.where(low, tail, pltpu.roll(tail, 4, 0))
                stage[CHIP[(j - 1) % 64], 14, :, :] = both[0:4]
            else:
                put(j, 1, pair)
                both = jnp.where(low, tails[8 * w - 8 : 8 * w], tail)
                stage[CHIP[j], 12:14, :, :] = both.reshape(2, 4, 128)
            if w % 8 == 0 and j > 0:
                send(j // 4 - 1)
    send(15)
    for copy in stores:
        copy.wait()


def chip_pair():
    y, lat = lax.axis_index("y"), lax.axis_index("lat")
    x, z = lat // 4, lat % 4
    column = x * 4 + jnp.where(x % 2 == 0, y, 3 - y)
    return 4 * column + (z + column) % 4


def place_kernel(recv_ref, own_ref, send_ref):
    def run(core):
        def put(row, t, cols, value):
            if t in (core, core + 1):
                at = 8 * (t - core)
                own_ref[row, at : at + 8, cols] = value
            other = 1 - core
            if t in (other, other + 1):
                at = 8 * (t - other)
                send_ref[row, at : at + 8, cols] = value

        def place(l, carry):
            def vreg(y, tile):
                return recv_ref[y * 16 + l, tile : tile + 2, :, :].reshape(8, 128)

            for t in range(3):
                for h in range(2):
                    for k in range(2):
                        tile = 4 * t + 2 * h
                        outs = pair_swap(vreg(2 * k, tile), vreg(2 * k + 1, tile))
                        for j, out in enumerate(outs):
                            put(4 * l + 2 * h + j, t, slice(128 * k, 128 * k + 128), out)
            last = slice(256, 384)
            outs = block_transpose([vreg(y, 12) for y in range(4)], 16)
            for r, out in enumerate(outs):
                turned = roll(out, 64)
                put(4 * l + r, 0, last, turned if core else out)
                put(4 * l + r, 1, last, out if core else turned)
            ends = []
            for y in range(4):
                part = recv_ref[y * 16 + l, 14, :, :]
                ends.append(jnp.concatenate([part, roll(part, 64)], axis=0))
            for r, out in enumerate(block_transpose(ends, 16)):
                put(4 * l + r, 2, last, roll(out, 64) if core else out)
            return carry

        lax.fori_loop(0, 16, place, 0, unroll=4)
        for ref, strip in (
            (own_ref, 2 * chip_pair() + core),
            (send_ref, 2 * chip_pair() + 1 - core),
        ):
            ref[64, 0:4, 0:128] = recv_ref[strip // 32 * 16 + strip % 16, 15, :, :]

    core = lax.axis_index("core")
    for value in range(2):
        pl.when(core == value)(functools.partial(run, value))


def advance(src, row, cols):
    c = src[row, :, cols]
    n = src[row - 1, :, cols]
    s = src[row + 1, :, cols]
    e = pltpu.roll(c, 15, 0)
    w = pltpu.roll(c, 1, 0)
    t = 0.1 * c
    return t + 0.4 * (n + s) + (0.05 - t) * e + (0.05 + t) * w


def march(first, fa, fb, finish):
    every = slice(None)
    for buf in (fa, fb):
        buf[0] = jnp.zeros(buf.shape[1:], F32)
        buf[65] = jnp.zeros(buf.shape[1:], F32)

    def load(i, carry):
        fa[i + 1] = first(i)
        return carry

    lax.fori_loop(0, 64, load, 0, unroll=8)
    for src, dst in ((fa, fb), (fb, fa), (fa, fb)):

        def move(i, carry):
            dst[i + 1] = advance(src, i + 1, every)
            return carry

        lax.fori_loop(0, 64, move, 0, unroll=8)

    def last(i, carry):
        finish(i, advance(fb, i + 1, every)[4:12, :])
        return carry

    lax.fori_loop(0, 64, last, 0, unroll=8)


def forecast_own_kernel(own_ref, x_ref, fa, fb):
    def finish(i, value):
        x_ref[pl.ds(pl.multiple_of(i * 8, 8), 8), :] = value

    march(lambda i: own_ref[i, :, 0:256], fa, fb, finish)


def forecast_kernel(own_ref, other_ref, part_ref, x_ref, obs_ref, fa, fb):
    core = lax.axis_index("core")
    low_core = core == 0
    low = lax.broadcasted_iota(jnp.int32, (16, 128), 1) < 64
    own_low = jnp.where(low_core, 1, 0)
    pick_own = low == (jnp.broadcast_to(own_low, (16, 128)) > 0)

    def first(i):
        ends = jnp.where(pick_own, own_ref[i, :, 256:384], other_ref[i, :, 256:384])
        return jnp.concatenate([other_ref[i, :, 0:256], ends], axis=1)

    def finish(i, value):
        rows = pl.ds(pl.multiple_of(i * 8, 8), 8)
        x_ref[rows, pl.ds(pl.multiple_of((1 - core) * 256, 128), 256)] = value[:, 0:256]
        x_ref[rows, pl.ds(pl.multiple_of(core * 256, 128), 256)] = part_ref[rows, :]
        x_ref[rows, 512:640] = value[:, 256:384]

    march(first, fa, fb, finish)
    here = jnp.broadcast_to(jnp.where((chip_pair() // 8) % 2 == core, 1, 0), (4, 128)) > 0
    meta = jnp.where(here, own_ref[64, 0:4, 0:128], other_ref[64, 0:4, 0:128])
    meta = jnp.concatenate([meta, jnp.zeros((4, 128), F32)], axis=0)
    cell = meta.T[:, 0:1]
    pick = jnp.where(
        lax.broadcasted_iota(jnp.int32, (128, CELLS), 1) == cell.astype(jnp.int32), 1.0, 0.0
    ).astype(BF16)
    for j in range(5):
        cols = slice(j * 128, (j + 1) * 128)
        x = x_ref[:, cols]
        x1 = x.astype(BF16)
        rest = x - x1.astype(F32)
        x2 = rest.astype(BF16)
        x3 = (rest - x2.astype(F32)).astype(BF16)
        obs_ref[0:128, cols] = mm(pick, x1) + mm(pick, x2) + mm(pick, x3)
    obs_ref[128:136, :] = jnp.zeros((8, K), F32)
    obs_ref[128:136, 0:128] = meta


def split(value):
    high = value.astype(BF16)
    return high, (value - high.astype(F32)).astype(BF16)


def left3(value):
    high, low = split(value)
    return jnp.concatenate([high, high, low], axis=1)


def right3(value):
    high, low = split(value)
    return jnp.concatenate([high, low, high], axis=0)


def mm(left, right):
    return jnp.dot(left, right, preferred_element_type=F32)


def as_row(column):
    return jnp.broadcast_to(column, (column.shape[0], 128)).T[0:1, :]


def prepare_kernel(x_ref, own_ref, x3_ref, own3_ref, y_ref, tu_ref, mean_ref):
    mean = jnp.sum(x_ref[...], axis=1, keepdims=True) * (1.0 / K)
    mean_ref[...] = mean
    high, low = split(x_ref[...] - mean)
    x3_ref[:, 0:K] = high
    x3_ref[:, K : 2 * K] = high
    x3_ref[:, 2 * K :] = low
    obs = own_ref[0:128, :]
    spread = obs - jnp.sum(obs, axis=1, keepdims=True) * (1.0 / K)
    high, low = split(spread)
    own3_ref[:, 0:K] = high
    own3_ref[:, K : 2 * K] = high
    own3_ref[:, 2 * K :] = low
    y_ref[...] = spread.T.astype(BF16)
    right = jnp.concatenate([high, low, high], axis=1)
    tu_ref[0:128, :] = mm_nt(own3_ref[...], right)
    tu_ref[128:, :] = mm_nt(x3_ref[...], right)


def patch_bounds(first):
    swap = first > 32.0
    zero, full = jnp.zeros_like(first), jnp.full_like(first, 64.0)
    lower = [jnp.where(swap, first, zero), jnp.where(swap, zero, first)]
    upper = [jnp.where(swap, full, first) - 1.0, jnp.where(swap, first, full) - 1.0]
    return lower, upper


def observed_places(ref, shift):
    cell = ref[128:129, 0:128].astype(jnp.int32)
    return (cell // 8).astype(F32), (cell % 8).astype(F32) + shift


def localize(orow, ocol, var, lower, upper):
    gap_row = jnp.maximum(jnp.maximum(lower - orow, orow - upper), 0.0) * (1.0 / 16.0)
    gap_col = jnp.maximum(jnp.maximum(-ocol, ocol - 7.0), 0.0) * (1.0 / 8.0)
    return jnp.exp(-gap_row * gap_row - gap_col * gap_col) / var


def side_shift():
    return jnp.where(lax.axis_index("core") == 0, 8.0, -8.0)


def beside_kernel(
    own_ref, obs_ref, x3_ref, own3_ref, turned_ref, near3_ref, tu_ref, gram_ref, y2, g2
):
    obs = obs_ref[0:128, :]
    spread = obs - jnp.sum(obs, axis=1, keepdims=True) * (1.0 / K)
    high, low = split(spread)
    near3_ref[:, 0:K] = high
    near3_ref[:, K : 2 * K] = high
    near3_ref[:, 2 * K :] = low
    right = jnp.concatenate([high, low, high], axis=1)
    tu_ref[0:128, :] = mm_nt(own3_ref[...], right)
    tu_ref[128:256, :] = mm_nt(near3_ref[...], right)
    tu_ref[256:, :] = mm_nt(x3_ref[...], right)
    turned = spread.T.astype(BF16)
    for n in range(2):
        y2[:, 256 * n : 256 * n + 128] = turned_ref[...]
        y2[:, 256 * n + 128 : 256 * n + 256] = turned
    places = [observed_places(own_ref, 0.0), observed_places(obs_ref, side_shift())]
    orow, ocol = (jnp.concatenate(v, axis=1) for v in zip(*places))
    var = jnp.concatenate([own_ref[130:131, 0:128], obs_ref[130:131, 0:128]], axis=1)
    lower, upper = patch_bounds(own_ref[131:132, 0:1])
    g = [localize(orow, ocol, var, lower[p], upper[p]) for p in range(2)]
    g_cols = jnp.concatenate(g + [jnp.zeros((6, 256), F32)], axis=0).T
    yt = jnp.concatenate(
        [own3_ref[:, 0:K].astype(F32) + own3_ref[:, 2 * K :].astype(F32), spread], axis=0
    )
    for p in range(2):
        high, low = split(yt * g_cols[:, p : p + 1])
        g2[0:256, p * K : (p + 1) * K] = high
        g2[256:512, p * K : (p + 1) * K] = low
    for n in range(5):
        cols = slice(n * 256, (n + 1) * 256)
        gram_ref[:, cols] = mm(y2[...], g2[:, cols])


def mm_nt(left, right):
    return lax.dot_general(left, right, (((1,), (1,)), ((), ())), preferred_element_type=F32)


def server_kernel(
    x_ref, own_ref, x3_ref, own3_ref, tu_ref, mean_ref,
    near_ref, near3_ref, ntu_ref, gram_ref, far_ref, out_ref,
    far3, y2, yt3, g2, u_ref, c_ref, d_ref, res
):
    innov, var, orow, ocol = [], [], [], []
    side = side_shift()
    for j, (ref, three) in enumerate(
        ((own_ref, own3_ref), (near_ref, near3_ref), (far_ref, None))
    ):
        obs = ref[0:128, :]
        obs_mean = jnp.sum(obs, axis=1, keepdims=True) * (1.0 / K)
        if three is None:
            spread = obs - obs_mean
            high, low = split(spread)
            far3[:, 0:K] = high
            far3[:, K : 2 * K] = high
            far3[:, 2 * K :] = low
            far_right = jnp.concatenate([high, low, high], axis=1)
            turned = spread.T.astype(BF16)
            y2[:, 0:128] = turned
            y2[:, 128:256] = turned
        else:
            high, low = three[:, 0:K], three[:, 2 * K :]
        for n, part in enumerate((high, low, high)):
            yt3[n * NOBS + j * 128 : n * NOBS + (j + 1) * 128, :] = part
        innov.append(ref[129:130, 0:128] - as_row(obs_mean))
        var.append(ref[130:131, 0:128])
        place = observed_places(ref, (0.0, side, -side)[j])
        orow.append(place[0])
        ocol.append(place[1])
    innov, var, orow, ocol = (jnp.concatenate(v, axis=1) for v in (innov, var, orow, ocol))

    first = own_ref[131:132, 0:1]
    swap_scalar = jnp.max(first) > 32.0
    eye128 = lax.broadcasted_iota(jnp.int32, (128, 128), 0) == lax.broadcasted_iota(
        jnp.int32, (128, 128), 1
    )
    eye = jnp.where(
        lax.broadcasted_iota(jnp.int32, (NOBS, NOBS), 0)
        == lax.broadcasted_iota(jnp.int32, (NOBS, NOBS), 1),
        1.0,
        0.0,
    )
    both = range(2)
    lower, upper = patch_bounds(first)
    sg, sgd, sg_col, sgd_col, diag = [], [], [], [], []
    yt = yt3[0:NOBS, :].astype(F32) + yt3[NOBS : 2 * NOBS, :].astype(F32)
    for p in both:
        g = localize(orow, ocol, var, lower[p], upper[p])
        sg.append(jnp.sqrt(g))
        sgd.append(sg[p] * innov)
        cols = jnp.concatenate([sg[p], sgd[p], g, jnp.zeros((5, NOBS), F32)], axis=0).T
        sg_col.append(cols[:, 0:1])
        sgd_col.append(cols[:, 1:2])
        scaled = yt * cols[:, 2:3]
        diag.append(jnp.sum(scaled * yt, axis=0, keepdims=True))
        high, low = split(scaled[256:384])
        g2[0:128, p * K : (p + 1) * K] = high
        g2[128:256, p * K : (p + 1) * K] = low

    t_own, t_near, t_far = (mm_nt(far_right, ref[...]) for ref in (own3_ref, near3_ref, far3))
    cross = ntu_ref[0:128, :]
    t_mat = jnp.concatenate(
        [
            jnp.concatenate([tu_ref[0:128, :], cross, t_own.T], axis=1),
            jnp.concatenate([cross.T, ntu_ref[128:256, :], t_near.T], axis=1),
            jnp.concatenate([t_own, t_near, t_far], axis=1),
        ],
        axis=0,
    )
    u_ref[:, 0:128] = tu_ref[128:, :]
    u_ref[:, 128:256] = ntu_ref[256:, :]
    u_ref[:, 256:384] = mm_nt(far_right, x3_ref[...]).T

    sums = []
    for n in range(5):
        cols = slice(n * 256, (n + 1) * 256)
        block = jnp.abs(gram_ref[:, cols] + mm(y2[...], g2[:, cols]))
        for half in range(2):
            own = (2 * n + half) % 5
            part = block[:, half * 128 : (half + 1) * 128]
            rows = [part[i * 128 : (i + 1) * 128] for i in range(5)]
            rows[own] = jnp.where(eye128, 0.0, rows[own])
            total = (rows[0] + rows[1]) + (rows[2] + rows[3]) + rows[4]
            sums.append(jnp.sum(total, axis=0, keepdims=True))
    inv, q0, a1, m20, z20, z30 = [], [], [], [], [], []
    for p in both:
        total = jnp.concatenate(sums[5 * p : 5 * p + 5], axis=1) + diag[p]
        bound = (K - 1.0) + jnp.max(total, axis=1, keepdims=True)
        inv.append(1.0 / bound)
        q0.append((K - 1.0) * inv[p])
        a1.append(1.5 - 0.5 * q0[p])
        m20.append(1.5 - 0.5 * q0[p] * a1[p] * a1[p])
        z20.append(a1[p] * m20[p])
        z30.append(z20[p] * (1.5 - 0.5 * q0[p] * z20[p] * z20[p]))
    s = [(sg_col[p] * inv[p]) * t_mat * sg[p] for p in both]
    s_right = [right3(s[p]) for p in both]
    s2 = [mm(left3(s[p]), s_right[p]) for p in both]
    s34 = [mm(left3(s2[p]), jnp.concatenate([s_right[p], right3(s2[p])], axis=1)) for p in both]
    kz2, z2 = [], []
    for p in both:
        s3, s4 = s34[p][:, 0:NOBS], s34[p][:, NOBS:]
        e0 = -0.5 * (a1[p] * a1[p] - q0[p] * a1[p])
        e1 = -0.5 * (0.25 * q0[p] - a1[p])
        c0 = a1[p] * e0 - 0.5 * m20[p]
        c1 = a1[p] * e1 - 0.5 * e0
        c2 = -0.125 * a1[p] - 0.5 * e1
        kz2.append(c0 * eye + c1 * s[p] + c2 * s2[p] + 0.0625 * s3)
        z2.append(z20[p] * eye + c0 * s[p] + c1 * s2[p] + c2 * s3 + 0.0625 * s4)
    z2_right = [right3(z2[p]) for p in both]
    size = (256, 384)
    start = [
        pl.multiple_of(jnp.where(swap_scalar, 256, 0), 128),
        pl.multiple_of(jnp.where(swap_scalar, 0, 128), 128),
    ]
    v = [
        jnp.concatenate(
            [u_ref[pl.ds(start[p], size[p]), :] * sg[p], jnp.broadcast_to(sgd[p], (8, NOBS))],
            axis=0,
        )
        for p in both
    ]
    w1 = [
        mm(
            left3(v[p]),
            jnp.concatenate([right3(z2[p] + q0[p] * kz2[p]), right3(kz2[p])], axis=1),
        )
        for p in both
    ]
    kv = [w1[p][:, NOBS:] for p in both]
    w2 = [mm(left3(w1[p][:, 0:NOBS]), z2_right[p]) for p in both]
    w3 = [mm(left3(w2[p] + (q0[p] * z20[p]) * kv[p]), z2_right[p]) for p in both]
    hv = [(1.5 - 0.5 * q0[p] * z20[p] * z20[p]) * kv[p] - 0.5 * w3[p] for p in both]
    scale = [jnp.sqrt(q0[p]) for p in both]
    for p in (1, 0):
        n = size[p]
        rows = pl.ds(start[p], n)
        u_col = z30[p] * sgd_col[p] + jnp.sum(hv[p][n : n + 1] * s[p], axis=1, keepdims=True)
        su = jnp.sum(u_col * s[p], axis=0, keepdims=True)
        u = as_row(u_col)
        drift = inv[p] * jnp.sum(
            (z30[p] * u) * v[p][0:n] + su * hv[p][0:n], axis=1, keepdims=True
        )
        part = hv[p][0:n] * (sg[p] * (scale[p] * inv[p]))
        if p == 0:
            cell_row = (
                (lax.broadcasted_iota(jnp.int32, (n, 1), 0) + start[p]) // 8
            ).astype(F32)
            inside = (cell_row >= lower[0]) & (cell_row <= upper[0])
            part = jnp.where(inside, part, c_ref[rows, :])
            drift = jnp.where(inside, drift, d_ref[rows, :])
        c_ref[rows, :] = part
        d_ref[rows, :] = drift
    cell_row = (lax.broadcasted_iota(jnp.int32, (CELLS, 1), 0) // 8).astype(F32)
    inside = (cell_row >= lower[0]) & (cell_row <= upper[0])
    coef = jnp.where(inside, scale[0] * z30[0], scale[1] * z30[1])
    base = mean_ref[...] * (1.0 - coef) + d_ref[...]
    low = lane_iota() < 64
    for i in range(4):
        rows = slice(i * 128, (i + 1) * 128)
        res[rows, :] = (
            coef[rows] * x_ref[rows, :] + base[rows] + mm(left3(c_ref[rows, :]), yt3[...])
        )
        for l in range(4 * i, 4 * i + 4):

            def block(r, k):
                return res[32 * l + 8 * r : 32 * l + 8 * r + 8, k * 128 : (k + 1) * 128]

            for half in range(2):
                for k in range(4):
                    outs = pair_swap(block(2 * half, k), block(2 * half + 1, k))
                    for j, out in enumerate(outs):
                        dest = (2 * (2 * (k % 2) + j) + k // 2) * 16 + l
                        out_ref[dest, 2 * half : 2 * half + 2, :, :] = out.reshape(2, 4, 128)
            ends = [block(r, 4) for r in range(4)]
            for j, out in enumerate(block_transpose(ends, 16)):
                turned = roll(out, 64)
                first_half = jnp.where(low, out, pltpu.roll(turned, 4, 0))
                second_half = jnp.where(low, turned, pltpu.roll(out, 4, 0))
                out_ref[2 * j * 16 + l, 4, :, :] = first_half[0:4]
                out_ref[(2 * j + 1) * 16 + l, 4, :, :] = second_half[0:4]


def unpack_kernel(recv_ref, out_ref):
    for g in range(8):
        cols = slice(g * 128, (g + 1) * 128)
        for b in range(3):
            parts = []
            for w in range(16):
                src = PLACE[16 * g + w]
                if b < 2:
                    parts.append(recv_ref[src, 2 * b : 2 * b + 2, :, :].reshape(8, 128))
                else:
                    part = recv_ref[src, 4, :, :]
                    parts.append(jnp.concatenate([part, roll(part, 64)], axis=0))
            block = jnp.concatenate(parts, axis=0).T
            if b < 2:
                out_ref[0:64, 2 * b, cols] = block[0:64]
                out_ref[0:64, 2 * b + 1, cols] = block[64:128]
            else:
                for r in range(4):
                    out_ref[64:80, r, cols] = block[16 * r : 16 * r + 16]


WHOLE = pl.BlockSpec(memory_space=pltpu.VMEM)
THERE = pl.BlockSpec(memory_space=pltpu.HBM)


def call(kernel, out_shape, *args, scratch=(), name=None, vmem=16, ins=None, outs=None, cost=None):
    return pl.pallas_call(
        kernel,
        out_shape=out_shape,
        in_specs=ins or [WHOLE] * len(args),
        out_specs=outs or jax.tree.map(lambda _: WHOLE, out_shape),
        scratch_shapes=scratch,
        compiler_params=pltpu.CompilerParams(vmem_limit_bytes=vmem * 1024 * 1024),
        cost_estimate=cost,
        name=name,
    )(*args)


def shaped(*shape, dtype=F32):
    return jax.ShapeDtypeStruct(shape, dtype)


def per_device(ensemble, obs_cell, obs_value, obs_var, patch_rows):
    chunks = call(
        pack_kernel,
        shaped(64, 16, 4, 128),
        ensemble,
        obs_cell,
        obs_value,
        obs_var,
        patch_rows,
        scratch=[
            pltpu.VMEM((MEM, 4, 1024), F32),
            pltpu.VMEM((4, MEM, 1024), F32),
            pltpu.VMEM((64, 16, 4, 128), F32),
            pltpu.VMEM((1, 128), jnp.int32),
            pltpu.VMEM((1, 128), F32),
            pltpu.VMEM((1, 128), F32),
            pltpu.VMEM((1, 2), jnp.int32),
            pltpu.SemaphoreType.DMA((10,)),
            pltpu.SemaphoreType.DMA((4,)),
            pltpu.SemaphoreType.DMA((16,)),
        ],
        ins=[THERE] * 5,
        outs=THERE,
        name="pack",
        vmem=58,
    )
    recv = lax.all_to_all(chunks, CHIPS, split_axis=0, concat_axis=0, tiled=True)
    own, other = call(
        place_kernel, (shaped(65, 16, 384), shaped(65, 16, 384)), recv, name="place", vmem=4
    )
    other = lax.ppermute(other, "core", [(0, 1), (1, 0)])
    part = call(
        forecast_own_kernel,
        shaped(CELLS, 256),
        own,
        scratch=[pltpu.VMEM((66, 16, 256), F32)] * 2,
        name="forecast_own",
        vmem=6,
        cost=pl.CostEstimate(flops=8 << 20, bytes_accessed=8 << 20, transcendentals=0),
    )
    x, obs = call(
        forecast_kernel,
        (shaped(CELLS, K), shaped(136, K)),
        own,
        other,
        part,
        scratch=[pltpu.VMEM((66, 16, 384), F32)] * 2,
        name="forecast",
        vmem=10,
    )
    far_pairs = [(PLACE[s], PLACE[(s + 1) % 128]) for s in range(1, 128, 2)]
    far = lax.ppermute(obs, ALL, far_pairs + [(b, a) for a, b in far_pairs])
    near = lax.ppermute(obs, "core", [(0, 1), (1, 0)])
    own = call(
        prepare_kernel,
        (
            shaped(CELLS, 3 * K, dtype=BF16),
            shaped(128, 3 * K, dtype=BF16),
            shaped(K, 128, dtype=BF16),
            shaped(128 + CELLS, 128),
            shaped(CELLS, 1),
        ),
        x,
        obs,
        name="prepare",
        vmem=6,
        cost=pl.CostEstimate(flops=2 * K * K * 128 * 3, bytes_accessed=8 << 20, transcendentals=0),
    )
    x3, own3, turned, tu, mean = own
    beside = call(
        beside_kernel,
        (
            shaped(128, 3 * K, dtype=BF16),
            shaped(256 + CELLS, 128),
            shaped(K, 2 * K),
        ),
        obs,
        near,
        x3,
        own3,
        turned,
        scratch=[pltpu.VMEM((K, 512), BF16), pltpu.VMEM((512, 2 * K), BF16)],
        name="beside",
        vmem=10,
        cost=pl.CostEstimate(flops=2 * K * K * 512 * 3, bytes_accessed=8 << 20, transcendentals=0),
    )
    back = call(
        server_kernel,
        shaped(128, 5, 4, 128),
        x,
        obs,
        x3,
        own3,
        tu,
        mean,
        near,
        *beside,
        far,
        scratch=[
            pltpu.VMEM((128, 3 * K), BF16),
            pltpu.VMEM((K, 256), BF16),
            pltpu.VMEM((3 * NOBS, K), BF16),
            pltpu.VMEM((256, 2 * K), BF16),
            pltpu.VMEM((CELLS, NOBS), F32),
            pltpu.VMEM((CELLS, NOBS), F32),
            pltpu.VMEM((CELLS, 1), F32),
            pltpu.VMEM((CELLS, K), F32),
        ],
        name="server",
        vmem=32,
    )
    back = lax.all_to_all(back, ALL, split_axis=0, concat_axis=0, tiled=True)
    return call(unpack_kernel, shaped(MEM, 4, 1024), back, name="unpack", vmem=6)


def solution(mesh):
    split_mesh = Mesh(mesh.devices.reshape(4, 2, 16), ALL)
    in_specs = (P(("y", "core"), "lat", None),) + (P(ALL, None),) * 4
    return jax.shard_map(
        per_device,
        mesh=split_mesh,
        in_specs=in_specs,
        out_specs=P(("y", "core"), "lat", None),
        check_vma=False,
    )
```

```python
import functools

import jax
import jax.numpy as jnp
import numpy as np
from jax import lax
from jax.experimental import pallas as pl
from jax.experimental.pallas import tpu as pltpu
from jax.sharding import Mesh
from jax.sharding import PartitionSpec as P

ALL = ("y", "core", "lat")
CHIPS = ("y", "lat")
K = 640
MEM = 80
NOBS = 384
CELLS = 512
F32 = jnp.float32
BF16 = jnp.bfloat16


def strip_places():
    columns = []
    for x in range(4):
        for y in range(4) if x % 2 == 0 else range(3, -1, -1):
            columns.append((x, y))
    places, z = [], 0
    for x, y in columns:
        for k in range(4):
            for core in range(2):
                places.append((y * 2 + core) * 16 + x * 4 + (z + k) % 4)
        z = (z + 3) % 4
    return places


PLACE = strip_places()
CHIP = [PLACE[2 * j] // 32 * 16 + PLACE[2 * j] % 16 for j in range(64)]


def lane_iota(rows=8):
    return lax.broadcasted_iota(jnp.int32, (rows, 128), 1)


def roll(value, shift):
    return pltpu.roll(value, shift % value.shape[-1], value.ndim - 1)


def block_transpose(values, size):
    values = list(values)
    count = len(values)
    lane = lane_iota()
    dist = 1
    while dist < count:
        low = (lane // (size * dist)) % 2 == 0
        for i in range(count):
            if i & dist:
                continue
            a, b = values[i], values[i + dist]
            values[i] = jnp.where(low, a, roll(b, size * dist))
            values[i + dist] = jnp.where(low, roll(a, -size * dist), b)
        dist *= 2
    return values


def pair_swap(a, b):
    low = lane_iota() < 64
    cross = roll(jnp.where(low, b, a), 64)
    return jnp.where(low, a, cross), jnp.where(low, cross, b)


def pack_kernel(
    ens_hbm, cell_hbm, value_hbm, var_hbm, rows_hbm, out_hbm,
    ens, moved, stage, cell, value, var, rows_v, ens_sem, meta_sem, out_sem
):
    loads = [
        pltpu.make_async_copy(ens_hbm.at[8 * i : 8 * i + 8], ens.at[8 * i : 8 * i + 8], ens_sem.at[i])
        for i in range(10)
    ]
    smalls = [
        pltpu.make_async_copy(src, dst, meta_sem.at[i])
        for i, (src, dst) in enumerate(
            ((cell_hbm, cell), (value_hbm, value), (var_hbm, var), (rows_hbm, rows_v))
        )
    ]
    for copy in loads + smalls:
        copy.start()
    for i in range(10):
        loads[i].wait()
        rows = slice(8 * i, 8 * i + 8)
        for r in range(4):
            moved[r, rows, :] = roll(0.1 * ens[rows, r, :], 4)
    for copy in smalls:
        copy.wait()
    meta = jnp.concatenate(
        [
            cell[...].astype(F32),
            value[...],
            var[...],
            jnp.broadcast_to(rows_v[0:1, 0:1].astype(F32), (1, 128)),
        ],
        axis=0,
    )
    for chip in range(64):
        stage[chip, 15, :, :] = meta
    stores = []

    def send(column):
        base = min(CHIP[4 * column : 4 * column + 4])
        part = slice(base, base + 4)
        stores.append(
            pltpu.make_async_copy(stage.at[part], out_hbm.at[part], out_sem.at[column])
        )
        stores[-1].start()

    low = lane_iota() < 64

    def put(j, t, pair):
        for h in range(2):
            tile = 4 * t + 2 * h
            stage[CHIP[j % 64], tile : tile + 2, :, :] = pair[h].reshape(2, 4, 128)

    for g in range(8):
        cols = slice(g * 128, (g + 1) * 128)
        main = [
            jnp.concatenate([moved[2 * h, 0:64, cols], moved[2 * h + 1, 0:64, cols]], axis=0).T
            for h in range(2)
        ]
        tails = jnp.concatenate([moved[r, 64:80, cols] for r in range(4)] * 2, axis=0).T
        for w in range(16):
            rows = slice(8 * w, 8 * w + 8)
            pair = [main[0][rows], main[1][rows]]
            tail = tails[rows]
            j = 8 * g + w // 2
            if w % 2 == 0:
                put(j - 1, 2, pair)
                put(j, 0, pair)
                both = jnp.where(low, tail, pltpu.roll(tail, 4, 0))
                stage[CHIP[(j - 1) % 64], 14, :, :] = both[0:4]
            else:
                put(j, 1, pair)
                both = jnp.where(low, tails[8 * w - 8 : 8 * w], tail)
                stage[CHIP[j], 12:14, :, :] = both.reshape(2, 4, 128)
            if w % 8 == 0 and j > 0:
                send(j // 4 - 1)
    send(15)
    for copy in stores:
        copy.wait()


def chip_pair():
    y, lat = lax.axis_index("y"), lax.axis_index("lat")
    x, z = lat // 4, lat % 4
    column = x * 4 + jnp.where(x % 2 == 0, y, 3 - y)
    return 4 * column + (z + column) % 4


def place_tiles(recv_ref, core, first, put):
    tiles = (first, first + 1)
    last = slice(256, 384)

    def place(l, carry):
        def vreg(y, tile):
            return recv_ref[y * 16 + l, tile : tile + 2, :, :].reshape(8, 128)

        for t in tiles:
            for h in range(2):
                for k in range(2):
                    tile = 4 * t + 2 * h
                    outs = pair_swap(vreg(2 * k, tile), vreg(2 * k + 1, tile))
                    for j, out in enumerate(outs):
                        put(4 * l + 2 * h + j, t - first, slice(128 * k, 128 * k + 128), out)
        outs = block_transpose([vreg(y, 12) for y in range(4)], 16)
        for r, out in enumerate(outs):
            turned = roll(out, 64)
            if 0 in tiles:
                put(4 * l + r, 0 - first, last, turned if core else out)
            put(4 * l + r, 1 - first, last, out if core else turned)
        if 2 in tiles:
            ends = []
            for y in range(4):
                part = recv_ref[y * 16 + l, 14, :, :]
                ends.append(jnp.concatenate([part, roll(part, 64)], axis=0))
            for r, out in enumerate(block_transpose(ends, 16)):
                put(4 * l + r, 2 - first, last, roll(out, 64) if core else out)
        return carry

    lax.fori_loop(0, 16, place, 0, unroll=2)


def for_core(run):
    core = lax.axis_index("core")
    for value in range(2):
        pl.when(core == value)(functools.partial(run, value))


def observations(recv_ref, strip):
    return recv_ref[strip // 32 * 16 + strip % 16, 15, :, :]


def place_kernel(recv_ref, send_ref):
    def run(core):
        def put(row, half, cols, value):
            send_ref[row, 8 * half : 8 * half + 8, cols] = value

        place_tiles(recv_ref, core, 1 - core, put)
        send_ref[64, 0:4, 0:128] = observations(recv_ref, 2 * chip_pair() + 1 - core)

    for_core(run)


def advance(src, row):
    n, c, s = ((src[row + d, 0:8, :], src[row + d, 8:16, :]) for d in (-1, 0, 1))
    column = lax.broadcasted_iota(jnp.int32, c[0].shape, 0)
    up = [pltpu.roll(v, 7, 0) for v in c]
    down = [pltpu.roll(v, 1, 0) for v in c]
    east = (jnp.where(column == 7, up[1], up[0]), up[1])
    west = (down[0], jnp.where(column == 0, down[0], down[1]))
    return [
        0.4 * ((n[h] + s[h]) + 0.125 * (east[h] + west[h])) + c[h] * ((west[h] - east[h]) + 0.1)
        for h in range(2)
    ]


def march(fa, fb, finish):
    for buf in (fa, fb):
        buf[0] = jnp.zeros(buf.shape[1:], F32)
        buf[65] = jnp.zeros(buf.shape[1:], F32)
    for src, dst in ((fa, fb), (fb, fa), (fa, fb)):

        def move(i, carry):
            for h, value in enumerate(advance(src, i + 1)):
                dst[i + 1, 8 * h : 8 * h + 8, :] = value
            return carry

        lax.fori_loop(0, 64, move, 0, unroll=8)

    def last(i, carry):
        a, b = (pltpu.roll(value, 4, 0) for value in advance(fb, i + 1))
        column = lax.broadcasted_iota(jnp.int32, a.shape, 0)
        finish(i, 10.0 * jnp.where(column < 4, a, b))
        return carry

    lax.fori_loop(0, 64, last, 0, unroll=8)


def forecast_own_kernel(recv_ref, x_ref, tail_ref, fa, fb):
    def run(core):
        def put(row, half, cols, value):
            rows = slice(8 * half, 8 * half + 8)
            if cols.start < 256:
                fa[row + 1, rows, cols] = value
            else:
                tail_ref[row, rows, :] = value

        place_tiles(recv_ref, core, core, put)
        tail_ref[64, 0:4, :] = observations(recv_ref, 2 * chip_pair() + core)

    for_core(run)

    def finish(i, value):
        x_ref[pl.ds(pl.multiple_of(i * 8, 8), 8), :] = value

    march(fa, fb, finish)


def forecast_kernel(tail_ref, other_ref, part_ref, x_ref, obs_ref, fa, fb):
    core = lax.axis_index("core")
    low_core = core == 0
    low = lax.broadcasted_iota(jnp.int32, (16, 128), 1) < 64
    own_low = jnp.where(low_core, 1, 0)
    pick_own = low == (jnp.broadcast_to(own_low, (16, 128)) > 0)

    def load(i, carry):
        fa[i + 1, :, 0:256] = other_ref[i, :, 0:256]
        fa[i + 1, :, 256:384] = jnp.where(pick_own, tail_ref[i], other_ref[i, :, 256:384])
        return carry

    lax.fori_loop(0, 64, load, 0, unroll=8)

    def finish(i, value):
        rows = pl.ds(pl.multiple_of(i * 8, 8), 8)
        x_ref[rows, pl.ds(pl.multiple_of((1 - core) * 256, 128), 256)] = value[:, 0:256]
        x_ref[rows, pl.ds(pl.multiple_of(core * 256, 128), 256)] = part_ref[rows, :]
        x_ref[rows, 512:640] = value[:, 256:384]

    march(fa, fb, finish)
    here = jnp.broadcast_to(jnp.where((chip_pair() // 8) % 2 == core, 1, 0), (4, 128)) > 0
    meta = jnp.where(here, tail_ref[64, 0:4, :], other_ref[64, 0:4, 0:128])
    meta = jnp.concatenate([meta, jnp.zeros((4, 128), F32)], axis=0)
    cell = meta.T[:, 0:1]
    pick = jnp.where(
        lax.broadcasted_iota(jnp.int32, (128, CELLS), 1) == cell.astype(jnp.int32), 1.0, 0.0
    ).astype(BF16)
    for j in range(5):
        cols = slice(j * 128, (j + 1) * 128)
        x = x_ref[:, cols]
        x1 = x.astype(BF16)
        rest = x - x1.astype(F32)
        x2 = rest.astype(BF16)
        x3 = (rest - x2.astype(F32)).astype(BF16)
        obs_ref[0:128, cols] = mm(pick, x1) + mm(pick, x2) + mm(pick, x3)
    obs_ref[128:136, :] = jnp.zeros((8, K), F32)
    obs_ref[128:136, 0:128] = meta


def split(value):
    high = value.astype(BF16)
    return high, (value - high.astype(F32)).astype(BF16)


def left3(value):
    high, low = split(value)
    return jnp.concatenate([high, high, low], axis=1)


def right3(value):
    high, low = split(value)
    return jnp.concatenate([high, low, high], axis=0)


def mm(left, right):
    return jnp.dot(left, right, preferred_element_type=F32)


def as_row(column):
    return jnp.broadcast_to(column, (column.shape[0], 128)).T[0:1, :]


def prepare_kernel(x_ref, own_ref, x3_ref, own3_ref, y_ref, tu_ref, mean_ref):
    mean = jnp.sum(x_ref[...], axis=1, keepdims=True) * (1.0 / K)
    mean_ref[...] = mean
    high, low = split(x_ref[...] - mean)
    x3_ref[:, 0:K] = high
    x3_ref[:, K : 2 * K] = high
    x3_ref[:, 2 * K :] = low
    obs = own_ref[0:128, :]
    spread = obs - jnp.sum(obs, axis=1, keepdims=True) * (1.0 / K)
    high, low = split(spread)
    own3_ref[:, 0:K] = high
    own3_ref[:, K : 2 * K] = high
    own3_ref[:, 2 * K :] = low
    y_ref[...] = spread.T.astype(BF16)
    right = jnp.concatenate([high, low, high], axis=1)
    tu_ref[0:128, :] = mm_nt(own3_ref[...], right)
    tu_ref[128:, :] = mm_nt(x3_ref[...], right)


def patch_bounds(first):
    swap = first > 32.0
    zero, full = jnp.zeros_like(first), jnp.full_like(first, 64.0)
    lower = [jnp.where(swap, first, zero), jnp.where(swap, zero, first)]
    upper = [jnp.where(swap, full, first) - 1.0, jnp.where(swap, first, full) - 1.0]
    return lower, upper


def observed_places(ref, shift):
    cell = ref[128:129, 0:128].astype(jnp.int32)
    return (cell // 8).astype(F32), (cell % 8).astype(F32) + shift


def localize(orow, ocol, var, lower, upper):
    gap_row = jnp.maximum(jnp.maximum(lower - orow, orow - upper), 0.0) * (1.0 / 16.0)
    gap_col = jnp.maximum(jnp.maximum(-ocol, ocol - 7.0), 0.0) * (1.0 / 8.0)
    return jnp.exp(-gap_row * gap_row - gap_col * gap_col) / var


def side_shift():
    return jnp.where(lax.axis_index("core") == 0, 8.0, -8.0)


def beside_kernel(
    own_ref, obs_ref, x3_ref, own3_ref, turned_ref, near3_ref, tu_ref, gram_ref, y2, g2
):
    obs = obs_ref[0:128, :]
    spread = obs - jnp.sum(obs, axis=1, keepdims=True) * (1.0 / K)
    high, low = split(spread)
    near3_ref[:, 0:K] = high
    near3_ref[:, K : 2 * K] = high
    near3_ref[:, 2 * K :] = low
    right = jnp.concatenate([high, low, high], axis=1)
    tu_ref[0:128, :] = mm_nt(own3_ref[...], right)
    tu_ref[128:256, :] = mm_nt(near3_ref[...], right)
    tu_ref[256:, :] = mm_nt(x3_ref[...], right)
    turned = spread.T.astype(BF16)
    for n in range(2):
        y2[:, 256 * n : 256 * n + 128] = turned_ref[...]
        y2[:, 256 * n + 128 : 256 * n + 256] = turned
    places = [observed_places(own_ref, 0.0), observed_places(obs_ref, side_shift())]
    orow, ocol = (jnp.concatenate(v, axis=1) for v in zip(*places))
    var = jnp.concatenate([own_ref[130:131, 0:128], obs_ref[130:131, 0:128]], axis=1)
    lower, upper = patch_bounds(own_ref[131:132, 0:1])
    g = [localize(orow, ocol, var, lower[p], upper[p]) for p in range(2)]
    g_cols = jnp.concatenate(g + [jnp.zeros((6, 256), F32)], axis=0).T
    yt = jnp.concatenate(
        [own3_ref[:, 0:K].astype(F32) + own3_ref[:, 2 * K :].astype(F32), spread], axis=0
    )
    for p in range(2):
        high, low = split(yt * g_cols[:, p : p + 1])
        g2[0:256, p * K : (p + 1) * K] = high
        g2[256:512, p * K : (p + 1) * K] = low
    for n in range(5):
        cols = slice(n * 256, (n + 1) * 256)
        gram_ref[:, cols] = mm(y2[...], g2[:, cols])


def mm_nt(left, right):
    return lax.dot_general(left, right, (((1,), (1,)), ((), ())), preferred_element_type=F32)


def server_kernel(
    x_ref, own_ref, x3_ref, own3_ref, tu_ref, mean_ref,
    near_ref, near3_ref, ntu_ref, gram_ref, far_ref, out_ref,
    far3, y2, yt3, g2, u_ref, c_ref, d_ref, res
):
    innov, var, orow, ocol = [], [], [], []
    side = side_shift()
    for j, (ref, three) in enumerate(
        ((own_ref, own3_ref), (near_ref, near3_ref), (far_ref, None))
    ):
        obs = ref[0:128, :]
        obs_mean = jnp.sum(obs, axis=1, keepdims=True) * (1.0 / K)
        if three is None:
            spread = obs - obs_mean
            high, low = split(spread)
            far3[:, 0:K] = high
            far3[:, K : 2 * K] = high
            far3[:, 2 * K :] = low
            far_right = jnp.concatenate([high, low, high], axis=1)
            turned = spread.T.astype(BF16)
            y2[:, 0:128] = turned
            y2[:, 128:256] = turned
        else:
            high, low = three[:, 0:K], three[:, 2 * K :]
        for n, part in enumerate((high, low, high)):
            yt3[n * NOBS + j * 128 : n * NOBS + (j + 1) * 128, :] = part
        innov.append(ref[129:130, 0:128] - as_row(obs_mean))
        var.append(ref[130:131, 0:128])
        place = observed_places(ref, (0.0, side, -side)[j])
        orow.append(place[0])
        ocol.append(place[1])
    innov, var, orow, ocol = (jnp.concatenate(v, axis=1) for v in (innov, var, orow, ocol))

    first = own_ref[131:132, 0:1]
    swap_scalar = jnp.max(first) > 32.0
    eye128 = lax.broadcasted_iota(jnp.int32, (128, 128), 0) == lax.broadcasted_iota(
        jnp.int32, (128, 128), 1
    )
    eye = jnp.where(
        lax.broadcasted_iota(jnp.int32, (NOBS, NOBS), 0)
        == lax.broadcasted_iota(jnp.int32, (NOBS, NOBS), 1),
        1.0,
        0.0,
    )
    both = range(2)
    lower, upper = patch_bounds(first)
    sg, sgd, sg_col, sgd_col, diag = [], [], [], [], []
    yt = yt3[0:NOBS, :].astype(F32) + yt3[NOBS : 2 * NOBS, :].astype(F32)
    for p in both:
        g = localize(orow, ocol, var, lower[p], upper[p])
        sg.append(jnp.sqrt(g))
        sgd.append(sg[p] * innov)
        cols = jnp.concatenate([sg[p], sgd[p], g, jnp.zeros((5, NOBS), F32)], axis=0).T
        sg_col.append(cols[:, 0:1])
        sgd_col.append(cols[:, 1:2])
        scaled = yt * cols[:, 2:3]
        diag.append(jnp.sum(scaled * yt, axis=0, keepdims=True))
        high, low = split(scaled[256:384])
        g2[0:128, p * K : (p + 1) * K] = high
        g2[128:256, p * K : (p + 1) * K] = low

    t_own, t_near, t_far = (mm_nt(far_right, ref[...]) for ref in (own3_ref, near3_ref, far3))
    cross = ntu_ref[0:128, :]
    t_mat = jnp.concatenate(
        [
            jnp.concatenate([tu_ref[0:128, :], cross, t_own.T], axis=1),
            jnp.concatenate([cross.T, ntu_ref[128:256, :], t_near.T], axis=1),
            jnp.concatenate([t_own, t_near, t_far], axis=1),
        ],
        axis=0,
    )
    u_ref[:, 0:128] = tu_ref[128:, :]
    u_ref[:, 128:256] = ntu_ref[256:, :]
    u_ref[:, 256:384] = mm_nt(far_right, x3_ref[...]).T

    sums = []
    for n in range(5):
        cols = slice(n * 256, (n + 1) * 256)
        block = jnp.abs(gram_ref[:, cols] + mm(y2[...], g2[:, cols]))
        for half in range(2):
            own = (2 * n + half) % 5
            part = block[:, half * 128 : (half + 1) * 128]
            rows = [part[i * 128 : (i + 1) * 128] for i in range(5)]
            rows[own] = jnp.where(eye128, 0.0, rows[own])
            total = (rows[0] + rows[1]) + (rows[2] + rows[3]) + rows[4]
            sums.append(jnp.sum(total, axis=0, keepdims=True))
    inv, q0, a1, m20, z20, z30 = [], [], [], [], [], []
    for p in both:
        total = jnp.concatenate(sums[5 * p : 5 * p + 5], axis=1) + diag[p]
        bound = (K - 1.0) + jnp.max(total, axis=1, keepdims=True)
        inv.append(1.0 / bound)
        q0.append((K - 1.0) * inv[p])
        a1.append(1.5 - 0.5 * q0[p])
        m20.append(1.5 - 0.5 * q0[p] * a1[p] * a1[p])
        z20.append(a1[p] * m20[p])
        z30.append(z20[p] * (1.5 - 0.5 * q0[p] * z20[p] * z20[p]))
    s = [(sg_col[p] * inv[p]) * t_mat * sg[p] for p in both]
    s_right = [right3(s[p]) for p in both]
    s2 = [mm(left3(s[p]), s_right[p]) for p in both]
    s34 = [mm(left3(s2[p]), jnp.concatenate([s_right[p], right3(s2[p])], axis=1)) for p in both]
    kz2, z2 = [], []
    for p in both:
        s3, s4 = s34[p][:, 0:NOBS], s34[p][:, NOBS:]
        e0 = -0.5 * (a1[p] * a1[p] - q0[p] * a1[p])
        e1 = -0.5 * (0.25 * q0[p] - a1[p])
        c0 = a1[p] * e0 - 0.5 * m20[p]
        c1 = a1[p] * e1 - 0.5 * e0
        c2 = -0.125 * a1[p] - 0.5 * e1
        kz2.append(c0 * eye + c1 * s[p] + c2 * s2[p] + 0.0625 * s3)
        z2.append(z20[p] * eye + c0 * s[p] + c1 * s2[p] + c2 * s3 + 0.0625 * s4)
    z2_right = [right3(z2[p]) for p in both]
    size = (256, 384)
    start = [
        pl.multiple_of(jnp.where(swap_scalar, 256, 0), 128),
        pl.multiple_of(jnp.where(swap_scalar, 0, 128), 128),
    ]
    v = [
        jnp.concatenate(
            [u_ref[pl.ds(start[p], size[p]), :] * sg[p], jnp.broadcast_to(sgd[p], (8, NOBS))],
            axis=0,
        )
        for p in both
    ]
    w1 = [
        mm(
            left3(v[p]),
            jnp.concatenate([right3(z2[p] + q0[p] * kz2[p]), right3(kz2[p])], axis=1),
        )
        for p in both
    ]
    kv = [w1[p][:, NOBS:] for p in both]
    w2 = [mm(left3(w1[p][:, 0:NOBS]), z2_right[p]) for p in both]
    w3 = [mm(left3(w2[p] + (q0[p] * z20[p]) * kv[p]), z2_right[p]) for p in both]
    hv = [(1.5 - 0.5 * q0[p] * z20[p] * z20[p]) * kv[p] - 0.5 * w3[p] for p in both]
    scale = [jnp.sqrt(q0[p]) for p in both]
    for p in (1, 0):
        n = size[p]
        rows = pl.ds(start[p], n)
        u_col = z30[p] * sgd_col[p] + jnp.sum(hv[p][n : n + 1] * s[p], axis=1, keepdims=True)
        su = jnp.sum(u_col * s[p], axis=0, keepdims=True)
        u = as_row(u_col)
        drift = inv[p] * jnp.sum(
            (z30[p] * u) * v[p][0:n] + su * hv[p][0:n], axis=1, keepdims=True
        )
        part = hv[p][0:n] * (sg[p] * (scale[p] * inv[p]))
        if p == 0:
            cell_row = (
                (lax.broadcasted_iota(jnp.int32, (n, 1), 0) + start[p]) // 8
            ).astype(F32)
            inside = (cell_row >= lower[0]) & (cell_row <= upper[0])
            part = jnp.where(inside, part, c_ref[rows, :])
            drift = jnp.where(inside, drift, d_ref[rows, :])
        c_ref[rows, :] = part
        d_ref[rows, :] = drift
    cell_row = (lax.broadcasted_iota(jnp.int32, (CELLS, 1), 0) // 8).astype(F32)
    inside = (cell_row >= lower[0]) & (cell_row <= upper[0])
    coef = jnp.where(inside, scale[0] * z30[0], scale[1] * z30[1])
    base = mean_ref[...] * (1.0 - coef) + d_ref[...]
    low = lane_iota() < 64
    for i in range(4):
        rows = slice(i * 128, (i + 1) * 128)
        res[rows, :] = (
            coef[rows] * x_ref[rows, :] + base[rows] + mm(left3(c_ref[rows, :]), yt3[...])
        )
        for l in range(4 * i, 4 * i + 4):

            def block(r, k):
                return res[32 * l + 8 * r : 32 * l + 8 * r + 8, k * 128 : (k + 1) * 128]

            for half in range(2):
                for k in range(4):
                    outs = pair_swap(block(2 * half, k), block(2 * half + 1, k))
                    for j, out in enumerate(outs):
                        dest = (2 * (2 * (k % 2) + j) + k // 2) * 16 + l
                        out_ref[dest, 2 * half : 2 * half + 2, :, :] = out.reshape(2, 4, 128)
            ends = [block(r, 4) for r in range(4)]
            for j, out in enumerate(block_transpose(ends, 16)):
                turned = roll(out, 64)
                first_half = jnp.where(low, out, pltpu.roll(turned, 4, 0))
                second_half = jnp.where(low, turned, pltpu.roll(out, 4, 0))
                out_ref[2 * j * 16 + l, 4, :, :] = first_half[0:4]
                out_ref[(2 * j + 1) * 16 + l, 4, :, :] = second_half[0:4]


def unpack_kernel(recv_ref, out_ref):
    for g in range(8):
        cols = slice(g * 128, (g + 1) * 128)
        for b in range(3):
            parts = []
            for w in range(16):
                src = PLACE[16 * g + w]
                if b < 2:
                    parts.append(recv_ref[src, 2 * b : 2 * b + 2, :, :].reshape(8, 128))
                else:
                    part = recv_ref[src, 4, :, :]
                    parts.append(jnp.concatenate([part, roll(part, 64)], axis=0))
            block = jnp.concatenate(parts, axis=0).T
            if b < 2:
                out_ref[0:64, 2 * b, cols] = block[0:64]
                out_ref[0:64, 2 * b + 1, cols] = block[64:128]
            else:
                for r in range(4):
                    out_ref[64:80, r, cols] = block[16 * r : 16 * r + 16]


WHOLE = pl.BlockSpec(memory_space=pltpu.VMEM)
THERE = pl.BlockSpec(memory_space=pltpu.HBM)


def call(kernel, out_shape, *args, scratch=(), name=None, vmem=16, ins=None, outs=None, cost=None):
    return pl.pallas_call(
        kernel,
        out_shape=out_shape,
        in_specs=ins or [WHOLE] * len(args),
        out_specs=outs or jax.tree.map(lambda _: WHOLE, out_shape),
        scratch_shapes=scratch,
        compiler_params=pltpu.CompilerParams(vmem_limit_bytes=vmem * 1024 * 1024),
        cost_estimate=cost,
        name=name,
    )(*args)


def shaped(*shape, dtype=F32):
    return jax.ShapeDtypeStruct(shape, dtype)


def per_device(ensemble, obs_cell, obs_value, obs_var, patch_rows):
    chunks = call(
        pack_kernel,
        shaped(64, 16, 4, 128),
        ensemble,
        obs_cell,
        obs_value,
        obs_var,
        patch_rows,
        scratch=[
            pltpu.VMEM((MEM, 4, 1024), F32),
            pltpu.VMEM((4, MEM, 1024), F32),
            pltpu.VMEM((64, 16, 4, 128), F32),
            pltpu.VMEM((1, 128), jnp.int32),
            pltpu.VMEM((1, 128), F32),
            pltpu.VMEM((1, 128), F32),
            pltpu.VMEM((1, 2), jnp.int32),
            pltpu.SemaphoreType.DMA((10,)),
            pltpu.SemaphoreType.DMA((4,)),
            pltpu.SemaphoreType.DMA((16,)),
        ],
        ins=[THERE] * 5,
        outs=THERE,
        name="pack",
        vmem=58,
    )
    recv = lax.all_to_all(chunks, CHIPS, split_axis=0, concat_axis=0, tiled=True)
    other = call(place_kernel, shaped(65, 16, 384), recv, name="place", vmem=4)
    other = lax.ppermute(other, "core", [(0, 1), (1, 0)])
    part, tail = call(
        forecast_own_kernel,
        (shaped(CELLS, 256), shaped(65, 16, 128)),
        recv,
        scratch=[pltpu.VMEM((66, 16, 256), F32)] * 2,
        name="forecast_own",
        vmem=6,
        cost=pl.CostEstimate(flops=8 << 20, bytes_accessed=8 << 20, transcendentals=0),
    )
    x, obs = call(
        forecast_kernel,
        (shaped(CELLS, K), shaped(136, K)),
        tail,
        other,
        part,
        scratch=[pltpu.VMEM((66, 16, 384), F32)] * 2,
        name="forecast",
        vmem=10,
    )
    far_pairs = [(PLACE[s], PLACE[(s + 1) % 128]) for s in range(1, 128, 2)]
    far = lax.ppermute(obs, ALL, far_pairs + [(b, a) for a, b in far_pairs])
    near = lax.ppermute(obs, "core", [(0, 1), (1, 0)])
    own = call(
        prepare_kernel,
        (
            shaped(CELLS, 3 * K, dtype=BF16),
            shaped(128, 3 * K, dtype=BF16),
            shaped(K, 128, dtype=BF16),
            shaped(128 + CELLS, 128),
            shaped(CELLS, 1),
        ),
        x,
        obs,
        name="prepare",
        vmem=6,
        cost=pl.CostEstimate(flops=2 * K * K * 128 * 3, bytes_accessed=8 << 20, transcendentals=0),
    )
    x3, own3, turned, tu, mean = own
    beside = call(
        beside_kernel,
        (
            shaped(128, 3 * K, dtype=BF16),
            shaped(256 + CELLS, 128),
            shaped(K, 2 * K),
        ),
        obs,
        near,
        x3,
        own3,
        turned,
        scratch=[pltpu.VMEM((K, 512), BF16), pltpu.VMEM((512, 2 * K), BF16)],
        name="beside",
        vmem=10,
        cost=pl.CostEstimate(flops=2 * K * K * 512 * 3, bytes_accessed=8 << 20, transcendentals=0),
    )
    back = call(
        server_kernel,
        shaped(128, 5, 4, 128),
        x,
        obs,
        x3,
        own3,
        tu,
        mean,
        near,
        *beside,
        far,
        scratch=[
            pltpu.VMEM((128, 3 * K), BF16),
            pltpu.VMEM((K, 256), BF16),
            pltpu.VMEM((3 * NOBS, K), BF16),
            pltpu.VMEM((256, 2 * K), BF16),
            pltpu.VMEM((CELLS, NOBS), F32),
            pltpu.VMEM((CELLS, NOBS), F32),
            pltpu.VMEM((CELLS, 1), F32),
            pltpu.VMEM((CELLS, K), F32),
        ],
        name="server",
        vmem=32,
    )
    back = lax.all_to_all(back, ALL, split_axis=0, concat_axis=0, tiled=True)
    return call(unpack_kernel, shaped(MEM, 4, 1024), back, name="unpack", vmem=6)


def solution(mesh):
    split_mesh = Mesh(mesh.devices.reshape(4, 2, 16), ALL)
    in_specs = (P(("y", "core"), "lat", None),) + (P(ALL, None),) * 4
    return jax.shard_map(
        per_device,
        mesh=split_mesh,
        in_specs=in_specs,
        out_specs=P(("y", "core"), "lat", None),
        check_vma=False,
    )
```

```python
import functools

import jax
import jax.numpy as jnp
import numpy as np
from jax import lax
from jax.experimental import pallas as pl
from jax.experimental.pallas import tpu as pltpu
from jax.sharding import Mesh
from jax.sharding import PartitionSpec as P

ALL = ("y", "core", "lat")
CHIPS = ("y", "lat")
K = 640
MEM = 80
NOBS = 384
CELLS = 512
F32 = jnp.float32
BF16 = jnp.bfloat16


def strip_places():
    columns = []
    for x in range(4):
        for y in range(4) if x % 2 == 0 else range(3, -1, -1):
            columns.append((x, y))
    places, z = [], 0
    for x, y in columns:
        for k in range(4):
            for core in range(2):
                places.append((y * 2 + core) * 16 + x * 4 + (z + k) % 4)
        z = (z + 3) % 4
    return places


PLACE = strip_places()
CHIP = [PLACE[2 * j] // 32 * 16 + PLACE[2 * j] % 16 for j in range(64)]


def lane_iota(rows=8):
    return lax.broadcasted_iota(jnp.int32, (rows, 128), 1)


def roll(value, shift):
    return pltpu.roll(value, shift % value.shape[-1], value.ndim - 1)


def block_transpose(values, size):
    values = list(values)
    count = len(values)
    lane = lane_iota()
    dist = 1
    while dist < count:
        low = (lane // (size * dist)) % 2 == 0
        for i in range(count):
            if i & dist:
                continue
            a, b = values[i], values[i + dist]
            values[i] = jnp.where(low, a, roll(b, size * dist))
            values[i + dist] = jnp.where(low, roll(a, -size * dist), b)
        dist *= 2
    return values


def pair_swap(a, b):
    low = lane_iota() < 64
    cross = roll(jnp.where(low, b, a), 64)
    return jnp.where(low, a, cross), jnp.where(low, cross, b)


def pack_kernel(
    ens_hbm, cell_hbm, value_hbm, var_hbm, rows_hbm, out_hbm,
    ens, moved, stage, cell, value, var, rows_v, ens_sem, meta_sem, out_sem
):
    loads = [
        pltpu.make_async_copy(ens_hbm.at[8 * i : 8 * i + 8], ens.at[8 * i : 8 * i + 8], ens_sem.at[i])
        for i in range(10)
    ]
    smalls = [
        pltpu.make_async_copy(src, dst, meta_sem.at[i])
        for i, (src, dst) in enumerate(
            ((cell_hbm, cell), (value_hbm, value), (var_hbm, var), (rows_hbm, rows_v))
        )
    ]
    for copy in loads + smalls:
        copy.start()
    for i in range(10):
        loads[i].wait()
        rows = slice(8 * i, 8 * i + 8)
        for r in range(4):
            moved[r, rows, :] = roll(0.1 * ens[rows, r, :], 4)
    for copy in smalls:
        copy.wait()
    meta = jnp.concatenate(
        [
            cell[...].astype(F32),
            value[...],
            var[...],
            jnp.broadcast_to(rows_v[0:1, 0:1].astype(F32), (1, 128)),
        ],
        axis=0,
    )
    for chip in range(64):
        stage[chip, 15, :, :] = meta
    stores = []

    def send(column):
        base = min(CHIP[4 * column : 4 * column + 4])
        part = slice(base, base + 4)
        stores.append(
            pltpu.make_async_copy(stage.at[part], out_hbm.at[part], out_sem.at[column])
        )
        stores[-1].start()

    low = lane_iota() < 64

    def put(j, t, pair):
        for h in range(2):
            tile = 4 * t + 2 * h
            stage[CHIP[j % 64], tile : tile + 2, :, :] = pair[h].reshape(2, 4, 128)

    for g in range(8):
        cols = slice(g * 128, (g + 1) * 128)
        main = [
            jnp.concatenate([moved[2 * h, 0:64, cols], moved[2 * h + 1, 0:64, cols]], axis=0).T
            for h in range(2)
        ]
        tails = jnp.concatenate([moved[r, 64:80, cols] for r in range(4)] * 2, axis=0).T
        for w in range(16):
            rows = slice(8 * w, 8 * w + 8)
            pair = [main[0][rows], main[1][rows]]
            tail = tails[rows]
            j = 8 * g + w // 2
            if w % 2 == 0:
                put(j - 1, 2, pair)
                put(j, 0, pair)
                both = jnp.where(low, tail, pltpu.roll(tail, 4, 0))
                stage[CHIP[(j - 1) % 64], 14, :, :] = both[0:4]
            else:
                put(j, 1, pair)
                both = jnp.where(low, tails[8 * w - 8 : 8 * w], tail)
                stage[CHIP[j], 12:14, :, :] = both.reshape(2, 4, 128)
            if w % 8 == 0 and j > 0:
                send(j // 4 - 1)
    send(15)
    for copy in stores:
        copy.wait()


def chip_pair():
    y, lat = lax.axis_index("y"), lax.axis_index("lat")
    x, z = lat // 4, lat % 4
    column = x * 4 + jnp.where(x % 2 == 0, y, 3 - y)
    return 4 * column + (z + column) % 4


def place_tiles(recv_ref, core, first, put):
    tiles = (first, first + 1)
    last = slice(256, 384)

    def place(l, carry):
        def vreg(y, tile):
            return recv_ref[y * 16 + l, tile : tile + 2, :, :].reshape(8, 128)

        for t in tiles:
            for h in range(2):
                for k in range(2):
                    tile = 4 * t + 2 * h
                    outs = pair_swap(vreg(2 * k, tile), vreg(2 * k + 1, tile))
                    for j, out in enumerate(outs):
                        put(4 * l + 2 * h + j, t - first, slice(128 * k, 128 * k + 128), out)
        outs = block_transpose([vreg(y, 12) for y in range(4)], 16)
        for r, out in enumerate(outs):
            turned = roll(out, 64)
            if 0 in tiles:
                put(4 * l + r, 0 - first, last, turned if core else out)
            put(4 * l + r, 1 - first, last, out if core else turned)
        if 2 in tiles:
            ends = []
            for y in range(4):
                part = recv_ref[y * 16 + l, 14, :, :]
                ends.append(jnp.concatenate([part, roll(part, 64)], axis=0))
            for r, out in enumerate(block_transpose(ends, 16)):
                put(4 * l + r, 2 - first, last, roll(out, 64) if core else out)
        return carry

    lax.fori_loop(0, 16, place, 0, unroll=4)


def for_core(run):
    core = lax.axis_index("core")
    for value in range(2):
        pl.when(core == value)(functools.partial(run, value))


def observations(recv_ref, strip):
    return recv_ref[strip // 32 * 16 + strip % 16, 15, :, :]


def place_kernel(recv_ref, send_ref):
    def run(core):
        def put(row, half, cols, value):
            send_ref[row, 8 * half : 8 * half + 8, cols] = value

        place_tiles(recv_ref, core, 1 - core, put)
        send_ref[64, 0:4, 0:128] = observations(recv_ref, 2 * chip_pair() + 1 - core)

    for_core(run)


def advance(src, row):
    n, c, s = ((src[row + d, 0:8, :], src[row + d, 8:16, :]) for d in (-1, 0, 1))
    column = lax.broadcasted_iota(jnp.int32, c[0].shape, 0)
    up = [pltpu.roll(v, 7, 0) for v in c]
    down = [pltpu.roll(v, 1, 0) for v in c]
    east = (jnp.where(column == 7, up[1], up[0]), up[1])
    west = (down[0], jnp.where(column == 0, down[0], down[1]))
    return [
        0.4 * ((n[h] + s[h]) + 0.125 * (east[h] + west[h])) + c[h] * ((west[h] - east[h]) + 0.1)
        for h in range(2)
    ]


def march(fa, fb, finish):
    for buf in (fa, fb):
        buf[0] = jnp.zeros(buf.shape[1:], F32)
        buf[65] = jnp.zeros(buf.shape[1:], F32)
    for src, dst in ((fa, fb), (fb, fa), (fa, fb)):

        def move(i, carry):
            for h, value in enumerate(advance(src, i + 1)):
                dst[i + 1, 8 * h : 8 * h + 8, :] = value
            return carry

        lax.fori_loop(0, 64, move, 0, unroll=8)

    def last(i, carry):
        a, b = (pltpu.roll(value, 4, 0) for value in advance(fb, i + 1))
        column = lax.broadcasted_iota(jnp.int32, a.shape, 0)
        finish(i, 10.0 * jnp.where(column < 4, a, b))
        return carry

    lax.fori_loop(0, 64, last, 0, unroll=8)


def forecast_own_kernel(recv_ref, x_ref, tail_ref, fa, fb):
    def run(core):
        def put(row, half, cols, value):
            rows = slice(8 * half, 8 * half + 8)
            if cols.start < 256:
                fa[row + 1, rows, cols] = value
            else:
                tail_ref[row, rows, :] = value

        place_tiles(recv_ref, core, core, put)
        tail_ref[64, 0:4, :] = observations(recv_ref, 2 * chip_pair() + core)

    for_core(run)

    def finish(i, value):
        x_ref[pl.ds(pl.multiple_of(i * 8, 8), 8), :] = value

    march(fa, fb, finish)


def forecast_kernel(tail_ref, other_ref, part_ref, x_ref, obs_ref, fa, fb):
    core = lax.axis_index("core")
    low_core = core == 0
    low = lax.broadcasted_iota(jnp.int32, (16, 128), 1) < 64
    own_low = jnp.where(low_core, 1, 0)
    pick_own = low == (jnp.broadcast_to(own_low, (16, 128)) > 0)

    def load(i, carry):
        fa[i + 1, :, 0:256] = other_ref[i, :, 0:256]
        fa[i + 1, :, 256:384] = jnp.where(pick_own, tail_ref[i], other_ref[i, :, 256:384])
        return carry

    lax.fori_loop(0, 64, load, 0, unroll=8)

    def finish(i, value):
        rows = pl.ds(pl.multiple_of(i * 8, 8), 8)
        x_ref[rows, pl.ds(pl.multiple_of((1 - core) * 256, 128), 256)] = value[:, 0:256]
        x_ref[rows, pl.ds(pl.multiple_of(core * 256, 128), 256)] = part_ref[rows, :]
        x_ref[rows, 512:640] = value[:, 256:384]

    march(fa, fb, finish)
    here = jnp.broadcast_to(jnp.where((chip_pair() // 8) % 2 == core, 1, 0), (4, 128)) > 0
    meta = jnp.where(here, tail_ref[64, 0:4, :], other_ref[64, 0:4, 0:128])
    meta = jnp.concatenate([meta, jnp.zeros((4, 128), F32)], axis=0)
    cell = meta.T[:, 0:1]
    pick = jnp.where(
        lax.broadcasted_iota(jnp.int32, (128, CELLS), 1) == cell.astype(jnp.int32), 1.0, 0.0
    ).astype(BF16)
    for j in range(5):
        cols = slice(j * 128, (j + 1) * 128)
        x = x_ref[:, cols]
        x1 = x.astype(BF16)
        rest = x - x1.astype(F32)
        x2 = rest.astype(BF16)
        x3 = (rest - x2.astype(F32)).astype(BF16)
        obs_ref[0:128, cols] = mm(pick, x1) + mm(pick, x2) + mm(pick, x3)
    obs_ref[128:136, :] = jnp.zeros((8, K), F32)
    obs_ref[128:136, 0:128] = meta


def split(value):
    high = value.astype(BF16)
    return high, (value - high.astype(F32)).astype(BF16)


def left3(value):
    high, low = split(value)
    return jnp.concatenate([high, high, low], axis=1)


def right3(value):
    high, low = split(value)
    return jnp.concatenate([high, low, high], axis=0)


def mm(left, right):
    return jnp.dot(left, right, preferred_element_type=F32)


def as_row(column):
    return jnp.broadcast_to(column, (column.shape[0], 128)).T[0:1, :]


def prepare_kernel(x_ref, own_ref, x3_ref, own3_ref, y_ref, tu_ref, mean_ref):
    mean = jnp.sum(x_ref[...], axis=1, keepdims=True) * (1.0 / K)
    mean_ref[...] = mean
    high, low = split(x_ref[...] - mean)
    x3_ref[:, 0:K] = high
    x3_ref[:, K : 2 * K] = high
    x3_ref[:, 2 * K :] = low
    obs = own_ref[0:128, :]
    spread = obs - jnp.sum(obs, axis=1, keepdims=True) * (1.0 / K)
    high, low = split(spread)
    own3_ref[:, 0:K] = high
    own3_ref[:, K : 2 * K] = high
    own3_ref[:, 2 * K :] = low
    y_ref[...] = spread.T.astype(BF16)
    right = jnp.concatenate([high, low, high], axis=1)
    tu_ref[0:128, :] = mm_nt(own3_ref[...], right)
    tu_ref[128:, :] = mm_nt(x3_ref[...], right)


def patch_bounds(first):
    swap = first > 32.0
    zero, full = jnp.zeros_like(first), jnp.full_like(first, 64.0)
    lower = [jnp.where(swap, first, zero), jnp.where(swap, zero, first)]
    upper = [jnp.where(swap, full, first) - 1.0, jnp.where(swap, first, full) - 1.0]
    return lower, upper


def observed_places(ref, shift):
    cell = ref[128:129, 0:128].astype(jnp.int32)
    return (cell // 8).astype(F32), (cell % 8).astype(F32) + shift


def localize(orow, ocol, var, lower, upper):
    gap_row = jnp.maximum(jnp.maximum(lower - orow, orow - upper), 0.0) * (1.0 / 16.0)
    gap_col = jnp.maximum(jnp.maximum(-ocol, ocol - 7.0), 0.0) * (1.0 / 8.0)
    return jnp.exp(-gap_row * gap_row - gap_col * gap_col) / var


def side_shift():
    return jnp.where(lax.axis_index("core") == 0, 8.0, -8.0)


def beside_kernel(
    own_ref, obs_ref, x3_ref, own3_ref, turned_ref, near3_ref, tu_ref, gram_ref, y2, g2
):
    obs = obs_ref[0:128, :]
    spread = obs - jnp.sum(obs, axis=1, keepdims=True) * (1.0 / K)
    high, low = split(spread)
    near3_ref[:, 0:K] = high
    near3_ref[:, K : 2 * K] = high
    near3_ref[:, 2 * K :] = low
    right = jnp.concatenate([high, low, high], axis=1)
    tu_ref[0:128, :] = mm_nt(own3_ref[...], right)
    tu_ref[128:256, :] = mm_nt(near3_ref[...], right)
    tu_ref[256:, :] = mm_nt(x3_ref[...], right)
    turned = spread.T.astype(BF16)
    for n in range(2):
        y2[:, 256 * n : 256 * n + 128] = turned_ref[...]
        y2[:, 256 * n + 128 : 256 * n + 256] = turned
    places = [observed_places(own_ref, 0.0), observed_places(obs_ref, side_shift())]
    orow, ocol = (jnp.concatenate(v, axis=1) for v in zip(*places))
    var = jnp.concatenate([own_ref[130:131, 0:128], obs_ref[130:131, 0:128]], axis=1)
    lower, upper = patch_bounds(own_ref[131:132, 0:1])
    g = [localize(orow, ocol, var, lower[p], upper[p]) for p in range(2)]
    g_cols = jnp.concatenate(g + [jnp.zeros((6, 256), F32)], axis=0).T
    yt = jnp.concatenate(
        [own3_ref[:, 0:K].astype(F32) + own3_ref[:, 2 * K :].astype(F32), spread], axis=0
    )
    for p in range(2):
        high, low = split(yt * g_cols[:, p : p + 1])
        g2[0:256, p * K : (p + 1) * K] = high
        g2[256:512, p * K : (p + 1) * K] = low
    for n in range(5):
        cols = slice(n * 256, (n + 1) * 256)
        gram_ref[:, cols] = mm(y2[...], g2[:, cols])


def mm_nt(left, right):
    return lax.dot_general(left, right, (((1,), (1,)), ((), ())), preferred_element_type=F32)


def server_kernel(
    x_ref, own_ref, x3_ref, own3_ref, tu_ref, mean_ref,
    near_ref, near3_ref, ntu_ref, gram_ref, far_ref, out_ref,
    far3, y2, yt3, g2, u_ref, c_ref, d_ref, res
):
    innov, var, orow, ocol = [], [], [], []
    side = side_shift()
    for j, (ref, three) in enumerate(
        ((own_ref, own3_ref), (near_ref, near3_ref), (far_ref, None))
    ):
        obs = ref[0:128, :]
        obs_mean = jnp.sum(obs, axis=1, keepdims=True) * (1.0 / K)
        if three is None:
            spread = obs - obs_mean
            high, low = split(spread)
            far3[:, 0:K] = high
            far3[:, K : 2 * K] = high
            far3[:, 2 * K :] = low
            far_right = jnp.concatenate([high, low, high], axis=1)
            turned = spread.T.astype(BF16)
            y2[:, 0:128] = turned
            y2[:, 128:256] = turned
        else:
            high, low = three[:, 0:K], three[:, 2 * K :]
        for n, part in enumerate((high, low, high)):
            yt3[n * NOBS + j * 128 : n * NOBS + (j + 1) * 128, :] = part
        innov.append(ref[129:130, 0:128] - as_row(obs_mean))
        var.append(ref[130:131, 0:128])
        place = observed_places(ref, (0.0, side, -side)[j])
        orow.append(place[0])
        ocol.append(place[1])
    innov, var, orow, ocol = (jnp.concatenate(v, axis=1) for v in (innov, var, orow, ocol))

    first = own_ref[131:132, 0:1]
    swap_scalar = jnp.max(first) > 32.0
    eye128 = lax.broadcasted_iota(jnp.int32, (128, 128), 0) == lax.broadcasted_iota(
        jnp.int32, (128, 128), 1
    )
    eye = jnp.where(
        lax.broadcasted_iota(jnp.int32, (NOBS, NOBS), 0)
        == lax.broadcasted_iota(jnp.int32, (NOBS, NOBS), 1),
        1.0,
        0.0,
    )
    both = range(2)
    lower, upper = patch_bounds(first)
    sg, sgd, sg_col, sgd_col, diag = [], [], [], [], []
    yt = yt3[0:NOBS, :].astype(F32) + yt3[NOBS : 2 * NOBS, :].astype(F32)
    for p in both:
        g = localize(orow, ocol, var, lower[p], upper[p])
        sg.append(jnp.sqrt(g))
        sgd.append(sg[p] * innov)
        cols = jnp.concatenate([sg[p], sgd[p], g, jnp.zeros((5, NOBS), F32)], axis=0).T
        sg_col.append(cols[:, 0:1])
        sgd_col.append(cols[:, 1:2])
        scaled = yt * cols[:, 2:3]
        diag.append(jnp.sum(scaled * yt, axis=0, keepdims=True))
        high, low = split(scaled[256:384])
        g2[0:128, p * K : (p + 1) * K] = high
        g2[128:256, p * K : (p + 1) * K] = low

    t_own, t_near, t_far = (mm_nt(far_right, ref[...]) for ref in (own3_ref, near3_ref, far3))
    cross = ntu_ref[0:128, :]
    t_mat = jnp.concatenate(
        [
            jnp.concatenate([tu_ref[0:128, :], cross, t_own.T], axis=1),
            jnp.concatenate([cross.T, ntu_ref[128:256, :], t_near.T], axis=1),
            jnp.concatenate([t_own, t_near, t_far], axis=1),
        ],
        axis=0,
    )
    u_ref[:, 0:128] = tu_ref[128:, :]
    u_ref[:, 128:256] = ntu_ref[256:, :]
    u_ref[:, 256:384] = mm_nt(far_right, x3_ref[...]).T

    sums = []
    for n in range(5):
        cols = slice(n * 256, (n + 1) * 256)
        block = jnp.abs(gram_ref[:, cols] + mm(y2[...], g2[:, cols]))
        for half in range(2):
            own = (2 * n + half) % 5
            part = block[:, half * 128 : (half + 1) * 128]
            rows = [part[i * 128 : (i + 1) * 128] for i in range(5)]
            rows[own] = jnp.where(eye128, 0.0, rows[own])
            total = (rows[0] + rows[1]) + (rows[2] + rows[3]) + rows[4]
            sums.append(jnp.sum(total, axis=0, keepdims=True))
    inv, q0, a1, m20, z20, z30 = [], [], [], [], [], []
    for p in both:
        total = jnp.concatenate(sums[5 * p : 5 * p + 5], axis=1) + diag[p]
        bound = (K - 1.0) + jnp.max(total, axis=1, keepdims=True)
        inv.append(1.0 / bound)
        q0.append((K - 1.0) * inv[p])
        a1.append(1.5 - 0.5 * q0[p])
        m20.append(1.5 - 0.5 * q0[p] * a1[p] * a1[p])
        z20.append(a1[p] * m20[p])
        z30.append(z20[p] * (1.5 - 0.5 * q0[p] * z20[p] * z20[p]))
    s = [(sg_col[p] * inv[p]) * t_mat * sg[p] for p in both]
    s_right = [right3(s[p]) for p in both]
    s2 = [mm(left3(s[p]), s_right[p]) for p in both]
    s34 = [mm(left3(s2[p]), jnp.concatenate([s_right[p], right3(s2[p])], axis=1)) for p in both]
    kz2, z2 = [], []
    for p in both:
        s3, s4 = s34[p][:, 0:NOBS], s34[p][:, NOBS:]
        e0 = -0.5 * (a1[p] * a1[p] - q0[p] * a1[p])
        e1 = -0.5 * (0.25 * q0[p] - a1[p])
        c0 = a1[p] * e0 - 0.5 * m20[p]
        c1 = a1[p] * e1 - 0.5 * e0
        c2 = -0.125 * a1[p] - 0.5 * e1
        kz2.append(c0 * eye + c1 * s[p] + c2 * s2[p] + 0.0625 * s3)
        z2.append(z20[p] * eye + c0 * s[p] + c1 * s2[p] + c2 * s3 + 0.0625 * s4)
    z2_right = [right3(z2[p]) for p in both]
    size = (256, 384)
    start = [
        pl.multiple_of(jnp.where(swap_scalar, 256, 0), 128),
        pl.multiple_of(jnp.where(swap_scalar, 0, 128), 128),
    ]
    v = [
        jnp.concatenate(
            [u_ref[pl.ds(start[p], size[p]), :] * sg[p], jnp.broadcast_to(sgd[p], (8, NOBS))],
            axis=0,
        )
        for p in both
    ]
    w1 = [
        mm(
            left3(v[p]),
            jnp.concatenate([right3(z2[p] + q0[p] * kz2[p]), right3(kz2[p])], axis=1),
        )
        for p in both
    ]
    kv = [w1[p][:, NOBS:] for p in both]
    w2 = [mm(left3(w1[p][:, 0:NOBS]), z2_right[p]) for p in both]
    w3 = [mm(left3(w2[p] + (q0[p] * z20[p]) * kv[p]), z2_right[p]) for p in both]
    hv = [(1.5 - 0.5 * q0[p] * z20[p] * z20[p]) * kv[p] - 0.5 * w3[p] for p in both]
    scale = [jnp.sqrt(q0[p]) for p in both]
    for p in (1, 0):
        n = size[p]
        rows = pl.ds(start[p], n)
        u_col = z30[p] * sgd_col[p] + jnp.sum(hv[p][n : n + 1] * s[p], axis=1, keepdims=True)
        su = jnp.sum(u_col * s[p], axis=0, keepdims=True)
        u = as_row(u_col)
        drift = inv[p] * jnp.sum(
            (z30[p] * u) * v[p][0:n] + su * hv[p][0:n], axis=1, keepdims=True
        )
        part = hv[p][0:n] * (sg[p] * (scale[p] * inv[p]))
        if p == 0:
            cell_row = (
                (lax.broadcasted_iota(jnp.int32, (n, 1), 0) + start[p]) // 8
            ).astype(F32)
            inside = (cell_row >= lower[0]) & (cell_row <= upper[0])
            part = jnp.where(inside, part, c_ref[rows, :])
            drift = jnp.where(inside, drift, d_ref[rows, :])
        c_ref[rows, :] = part
        d_ref[rows, :] = drift
    cell_row = (lax.broadcasted_iota(jnp.int32, (CELLS, 1), 0) // 8).astype(F32)
    inside = (cell_row >= lower[0]) & (cell_row <= upper[0])
    coef = jnp.where(inside, scale[0] * z30[0], scale[1] * z30[1])
    base = mean_ref[...] * (1.0 - coef) + d_ref[...]
    low = lane_iota() < 64
    for i in range(4):
        rows = slice(i * 128, (i + 1) * 128)
        res[rows, :] = (
            coef[rows] * x_ref[rows, :] + base[rows] + mm(left3(c_ref[rows, :]), yt3[...])
        )
        for l in range(4 * i, 4 * i + 4):

            def block(r, k):
                return res[32 * l + 8 * r : 32 * l + 8 * r + 8, k * 128 : (k + 1) * 128]

            for half in range(2):
                for k in range(4):
                    outs = pair_swap(block(2 * half, k), block(2 * half + 1, k))
                    for j, out in enumerate(outs):
                        dest = (2 * (2 * (k % 2) + j) + k // 2) * 16 + l
                        out_ref[dest, 2 * half : 2 * half + 2, :, :] = out.reshape(2, 4, 128)
            ends = [block(r, 4) for r in range(4)]
            for j, out in enumerate(block_transpose(ends, 16)):
                turned = roll(out, 64)
                first_half = jnp.where(low, out, pltpu.roll(turned, 4, 0))
                second_half = jnp.where(low, turned, pltpu.roll(out, 4, 0))
                out_ref[2 * j * 16 + l, 4, :, :] = first_half[0:4]
                out_ref[(2 * j + 1) * 16 + l, 4, :, :] = second_half[0:4]


def unpack_kernel(recv_ref, out_ref):
    for g in range(8):
        cols = slice(g * 128, (g + 1) * 128)
        for b in range(3):
            parts = []
            for w in range(16):
                src = PLACE[16 * g + w]
                if b < 2:
                    parts.append(recv_ref[src, 2 * b : 2 * b + 2, :, :].reshape(8, 128))
                else:
                    part = recv_ref[src, 4, :, :]
                    parts.append(jnp.concatenate([part, roll(part, 64)], axis=0))
            block = jnp.concatenate(parts, axis=0).T
            if b < 2:
                out_ref[0:64, 2 * b, cols] = block[0:64]
                out_ref[0:64, 2 * b + 1, cols] = block[64:128]
            else:
                for r in range(4):
                    out_ref[64:80, r, cols] = block[16 * r : 16 * r + 16]


WHOLE = pl.BlockSpec(memory_space=pltpu.VMEM)
THERE = pl.BlockSpec(memory_space=pltpu.HBM)


def call(kernel, out_shape, *args, scratch=(), name=None, vmem=16, ins=None, outs=None, cost=None):
    return pl.pallas_call(
        kernel,
        out_shape=out_shape,
        in_specs=ins or [WHOLE] * len(args),
        out_specs=outs or jax.tree.map(lambda _: WHOLE, out_shape),
        scratch_shapes=scratch,
        compiler_params=pltpu.CompilerParams(vmem_limit_bytes=vmem * 1024 * 1024),
        cost_estimate=cost,
        name=name,
    )(*args)


def shaped(*shape, dtype=F32):
    return jax.ShapeDtypeStruct(shape, dtype)


def per_device(ensemble, obs_cell, obs_value, obs_var, patch_rows):
    chunks = call(
        pack_kernel,
        shaped(64, 16, 4, 128),
        ensemble,
        obs_cell,
        obs_value,
        obs_var,
        patch_rows,
        scratch=[
            pltpu.VMEM((MEM, 4, 1024), F32),
            pltpu.VMEM((4, MEM, 1024), F32),
            pltpu.VMEM((64, 16, 4, 128), F32),
            pltpu.VMEM((1, 128), jnp.int32),
            pltpu.VMEM((1, 128), F32),
            pltpu.VMEM((1, 128), F32),
            pltpu.VMEM((1, 2), jnp.int32),
            pltpu.SemaphoreType.DMA((10,)),
            pltpu.SemaphoreType.DMA((4,)),
            pltpu.SemaphoreType.DMA((16,)),
        ],
        ins=[THERE] * 5,
        outs=THERE,
        name="pack",
        vmem=58,
    )
    recv = lax.all_to_all(chunks, CHIPS, split_axis=0, concat_axis=0, tiled=True)
    other = call(place_kernel, shaped(65, 16, 384), recv, name="place", vmem=4)
    other = lax.ppermute(other, "core", [(0, 1), (1, 0)])
    part, tail = call(
        forecast_own_kernel,
        (shaped(CELLS, 256), shaped(65, 16, 128)),
        recv,
        scratch=[pltpu.VMEM((66, 16, 256), F32)] * 2,
        name="forecast_own",
        vmem=6,
        cost=pl.CostEstimate(flops=8 << 20, bytes_accessed=8 << 20, transcendentals=0),
    )
    x, obs = call(
        forecast_kernel,
        (shaped(CELLS, K), shaped(136, K)),
        tail,
        other,
        part,
        scratch=[pltpu.VMEM((66, 16, 384), F32)] * 2,
        name="forecast",
        vmem=10,
    )
    far_pairs = [(PLACE[s], PLACE[(s + 1) % 128]) for s in range(1, 128, 2)]
    far = lax.ppermute(obs, ALL, far_pairs + [(b, a) for a, b in far_pairs])
    near = lax.ppermute(obs, "core", [(0, 1), (1, 0)])
    own = call(
        prepare_kernel,
        (
            shaped(CELLS, 3 * K, dtype=BF16),
            shaped(128, 3 * K, dtype=BF16),
            shaped(K, 128, dtype=BF16),
            shaped(128 + CELLS, 128),
            shaped(CELLS, 1),
        ),
        x,
        obs,
        name="prepare",
        vmem=6,
        cost=pl.CostEstimate(flops=2 * K * K * 128 * 3, bytes_accessed=8 << 20, transcendentals=0),
    )
    x3, own3, turned, tu, mean = own
    beside = call(
        beside_kernel,
        (
            shaped(128, 3 * K, dtype=BF16),
            shaped(256 + CELLS, 128),
            shaped(K, 2 * K),
        ),
        obs,
        near,
        x3,
        own3,
        turned,
        scratch=[pltpu.VMEM((K, 512), BF16), pltpu.VMEM((512, 2 * K), BF16)],
        name="beside",
        vmem=10,
        cost=pl.CostEstimate(flops=2 * K * K * 512 * 3, bytes_accessed=8 << 20, transcendentals=0),
    )
    back = call(
        server_kernel,
        shaped(128, 5, 4, 128),
        x,
        obs,
        x3,
        own3,
        tu,
        mean,
        near,
        *beside,
        far,
        scratch=[
            pltpu.VMEM((128, 3 * K), BF16),
            pltpu.VMEM((K, 256), BF16),
            pltpu.VMEM((3 * NOBS, K), BF16),
            pltpu.VMEM((256, 2 * K), BF16),
            pltpu.VMEM((CELLS, NOBS), F32),
            pltpu.VMEM((CELLS, NOBS), F32),
            pltpu.VMEM((CELLS, 1), F32),
            pltpu.VMEM((CELLS, K), F32),
        ],
        name="server",
        vmem=32,
    )
    back = lax.all_to_all(back, ALL, split_axis=0, concat_axis=0, tiled=True)
    return call(unpack_kernel, shaped(MEM, 4, 1024), back, name="unpack", vmem=6)


def solution(mesh):
    split_mesh = Mesh(mesh.devices.reshape(4, 2, 16), ALL)
    in_specs = (P(("y", "core"), "lat", None),) + (P(ALL, None),) * 4
    return jax.shard_map(
        per_device,
        mesh=split_mesh,
        in_specs=in_specs,
        out_specs=P(("y", "core"), "lat", None),
        check_vma=False,
    )
```

```python
import functools

import jax
import jax.numpy as jnp
import numpy as np
from jax import lax
from jax.experimental import pallas as pl
from jax.experimental.pallas import tpu as pltpu
from jax.sharding import Mesh
from jax.sharding import PartitionSpec as P

ALL = ("y", "core", "lat")
CHIPS = ("y", "lat")
K = 640
MEM = 80
NOBS = 384
CELLS = 512
F32 = jnp.float32
BF16 = jnp.bfloat16


def strip_places():
    columns = []
    for x in range(4):
        for y in range(4) if x % 2 == 0 else range(3, -1, -1):
            columns.append((x, y))
    places, z = [], 0
    for x, y in columns:
        for k in range(4):
            for core in range(2):
                places.append((y * 2 + core) * 16 + x * 4 + (z + k) % 4)
        z = (z + 3) % 4
    return places


PLACE = strip_places()
CHIP = [PLACE[2 * j] // 32 * 16 + PLACE[2 * j] % 16 for j in range(64)]


def lane_iota(rows=8):
    return lax.broadcasted_iota(jnp.int32, (rows, 128), 1)


def roll(value, shift):
    return pltpu.roll(value, shift % value.shape[-1], value.ndim - 1)


def block_transpose(values, size):
    values = list(values)
    count = len(values)
    lane = lane_iota()
    dist = 1
    while dist < count:
        low = (lane // (size * dist)) % 2 == 0
        for i in range(count):
            if i & dist:
                continue
            a, b = values[i], values[i + dist]
            values[i] = jnp.where(low, a, roll(b, size * dist))
            values[i + dist] = jnp.where(low, roll(a, -size * dist), b)
        dist *= 2
    return values


def pair_swap(a, b):
    low = lane_iota() < 64
    cross = roll(jnp.where(low, b, a), 64)
    return jnp.where(low, a, cross), jnp.where(low, cross, b)


def pack_kernel(
    ens_hbm, cell_hbm, value_hbm, var_hbm, rows_hbm, out_hbm,
    ens, moved, stage, cell, value, var, rows_v, ens_sem, meta_sem, out_sem
):
    loads = [
        pltpu.make_async_copy(ens_hbm.at[8 * i : 8 * i + 8], ens.at[8 * i : 8 * i + 8], ens_sem.at[i])
        for i in range(10)
    ]
    smalls = [
        pltpu.make_async_copy(src, dst, meta_sem.at[i])
        for i, (src, dst) in enumerate(
            ((cell_hbm, cell), (value_hbm, value), (var_hbm, var), (rows_hbm, rows_v))
        )
    ]
    for copy in loads + smalls:
        copy.start()
    for i in range(10):
        loads[i].wait()
        rows = slice(8 * i, 8 * i + 8)
        for r in range(4):
            moved[r, rows, :] = roll(0.1 * ens[rows, r, :], 4)
    for copy in smalls:
        copy.wait()
    meta = jnp.concatenate(
        [
            cell[...].astype(F32),
            value[...],
            var[...],
            jnp.broadcast_to(rows_v[0:1, 0:1].astype(F32), (1, 128)),
        ],
        axis=0,
    )
    for chip in range(64):
        stage[chip, 15, :, :] = meta
    stores = []

    def send(column):
        base = min(CHIP[4 * column : 4 * column + 4])
        part = slice(base, base + 4)
        stores.append(
            pltpu.make_async_copy(stage.at[part], out_hbm.at[part], out_sem.at[column])
        )
        stores[-1].start()

    low = lane_iota() < 64

    def put(j, t, pair):
        for h in range(2):
            tile = 4 * t + 2 * h
            stage[CHIP[j % 64], tile : tile + 2, :, :] = pair[h].reshape(2, 4, 128)

    for g in range(8):
        cols = slice(g * 128, (g + 1) * 128)
        main = [
            jnp.concatenate([moved[2 * h, 0:64, cols], moved[2 * h + 1, 0:64, cols]], axis=0).T
            for h in range(2)
        ]
        tails = jnp.concatenate([moved[r, 64:80, cols] for r in range(4)] * 2, axis=0).T
        for w in range(16):
            rows = slice(8 * w, 8 * w + 8)
            pair = [main[0][rows], main[1][rows]]
            tail = tails[rows]
            j = 8 * g + w // 2
            if w % 2 == 0:
                put(j - 1, 2, pair)
                put(j, 0, pair)
                both = jnp.where(low, tail, pltpu.roll(tail, 4, 0))
                stage[CHIP[(j - 1) % 64], 14, :, :] = both[0:4]
            else:
                put(j, 1, pair)
                both = jnp.where(low, tails[8 * w - 8 : 8 * w], tail)
                stage[CHIP[j], 12:14, :, :] = both.reshape(2, 4, 128)
            if w % 8 == 0 and j > 0:
                send(j // 4 - 1)
    send(15)
    for copy in stores:
        copy.wait()


def chip_pair():
    y, lat = lax.axis_index("y"), lax.axis_index("lat")
    x, z = lat // 4, lat % 4
    column = x * 4 + jnp.where(x % 2 == 0, y, 3 - y)
    return 4 * column + (z + column) % 4


def place_tiles(recv_ref, core, first, put):
    tiles = (first, first + 1)
    last = slice(256, 384)

    def place(l, carry):
        def vreg(y, tile):
            return recv_ref[y * 16 + l, tile : tile + 2, :, :].reshape(8, 128)

        for t in tiles:
            for h in range(2):
                for k in range(2):
                    tile = 4 * t + 2 * h
                    outs = pair_swap(vreg(2 * k, tile), vreg(2 * k + 1, tile))
                    for j, out in enumerate(outs):
                        put(4 * l + 2 * h + j, t - first, slice(128 * k, 128 * k + 128), out)
        outs = block_transpose([vreg(y, 12) for y in range(4)], 16)
        for r, out in enumerate(outs):
            turned = roll(out, 64)
            if 0 in tiles:
                put(4 * l + r, 0 - first, last, turned if core else out)
            put(4 * l + r, 1 - first, last, out if core else turned)
        if 2 in tiles:
            ends = []
            for y in range(4):
                part = recv_ref[y * 16 + l, 14, :, :]
                ends.append(jnp.concatenate([part, roll(part, 64)], axis=0))
            for r, out in enumerate(block_transpose(ends, 16)):
                put(4 * l + r, 2 - first, last, roll(out, 64) if core else out)
        return carry

    lax.fori_loop(0, 16, place, 0, unroll=4)


def for_core(run):
    core = lax.axis_index("core")
    for value in range(2):
        pl.when(core == value)(functools.partial(run, value))


def observations(recv_ref, strip):
    return recv_ref[strip // 32 * 16 + strip % 16, 15, :, :]


def place_kernel(recv_ref, send_ref):
    def run(core):
        def put(row, half, cols, value):
            send_ref[row, 8 * half : 8 * half + 8, cols] = value

        place_tiles(recv_ref, core, 1 - core, put)
        send_ref[64, 0:4, 0:128] = observations(recv_ref, 2 * chip_pair() + 1 - core)

    for_core(run)


def advance(src, row):
    n, c, s = ((src[row + d, 0:8, :], src[row + d, 8:16, :]) for d in (-1, 0, 1))
    column = lax.broadcasted_iota(jnp.int32, c[0].shape, 0)
    up = [pltpu.roll(v, 7, 0) for v in c]
    down = [pltpu.roll(v, 1, 0) for v in c]
    east = (jnp.where(column == 7, up[1], up[0]), up[1])
    west = (down[0], jnp.where(column == 0, down[0], down[1]))
    return [
        0.4 * ((n[h] + s[h]) + 0.125 * (east[h] + west[h])) + c[h] * ((west[h] - east[h]) + 0.1)
        for h in range(2)
    ]


def march(fa, fb, finish):
    for buf in (fa, fb):
        buf[0] = jnp.zeros(buf.shape[1:], F32)
        buf[65] = jnp.zeros(buf.shape[1:], F32)
    for src, dst in ((fa, fb), (fb, fa), (fa, fb)):

        def move(i, carry):
            for h, value in enumerate(advance(src, i + 1)):
                dst[i + 1, 8 * h : 8 * h + 8, :] = value
            return carry

        lax.fori_loop(0, 64, move, 0, unroll=16)

    def last(i, carry):
        a, b = (pltpu.roll(value, 4, 0) for value in advance(fb, i + 1))
        column = lax.broadcasted_iota(jnp.int32, a.shape, 0)
        finish(i, 10.0 * jnp.where(column < 4, a, b))
        return carry

    lax.fori_loop(0, 64, last, 0, unroll=16)


def forecast_own_kernel(recv_ref, x_ref, tail_ref, fa, fb):
    def run(core):
        def put(row, half, cols, value):
            rows = slice(8 * half, 8 * half + 8)
            if cols.start < 256:
                fa[row + 1, rows, cols] = value
            else:
                tail_ref[row, rows, :] = value

        place_tiles(recv_ref, core, core, put)
        tail_ref[64, 0:4, :] = observations(recv_ref, 2 * chip_pair() + core)

    for_core(run)

    def finish(i, value):
        x_ref[pl.ds(pl.multiple_of(i * 8, 8), 8), :] = value

    march(fa, fb, finish)


def forecast_kernel(tail_ref, other_ref, part_ref, x_ref, obs_ref, fa, fb):
    core = lax.axis_index("core")
    low_core = core == 0
    low = lax.broadcasted_iota(jnp.int32, (16, 128), 1) < 64
    own_low = jnp.where(low_core, 1, 0)
    pick_own = low == (jnp.broadcast_to(own_low, (16, 128)) > 0)

    def load(i, carry):
        fa[i + 1, :, 0:256] = other_ref[i, :, 0:256]
        fa[i + 1, :, 256:384] = jnp.where(pick_own, tail_ref[i], other_ref[i, :, 256:384])
        return carry

    lax.fori_loop(0, 64, load, 0, unroll=8)

    def finish(i, value):
        rows = pl.ds(pl.multiple_of(i * 8, 8), 8)
        x_ref[rows, pl.ds(pl.multiple_of((1 - core) * 256, 128), 256)] = value[:, 0:256]
        x_ref[rows, pl.ds(pl.multiple_of(core * 256, 128), 256)] = part_ref[rows, :]
        x_ref[rows, 512:640] = value[:, 256:384]

    march(fa, fb, finish)
    here = jnp.broadcast_to(jnp.where((chip_pair() // 8) % 2 == core, 1, 0), (4, 128)) > 0
    meta = jnp.where(here, tail_ref[64, 0:4, :], other_ref[64, 0:4, 0:128])
    meta = jnp.concatenate([meta, jnp.zeros((4, 128), F32)], axis=0)
    cell = meta.T[:, 0:1]
    pick = jnp.where(
        lax.broadcasted_iota(jnp.int32, (128, CELLS), 1) == cell.astype(jnp.int32), 1.0, 0.0
    ).astype(BF16)
    for j in range(5):
        cols = slice(j * 128, (j + 1) * 128)
        x = x_ref[:, cols]
        x1 = x.astype(BF16)
        rest = x - x1.astype(F32)
        x2 = rest.astype(BF16)
        x3 = (rest - x2.astype(F32)).astype(BF16)
        obs_ref[0:128, cols] = mm(pick, x1) + mm(pick, x2) + mm(pick, x3)
    obs_ref[128:136, :] = jnp.zeros((8, K), F32)
    obs_ref[128:136, 0:128] = meta


def split(value):
    high = value.astype(BF16)
    return high, (value - high.astype(F32)).astype(BF16)


def left3(value):
    high, low = split(value)
    return jnp.concatenate([high, high, low], axis=1)


def right3(value):
    high, low = split(value)
    return jnp.concatenate([high, low, high], axis=0)


def mm(left, right):
    return jnp.dot(left, right, preferred_element_type=F32)


def as_row(column):
    return jnp.broadcast_to(column, (column.shape[0], 128)).T[0:1, :]


def prepare_kernel(x_ref, own_ref, x3_ref, own3_ref, y_ref, tu_ref, mean_ref):
    mean = jnp.sum(x_ref[...], axis=1, keepdims=True) * (1.0 / K)
    mean_ref[...] = mean
    high, low = split(x_ref[...] - mean)
    x3_ref[:, 0:K] = high
    x3_ref[:, K : 2 * K] = high
    x3_ref[:, 2 * K :] = low
    obs = own_ref[0:128, :]
    spread = obs - jnp.sum(obs, axis=1, keepdims=True) * (1.0 / K)
    high, low = split(spread)
    own3_ref[:, 0:K] = high
    own3_ref[:, K : 2 * K] = high
    own3_ref[:, 2 * K :] = low
    y_ref[...] = spread.T.astype(BF16)
    right = jnp.concatenate([high, low, high], axis=1)
    tu_ref[0:128, :] = mm_nt(own3_ref[...], right)
    tu_ref[128:, :] = mm_nt(x3_ref[...], right)


def patch_bounds(first):
    swap = first > 32.0
    zero, full = jnp.zeros_like(first), jnp.full_like(first, 64.0)
    lower = [jnp.where(swap, first, zero), jnp.where(swap, zero, first)]
    upper = [jnp.where(swap, full, first) - 1.0, jnp.where(swap, first, full) - 1.0]
    return lower, upper


def observed_places(ref, shift):
    cell = ref[128:129, 0:128].astype(jnp.int32)
    return (cell // 8).astype(F32), (cell % 8).astype(F32) + shift


def localize(orow, ocol, var, lower, upper):
    gap_row = jnp.maximum(jnp.maximum(lower - orow, orow - upper), 0.0) * (1.0 / 16.0)
    gap_col = jnp.maximum(jnp.maximum(-ocol, ocol - 7.0), 0.0) * (1.0 / 8.0)
    return jnp.exp(-gap_row * gap_row - gap_col * gap_col) / var


def side_shift():
    return jnp.where(lax.axis_index("core") == 0, 8.0, -8.0)


def beside_kernel(
    own_ref, obs_ref, x3_ref, own3_ref, turned_ref, near3_ref, tu_ref, gram_ref, y2, g2
):
    obs = obs_ref[0:128, :]
    spread = obs - jnp.sum(obs, axis=1, keepdims=True) * (1.0 / K)
    high, low = split(spread)
    near3_ref[:, 0:K] = high
    near3_ref[:, K : 2 * K] = high
    near3_ref[:, 2 * K :] = low
    right = jnp.concatenate([high, low, high], axis=1)
    tu_ref[0:128, :] = mm_nt(own3_ref[...], right)
    tu_ref[128:256, :] = mm_nt(near3_ref[...], right)
    tu_ref[256:, :] = mm_nt(x3_ref[...], right)
    turned = spread.T.astype(BF16)
    for n in range(2):
        y2[:, 256 * n : 256 * n + 128] = turned_ref[...]
        y2[:, 256 * n + 128 : 256 * n + 256] = turned
    places = [observed_places(own_ref, 0.0), observed_places(obs_ref, side_shift())]
    orow, ocol = (jnp.concatenate(v, axis=1) for v in zip(*places))
    var = jnp.concatenate([own_ref[130:131, 0:128], obs_ref[130:131, 0:128]], axis=1)
    lower, upper = patch_bounds(own_ref[131:132, 0:1])
    g = [localize(orow, ocol, var, lower[p], upper[p]) for p in range(2)]
    g_cols = jnp.concatenate(g + [jnp.zeros((6, 256), F32)], axis=0).T
    yt = jnp.concatenate(
        [own3_ref[:, 0:K].astype(F32) + own3_ref[:, 2 * K :].astype(F32), spread], axis=0
    )
    for p in range(2):
        high, low = split(yt * g_cols[:, p : p + 1])
        g2[0:256, p * K : (p + 1) * K] = high
        g2[256:512, p * K : (p + 1) * K] = low
    for n in range(5):
        cols = slice(n * 256, (n + 1) * 256)
        gram_ref[:, cols] = mm(y2[...], g2[:, cols])


def mm_nt(left, right):
    return lax.dot_general(left, right, (((1,), (1,)), ((), ())), preferred_element_type=F32)


def server_kernel(
    x_ref, own_ref, x3_ref, own3_ref, tu_ref, mean_ref,
    near_ref, near3_ref, ntu_ref, gram_ref, far_ref, out_ref,
    far3, y2, yt3, g2, u_ref, c_ref, d_ref, res
):
    innov, var, orow, ocol = [], [], [], []
    side = side_shift()
    for j, (ref, three) in enumerate(
        ((own_ref, own3_ref), (near_ref, near3_ref), (far_ref, None))
    ):
        obs = ref[0:128, :]
        obs_mean = jnp.sum(obs, axis=1, keepdims=True) * (1.0 / K)
        if three is None:
            spread = obs - obs_mean
            high, low = split(spread)
            far3[:, 0:K] = high
            far3[:, K : 2 * K] = high
            far3[:, 2 * K :] = low
            far_right = jnp.concatenate([high, low, high], axis=1)
            turned = spread.T.astype(BF16)
            y2[:, 0:128] = turned
            y2[:, 128:256] = turned
        else:
            high, low = three[:, 0:K], three[:, 2 * K :]
        for n, part in enumerate((high, low, high)):
            yt3[n * NOBS + j * 128 : n * NOBS + (j + 1) * 128, :] = part
        innov.append(ref[129:130, 0:128] - as_row(obs_mean))
        var.append(ref[130:131, 0:128])
        place = observed_places(ref, (0.0, side, -side)[j])
        orow.append(place[0])
        ocol.append(place[1])
    innov, var, orow, ocol = (jnp.concatenate(v, axis=1) for v in (innov, var, orow, ocol))

    first = own_ref[131:132, 0:1]
    swap_scalar = jnp.max(first) > 32.0
    eye128 = lax.broadcasted_iota(jnp.int32, (128, 128), 0) == lax.broadcasted_iota(
        jnp.int32, (128, 128), 1
    )
    eye = jnp.where(
        lax.broadcasted_iota(jnp.int32, (NOBS, NOBS), 0)
        == lax.broadcasted_iota(jnp.int32, (NOBS, NOBS), 1),
        1.0,
        0.0,
    )
    both = range(2)
    lower, upper = patch_bounds(first)
    sg, sgd, sg_col, sgd_col, diag = [], [], [], [], []
    yt = yt3[0:NOBS, :].astype(F32) + yt3[NOBS : 2 * NOBS, :].astype(F32)
    for p in both:
        g = localize(orow, ocol, var, lower[p], upper[p])
        sg.append(jnp.sqrt(g))
        sgd.append(sg[p] * innov)
        cols = jnp.concatenate([sg[p], sgd[p], g, jnp.zeros((5, NOBS), F32)], axis=0).T
        sg_col.append(cols[:, 0:1])
        sgd_col.append(cols[:, 1:2])
        scaled = yt * cols[:, 2:3]
        diag.append(jnp.sum(scaled * yt, axis=0, keepdims=True))
        high, low = split(scaled[256:384])
        g2[0:128, p * K : (p + 1) * K] = high
        g2[128:256, p * K : (p + 1) * K] = low

    t_own, t_near, t_far = (mm_nt(far_right, ref[...]) for ref in (own3_ref, near3_ref, far3))
    cross = ntu_ref[0:128, :]
    t_mat = jnp.concatenate(
        [
            jnp.concatenate([tu_ref[0:128, :], cross, t_own.T], axis=1),
            jnp.concatenate([cross.T, ntu_ref[128:256, :], t_near.T], axis=1),
            jnp.concatenate([t_own, t_near, t_far], axis=1),
        ],
        axis=0,
    )
    u_ref[:, 0:128] = tu_ref[128:, :]
    u_ref[:, 128:256] = ntu_ref[256:, :]
    u_ref[:, 256:384] = mm_nt(far_right, x3_ref[...]).T

    sums = []
    for n in range(5):
        cols = slice(n * 256, (n + 1) * 256)
        block = jnp.abs(gram_ref[:, cols] + mm(y2[...], g2[:, cols]))
        for half in range(2):
            own = (2 * n + half) % 5
            part = block[:, half * 128 : (half + 1) * 128]
            rows = [part[i * 128 : (i + 1) * 128] for i in range(5)]
            rows[own] = jnp.where(eye128, 0.0, rows[own])
            total = (rows[0] + rows[1]) + (rows[2] + rows[3]) + rows[4]
            sums.append(jnp.sum(total, axis=0, keepdims=True))
    inv, q0, a1, m20, z20, z30 = [], [], [], [], [], []
    for p in both:
        total = jnp.concatenate(sums[5 * p : 5 * p + 5], axis=1) + diag[p]
        bound = (K - 1.0) + jnp.max(total, axis=1, keepdims=True)
        inv.append(1.0 / bound)
        q0.append((K - 1.0) * inv[p])
        a1.append(1.5 - 0.5 * q0[p])
        m20.append(1.5 - 0.5 * q0[p] * a1[p] * a1[p])
        z20.append(a1[p] * m20[p])
        z30.append(z20[p] * (1.5 - 0.5 * q0[p] * z20[p] * z20[p]))
    s = [(sg_col[p] * inv[p]) * t_mat * sg[p] for p in both]
    s_right = [right3(s[p]) for p in both]
    s2 = [mm(left3(s[p]), s_right[p]) for p in both]
    s34 = [mm(left3(s2[p]), jnp.concatenate([s_right[p], right3(s2[p])], axis=1)) for p in both]
    kz2, z2 = [], []
    for p in both:
        s3, s4 = s34[p][:, 0:NOBS], s34[p][:, NOBS:]
        e0 = -0.5 * (a1[p] * a1[p] - q0[p] * a1[p])
        e1 = -0.5 * (0.25 * q0[p] - a1[p])
        c0 = a1[p] * e0 - 0.5 * m20[p]
        c1 = a1[p] * e1 - 0.5 * e0
        c2 = -0.125 * a1[p] - 0.5 * e1
        kz2.append(c0 * eye + c1 * s[p] + c2 * s2[p] + 0.0625 * s3)
        z2.append(z20[p] * eye + c0 * s[p] + c1 * s2[p] + c2 * s3 + 0.0625 * s4)
    z2_right = [right3(z2[p]) for p in both]
    size = (256, 384)
    start = [
        pl.multiple_of(jnp.where(swap_scalar, 256, 0), 128),
        pl.multiple_of(jnp.where(swap_scalar, 0, 128), 128),
    ]
    v = [
        jnp.concatenate(
            [u_ref[pl.ds(start[p], size[p]), :] * sg[p], jnp.broadcast_to(sgd[p], (8, NOBS))],
            axis=0,
        )
        for p in both
    ]
    w1 = [
        mm(
            left3(v[p]),
            jnp.concatenate([right3(z2[p] + q0[p] * kz2[p]), right3(kz2[p])], axis=1),
        )
        for p in both
    ]
    kv = [w1[p][:, NOBS:] for p in both]
    w2 = [mm(left3(w1[p][:, 0:NOBS]), z2_right[p]) for p in both]
    w3 = [mm(left3(w2[p] + (q0[p] * z20[p]) * kv[p]), z2_right[p]) for p in both]
    hv = [(1.5 - 0.5 * q0[p] * z20[p] * z20[p]) * kv[p] - 0.5 * w3[p] for p in both]
    scale = [jnp.sqrt(q0[p]) for p in both]
    for p in (1, 0):
        n = size[p]
        rows = pl.ds(start[p], n)
        u_col = z30[p] * sgd_col[p] + jnp.sum(hv[p][n : n + 1] * s[p], axis=1, keepdims=True)
        su = jnp.sum(u_col * s[p], axis=0, keepdims=True)
        u = as_row(u_col)
        drift = inv[p] * jnp.sum(
            (z30[p] * u) * v[p][0:n] + su * hv[p][0:n], axis=1, keepdims=True
        )
        part = hv[p][0:n] * (sg[p] * (scale[p] * inv[p]))
        if p == 0:
            cell_row = (
                (lax.broadcasted_iota(jnp.int32, (n, 1), 0) + start[p]) // 8
            ).astype(F32)
            inside = (cell_row >= lower[0]) & (cell_row <= upper[0])
            part = jnp.where(inside, part, c_ref[rows, :])
            drift = jnp.where(inside, drift, d_ref[rows, :])
        c_ref[rows, :] = part
        d_ref[rows, :] = drift
    cell_row = (lax.broadcasted_iota(jnp.int32, (CELLS, 1), 0) // 8).astype(F32)
    inside = (cell_row >= lower[0]) & (cell_row <= upper[0])
    coef = jnp.where(inside, scale[0] * z30[0], scale[1] * z30[1])
    base = mean_ref[...] * (1.0 - coef) + d_ref[...]
    low = lane_iota() < 64
    for i in range(4):
        rows = slice(i * 128, (i + 1) * 128)
        res[rows, :] = (
            coef[rows] * x_ref[rows, :] + base[rows] + mm(left3(c_ref[rows, :]), yt3[...])
        )
        for l in range(4 * i, 4 * i + 4):

            def block(r, k):
                return res[32 * l + 8 * r : 32 * l + 8 * r + 8, k * 128 : (k + 1) * 128]

            for half in range(2):
                for k in range(4):
                    outs = pair_swap(block(2 * half, k), block(2 * half + 1, k))
                    for j, out in enumerate(outs):
                        dest = (2 * (2 * (k % 2) + j) + k // 2) * 16 + l
                        out_ref[dest, 2 * half : 2 * half + 2, :, :] = out.reshape(2, 4, 128)
            ends = [block(r, 4) for r in range(4)]
            for j, out in enumerate(block_transpose(ends, 16)):
                turned = roll(out, 64)
                first_half = jnp.where(low, out, pltpu.roll(turned, 4, 0))
                second_half = jnp.where(low, turned, pltpu.roll(out, 4, 0))
                out_ref[2 * j * 16 + l, 4, :, :] = first_half[0:4]
                out_ref[(2 * j + 1) * 16 + l, 4, :, :] = second_half[0:4]


def unpack_kernel(recv_ref, out_ref):
    for g in range(8):
        cols = slice(g * 128, (g + 1) * 128)
        for b in range(3):
            parts = []
            for w in range(16):
                src = PLACE[16 * g + w]
                if b < 2:
                    parts.append(recv_ref[src, 2 * b : 2 * b + 2, :, :].reshape(8, 128))
                else:
                    part = recv_ref[src, 4, :, :]
                    parts.append(jnp.concatenate([part, roll(part, 64)], axis=0))
            block = jnp.concatenate(parts, axis=0).T
            if b < 2:
                out_ref[0:64, 2 * b, cols] = block[0:64]
                out_ref[0:64, 2 * b + 1, cols] = block[64:128]
            else:
                for r in range(4):
                    out_ref[64:80, r, cols] = block[16 * r : 16 * r + 16]


WHOLE = pl.BlockSpec(memory_space=pltpu.VMEM)
THERE = pl.BlockSpec(memory_space=pltpu.HBM)


def call(kernel, out_shape, *args, scratch=(), name=None, vmem=16, ins=None, outs=None, cost=None):
    return pl.pallas_call(
        kernel,
        out_shape=out_shape,
        in_specs=ins or [WHOLE] * len(args),
        out_specs=outs or jax.tree.map(lambda _: WHOLE, out_shape),
        scratch_shapes=scratch,
        compiler_params=pltpu.CompilerParams(vmem_limit_bytes=vmem * 1024 * 1024),
        cost_estimate=cost,
        name=name,
    )(*args)


def shaped(*shape, dtype=F32):
    return jax.ShapeDtypeStruct(shape, dtype)


def per_device(ensemble, obs_cell, obs_value, obs_var, patch_rows):
    chunks = call(
        pack_kernel,
        shaped(64, 16, 4, 128),
        ensemble,
        obs_cell,
        obs_value,
        obs_var,
        patch_rows,
        scratch=[
            pltpu.VMEM((MEM, 4, 1024), F32),
            pltpu.VMEM((4, MEM, 1024), F32),
            pltpu.VMEM((64, 16, 4, 128), F32),
            pltpu.VMEM((1, 128), jnp.int32),
            pltpu.VMEM((1, 128), F32),
            pltpu.VMEM((1, 128), F32),
            pltpu.VMEM((1, 2), jnp.int32),
            pltpu.SemaphoreType.DMA((10,)),
            pltpu.SemaphoreType.DMA((4,)),
            pltpu.SemaphoreType.DMA((16,)),
        ],
        ins=[THERE] * 5,
        outs=THERE,
        name="pack",
        vmem=58,
    )
    recv = lax.all_to_all(chunks, CHIPS, split_axis=0, concat_axis=0, tiled=True)
    other = call(place_kernel, shaped(65, 16, 384), recv, name="place", vmem=4)
    other = lax.ppermute(other, "core", [(0, 1), (1, 0)])
    part, tail = call(
        forecast_own_kernel,
        (shaped(CELLS, 256), shaped(65, 16, 128)),
        recv,
        scratch=[pltpu.VMEM((66, 16, 256), F32)] * 2,
        name="forecast_own",
        vmem=6,
        cost=pl.CostEstimate(flops=8 << 20, bytes_accessed=8 << 20, transcendentals=0),
    )
    x, obs = call(
        forecast_kernel,
        (shaped(CELLS, K), shaped(136, K)),
        tail,
        other,
        part,
        scratch=[pltpu.VMEM((66, 16, 384), F32)] * 2,
        name="forecast",
        vmem=10,
    )
    far_pairs = [(PLACE[s], PLACE[(s + 1) % 128]) for s in range(1, 128, 2)]
    far = lax.ppermute(obs, ALL, far_pairs + [(b, a) for a, b in far_pairs])
    near = lax.ppermute(obs, "core", [(0, 1), (1, 0)])
    own = call(
        prepare_kernel,
        (
            shaped(CELLS, 3 * K, dtype=BF16),
            shaped(128, 3 * K, dtype=BF16),
            shaped(K, 128, dtype=BF16),
            shaped(128 + CELLS, 128),
            shaped(CELLS, 1),
        ),
        x,
        obs,
        name="prepare",
        vmem=6,
        cost=pl.CostEstimate(flops=2 * K * K * 128 * 3, bytes_accessed=8 << 20, transcendentals=0),
    )
    x3, own3, turned, tu, mean = own
    beside = call(
        beside_kernel,
        (
            shaped(128, 3 * K, dtype=BF16),
            shaped(256 + CELLS, 128),
            shaped(K, 2 * K),
        ),
        obs,
        near,
        x3,
        own3,
        turned,
        scratch=[pltpu.VMEM((K, 512), BF16), pltpu.VMEM((512, 2 * K), BF16)],
        name="beside",
        vmem=10,
        cost=pl.CostEstimate(flops=2 * K * K * 512 * 3, bytes_accessed=8 << 20, transcendentals=0),
    )
    back = call(
        server_kernel,
        shaped(128, 5, 4, 128),
        x,
        obs,
        x3,
        own3,
        tu,
        mean,
        near,
        *beside,
        far,
        scratch=[
            pltpu.VMEM((128, 3 * K), BF16),
            pltpu.VMEM((K, 256), BF16),
            pltpu.VMEM((3 * NOBS, K), BF16),
            pltpu.VMEM((256, 2 * K), BF16),
            pltpu.VMEM((CELLS, NOBS), F32),
            pltpu.VMEM((CELLS, NOBS), F32),
            pltpu.VMEM((CELLS, 1), F32),
            pltpu.VMEM((CELLS, K), F32),
        ],
        name="server",
        vmem=32,
    )
    back = lax.all_to_all(back, ALL, split_axis=0, concat_axis=0, tiled=True)
    return call(unpack_kernel, shaped(MEM, 4, 1024), back, name="unpack", vmem=6)


def solution(mesh):
    split_mesh = Mesh(mesh.devices.reshape(4, 2, 16), ALL)
    in_specs = (P(("y", "core"), "lat", None),) + (P(ALL, None),) * 4
    return jax.shard_map(
        per_device,
        mesh=split_mesh,
        in_specs=in_specs,
        out_specs=P(("y", "core"), "lat", None),
        check_vma=False,
    )
```

```python
import functools

import jax
import jax.numpy as jnp
import numpy as np
from jax import lax
from jax.experimental import pallas as pl
from jax.experimental.pallas import tpu as pltpu
from jax.sharding import Mesh
from jax.sharding import PartitionSpec as P

ALL = ("y", "core", "lat")
CHIPS = ("y", "lat")
K = 640
MEM = 80
NOBS = 384
CELLS = 512
F32 = jnp.float32
BF16 = jnp.bfloat16


def strip_places():
    columns = []
    for x in range(4):
        for y in range(4) if x % 2 == 0 else range(3, -1, -1):
            columns.append((x, y))
    places, z = [], 0
    for x, y in columns:
        for k in range(4):
            for core in range(2):
                places.append((y * 2 + core) * 16 + x * 4 + (z + k) % 4)
        z = (z + 3) % 4
    return places


PLACE = strip_places()
CHIP = [PLACE[2 * j] // 32 * 16 + PLACE[2 * j] % 16 for j in range(64)]


def lane_iota(rows=8):
    return lax.broadcasted_iota(jnp.int32, (rows, 128), 1)


def roll(value, shift):
    return pltpu.roll(value, shift % value.shape[-1], value.ndim - 1)


def block_transpose(values, size):
    values = list(values)
    count = len(values)
    lane = lane_iota()
    dist = 1
    while dist < count:
        low = (lane // (size * dist)) % 2 == 0
        for i in range(count):
            if i & dist:
                continue
            a, b = values[i], values[i + dist]
            values[i] = jnp.where(low, a, roll(b, size * dist))
            values[i + dist] = jnp.where(low, roll(a, -size * dist), b)
        dist *= 2
    return values


def pair_swap(a, b):
    low = lane_iota() < 64
    cross = roll(jnp.where(low, b, a), 64)
    return jnp.where(low, a, cross), jnp.where(low, cross, b)


def pack_kernel(
    ens_hbm, cell_hbm, value_hbm, var_hbm, rows_hbm, out_hbm,
    ens, moved, stage, cell, value, var, rows_v, ens_sem, meta_sem, out_sem
):
    loads = [
        pltpu.make_async_copy(ens_hbm.at[8 * i : 8 * i + 8], ens.at[8 * i : 8 * i + 8], ens_sem.at[i])
        for i in range(10)
    ]
    smalls = [
        pltpu.make_async_copy(src, dst, meta_sem.at[i])
        for i, (src, dst) in enumerate(
            ((cell_hbm, cell), (value_hbm, value), (var_hbm, var), (rows_hbm, rows_v))
        )
    ]
    for copy in loads + smalls:
        copy.start()
    for i in range(10):
        loads[i].wait()
        rows = slice(8 * i, 8 * i + 8)
        for r in range(4):
            moved[r, rows, :] = roll(0.1 * ens[rows, r, :], 4)
    for copy in smalls:
        copy.wait()
    meta = jnp.concatenate(
        [
            cell[...].astype(F32),
            value[...],
            var[...],
            jnp.broadcast_to(rows_v[0:1, 0:1].astype(F32), (1, 128)),
        ],
        axis=0,
    )
    for chip in range(64):
        stage[chip, 15, :, :] = meta
    stores = []

    def send(column):
        base = min(CHIP[4 * column : 4 * column + 4])
        part = slice(base, base + 4)
        stores.append(
            pltpu.make_async_copy(stage.at[part], out_hbm.at[part], out_sem.at[column])
        )
        stores[-1].start()

    low = lane_iota() < 64

    def put(j, t, pair):
        for h in range(2):
            tile = 4 * t + 2 * h
            stage[CHIP[j % 64], tile : tile + 2, :, :] = pair[h].reshape(2, 4, 128)

    for g in range(8):
        cols = slice(g * 128, (g + 1) * 128)
        main = [
            jnp.concatenate([moved[2 * h, 0:64, cols], moved[2 * h + 1, 0:64, cols]], axis=0).T
            for h in range(2)
        ]
        tails = jnp.concatenate([moved[r, 64:80, cols] for r in range(4)] * 2, axis=0).T
        for w in range(16):
            rows = slice(8 * w, 8 * w + 8)
            pair = [main[0][rows], main[1][rows]]
            tail = tails[rows]
            j = 8 * g + w // 2
            if w % 2 == 0:
                put(j - 1, 2, pair)
                put(j, 0, pair)
                both = jnp.where(low, tail, pltpu.roll(tail, 4, 0))
                stage[CHIP[(j - 1) % 64], 14, :, :] = both[0:4]
            else:
                put(j, 1, pair)
                both = jnp.where(low, tails[8 * w - 8 : 8 * w], tail)
                stage[CHIP[j], 12:14, :, :] = both.reshape(2, 4, 128)
            if w % 8 == 0 and j > 0:
                send(j // 4 - 1)
    send(15)
    for copy in stores:
        copy.wait()


def chip_pair():
    y, lat = lax.axis_index("y"), lax.axis_index("lat")
    x, z = lat // 4, lat % 4
    column = x * 4 + jnp.where(x % 2 == 0, y, 3 - y)
    return 4 * column + (z + column) % 4


def place_tiles(recv_ref, core, first, put):
    tiles = (first, first + 1)
    last = slice(256, 384)

    def place(l, carry):
        def vreg(y, tile):
            return recv_ref[y * 16 + l, tile : tile + 2, :, :].reshape(8, 128)

        for t in tiles:
            for h in range(2):
                for k in range(2):
                    tile = 4 * t + 2 * h
                    outs = pair_swap(vreg(2 * k, tile), vreg(2 * k + 1, tile))
                    for j, out in enumerate(outs):
                        put(4 * l + 2 * h + j, t - first, slice(128 * k, 128 * k + 128), out)
        outs = block_transpose([vreg(y, 12) for y in range(4)], 16)
        for r, out in enumerate(outs):
            turned = roll(out, 64)
            if 0 in tiles:
                put(4 * l + r, 0 - first, last, turned if core else out)
            put(4 * l + r, 1 - first, last, out if core else turned)
        if 2 in tiles:
            ends = []
            for y in range(4):
                part = recv_ref[y * 16 + l, 14, :, :]
                ends.append(jnp.concatenate([part, roll(part, 64)], axis=0))
            for r, out in enumerate(block_transpose(ends, 16)):
                put(4 * l + r, 2 - first, last, roll(out, 64) if core else out)
        return carry

    lax.fori_loop(0, 16, place, 0, unroll=4)


def for_core(run):
    core = lax.axis_index("core")
    for value in range(2):
        pl.when(core == value)(functools.partial(run, value))


def observations(recv_ref, strip):
    return recv_ref[strip // 32 * 16 + strip % 16, 15, :, :]


def place_kernel(recv_ref, send_ref):
    def run(core):
        def put(row, half, cols, value):
            send_ref[row, 8 * half : 8 * half + 8, cols] = value

        place_tiles(recv_ref, core, 1 - core, put)
        send_ref[64, 0:4, 0:128] = observations(recv_ref, 2 * chip_pair() + 1 - core)

    for_core(run)


def advance(src, row):
    n, c, s = ((src[row + d, 0:8, :], src[row + d, 8:16, :]) for d in (-1, 0, 1))
    column = lax.broadcasted_iota(jnp.int32, c[0].shape, 0)
    up = [pltpu.roll(v, 7, 0) for v in c]
    down = [pltpu.roll(v, 1, 0) for v in c]
    east = (jnp.where(column == 7, up[1], up[0]), up[1])
    west = (down[0], jnp.where(column == 0, down[0], down[1]))
    return [
        0.4 * ((n[h] + s[h]) + 0.125 * (east[h] + west[h])) + c[h] * ((west[h] - east[h]) + 0.1)
        for h in range(2)
    ]


def march(fa, fb, finish):
    for buf in (fa, fb):
        buf[0] = jnp.zeros(buf.shape[1:], F32)
        buf[65] = jnp.zeros(buf.shape[1:], F32)
    for src, dst in ((fa, fb), (fb, fa), (fa, fb)):

        def move(i, carry):
            for h, value in enumerate(advance(src, i + 1)):
                dst[i + 1, 8 * h : 8 * h + 8, :] = value
            return carry

        lax.fori_loop(0, 64, move, 0, unroll=8)

    def last(i, carry):
        a, b = (pltpu.roll(value, 4, 0) for value in advance(fb, i + 1))
        column = lax.broadcasted_iota(jnp.int32, a.shape, 0)
        finish(i, 10.0 * jnp.where(column < 4, a, b))
        return carry

    lax.fori_loop(0, 64, last, 0, unroll=8)


def forecast_own_kernel(recv_ref, x_ref, tail_ref, fa, fb):
    def run(core):
        def put(row, half, cols, value):
            rows = slice(8 * half, 8 * half + 8)
            if cols.start < 256:
                fa[row + 1, rows, cols] = value
            else:
                tail_ref[row, rows, :] = value

        place_tiles(recv_ref, core, core, put)
        tail_ref[64, 0:4, :] = observations(recv_ref, 2 * chip_pair() + core)

    for_core(run)

    def finish(i, value):
        x_ref[pl.ds(pl.multiple_of(i * 8, 8), 8), :] = value

    march(fa, fb, finish)


def forecast_kernel(tail_ref, other_ref, part_ref, x_ref, obs_ref, fa, fb):
    core = lax.axis_index("core")
    low_core = core == 0
    low = lax.broadcasted_iota(jnp.int32, (16, 128), 1) < 64
    own_low = jnp.where(low_core, 1, 0)
    pick_own = low == (jnp.broadcast_to(own_low, (16, 128)) > 0)

    def load(i, carry):
        fa[i + 1, :, 0:256] = other_ref[i, :, 0:256]
        fa[i + 1, :, 256:384] = jnp.where(pick_own, tail_ref[i], other_ref[i, :, 256:384])
        return carry

    lax.fori_loop(0, 64, load, 0, unroll=8)

    def finish(i, value):
        rows = pl.ds(pl.multiple_of(i * 8, 8), 8)
        x_ref[rows, pl.ds(pl.multiple_of((1 - core) * 256, 128), 256)] = value[:, 0:256]
        x_ref[rows, pl.ds(pl.multiple_of(core * 256, 128), 256)] = part_ref[rows, :]
        x_ref[rows, 512:640] = value[:, 256:384]

    march(fa, fb, finish)
    here = jnp.broadcast_to(jnp.where((chip_pair() // 8) % 2 == core, 1, 0), (4, 128)) > 0
    meta = jnp.where(here, tail_ref[64, 0:4, :], other_ref[64, 0:4, 0:128])
    meta = jnp.concatenate([meta, jnp.zeros((4, 128), F32)], axis=0)
    cell = meta.T[:, 0:1]
    pick = jnp.where(
        lax.broadcasted_iota(jnp.int32, (128, CELLS), 1) == cell.astype(jnp.int32), 1.0, 0.0
    ).astype(BF16)
    for cols in (slice(0, 256), slice(256, 512), slice(512, 640)):
        x = x_ref[:, cols]
        x1 = x.astype(BF16)
        rest = x - x1.astype(F32)
        x2 = rest.astype(BF16)
        x3 = (rest - x2.astype(F32)).astype(BF16)
        obs_ref[0:128, cols] = mm(pick, x1) + mm(pick, x2) + mm(pick, x3)
    obs_ref[128:136, :] = jnp.zeros((8, K), F32)
    obs_ref[128:136, 0:128] = meta


def split(value):
    high = value.astype(BF16)
    return high, (value - high.astype(F32)).astype(BF16)


def left3(value):
    high, low = split(value)
    return jnp.concatenate([high, high, low], axis=1)


def right3(value):
    high, low = split(value)
    return jnp.concatenate([high, low, high], axis=0)


def mm(left, right):
    return jnp.dot(left, right, preferred_element_type=F32)


def as_row(column):
    return jnp.broadcast_to(column, (column.shape[0], 128)).T[0:1, :]


def prepare_kernel(x_ref, own_ref, x3_ref, own3_ref, y_ref, tu_ref, mean_ref):
    mean = jnp.sum(x_ref[...], axis=1, keepdims=True) * (1.0 / K)
    mean_ref[...] = mean
    high, low = split(x_ref[...] - mean)
    x3_ref[:, 0:K] = high
    x3_ref[:, K : 2 * K] = high
    x3_ref[:, 2 * K :] = low
    obs = own_ref[0:128, :]
    spread = obs - jnp.sum(obs, axis=1, keepdims=True) * (1.0 / K)
    high, low = split(spread)
    own3_ref[:, 0:K] = high
    own3_ref[:, K : 2 * K] = high
    own3_ref[:, 2 * K :] = low
    y_ref[...] = spread.T.astype(BF16)
    right = jnp.concatenate([high, low, high], axis=1)
    tu_ref[0:128, :] = mm_nt(own3_ref[...], right)
    tu_ref[128:, :] = mm_nt(x3_ref[...], right)


def patch_bounds(first):
    swap = first > 32.0
    zero, full = jnp.zeros_like(first), jnp.full_like(first, 64.0)
    lower = [jnp.where(swap, first, zero), jnp.where(swap, zero, first)]
    upper = [jnp.where(swap, full, first) - 1.0, jnp.where(swap, first, full) - 1.0]
    return lower, upper


def observed_places(ref, shift):
    cell = ref[128:129, 0:128].astype(jnp.int32)
    return (cell // 8).astype(F32), (cell % 8).astype(F32) + shift


def localize(orow, ocol, var, lower, upper):
    gap_row = jnp.maximum(jnp.maximum(lower - orow, orow - upper), 0.0) * (1.0 / 16.0)
    gap_col = jnp.maximum(jnp.maximum(-ocol, ocol - 7.0), 0.0) * (1.0 / 8.0)
    return jnp.exp(-gap_row * gap_row - gap_col * gap_col) / var


def side_shift():
    return jnp.where(lax.axis_index("core") == 0, 8.0, -8.0)


def beside_kernel(
    own_ref, obs_ref, x3_ref, own3_ref, turned_ref, near3_ref, tu_ref, gram_ref, y2, g2
):
    obs = obs_ref[0:128, :]
    spread = obs - jnp.sum(obs, axis=1, keepdims=True) * (1.0 / K)
    high, low = split(spread)
    near3_ref[:, 0:K] = high
    near3_ref[:, K : 2 * K] = high
    near3_ref[:, 2 * K :] = low
    right = jnp.concatenate([high, low, high], axis=1)
    tu_ref[0:128, :] = mm_nt(own3_ref[...], right)
    tu_ref[128:256, :] = mm_nt(near3_ref[...], right)
    tu_ref[256:, :] = mm_nt(x3_ref[...], right)
    turned = spread.T.astype(BF16)
    for n in range(2):
        y2[:, 256 * n : 256 * n + 128] = turned_ref[...]
        y2[:, 256 * n + 128 : 256 * n + 256] = turned
    places = [observed_places(own_ref, 0.0), observed_places(obs_ref, side_shift())]
    orow, ocol = (jnp.concatenate(v, axis=1) for v in zip(*places))
    var = jnp.concatenate([own_ref[130:131, 0:128], obs_ref[130:131, 0:128]], axis=1)
    lower, upper = patch_bounds(own_ref[131:132, 0:1])
    g = [localize(orow, ocol, var, lower[p], upper[p]) for p in range(2)]
    g_cols = jnp.concatenate(g + [jnp.zeros((6, 256), F32)], axis=0).T
    yt = jnp.concatenate(
        [own3_ref[:, 0:K].astype(F32) + own3_ref[:, 2 * K :].astype(F32), spread], axis=0
    )
    for p in range(2):
        high, low = split(yt * g_cols[:, p : p + 1])
        g2[0:256, p * K : (p + 1) * K] = high
        g2[256:512, p * K : (p + 1) * K] = low
    for n in range(5):
        cols = slice(n * 256, (n + 1) * 256)
        gram_ref[:, cols] = mm(y2[...], g2[:, cols])


def mm_nt(left, right):
    return lax.dot_general(left, right, (((1,), (1,)), ((), ())), preferred_element_type=F32)


def server_kernel(
    x_ref, own_ref, x3_ref, own3_ref, tu_ref, mean_ref,
    near_ref, near3_ref, ntu_ref, gram_ref, far_ref, out_ref,
    far3, y2, yt3, g2, u_ref, c_ref, d_ref, res
):
    innov, var, orow, ocol = [], [], [], []
    side = side_shift()
    for j, (ref, three) in enumerate(
        ((own_ref, own3_ref), (near_ref, near3_ref), (far_ref, None))
    ):
        obs = ref[0:128, :]
        obs_mean = jnp.sum(obs, axis=1, keepdims=True) * (1.0 / K)
        if three is None:
            spread = obs - obs_mean
            high, low = split(spread)
            far3[:, 0:K] = high
            far3[:, K : 2 * K] = high
            far3[:, 2 * K :] = low
            far_right = jnp.concatenate([high, low, high], axis=1)
            turned = spread.T.astype(BF16)
            y2[:, 0:128] = turned
            y2[:, 128:256] = turned
        else:
            high, low = three[:, 0:K], three[:, 2 * K :]
        for n, part in enumerate((high, low, high)):
            yt3[n * NOBS + j * 128 : n * NOBS + (j + 1) * 128, :] = part
        innov.append(ref[129:130, 0:128] - as_row(obs_mean))
        var.append(ref[130:131, 0:128])
        place = observed_places(ref, (0.0, side, -side)[j])
        orow.append(place[0])
        ocol.append(place[1])
    innov, var, orow, ocol = (jnp.concatenate(v, axis=1) for v in (innov, var, orow, ocol))

    first = own_ref[131:132, 0:1]
    swap_scalar = jnp.max(first) > 32.0
    eye128 = lax.broadcasted_iota(jnp.int32, (128, 128), 0) == lax.broadcasted_iota(
        jnp.int32, (128, 128), 1
    )
    eye = jnp.where(
        lax.broadcasted_iota(jnp.int32, (NOBS, NOBS), 0)
        == lax.broadcasted_iota(jnp.int32, (NOBS, NOBS), 1),
        1.0,
        0.0,
    )
    both = range(2)
    lower, upper = patch_bounds(first)
    sg, sgd, sg_col, sgd_col, diag = [], [], [], [], []
    yt = yt3[0:NOBS, :].astype(F32) + yt3[NOBS : 2 * NOBS, :].astype(F32)
    for p in both:
        g = localize(orow, ocol, var, lower[p], upper[p])
        sg.append(jnp.sqrt(g))
        sgd.append(sg[p] * innov)
        cols = jnp.concatenate([sg[p], sgd[p], g, jnp.zeros((5, NOBS), F32)], axis=0).T
        sg_col.append(cols[:, 0:1])
        sgd_col.append(cols[:, 1:2])
        scaled = yt * cols[:, 2:3]
        diag.append(jnp.sum(scaled * yt, axis=0, keepdims=True))
        high, low = split(scaled[256:384])
        g2[0:128, p * K : (p + 1) * K] = high
        g2[128:256, p * K : (p + 1) * K] = low

    t_own, t_near, t_far = (mm_nt(far_right, ref[...]) for ref in (own3_ref, near3_ref, far3))
    cross = ntu_ref[0:128, :]
    t_mat = jnp.concatenate(
        [
            jnp.concatenate([tu_ref[0:128, :], cross, t_own.T], axis=1),
            jnp.concatenate([cross.T, ntu_ref[128:256, :], t_near.T], axis=1),
            jnp.concatenate([t_own, t_near, t_far], axis=1),
        ],
        axis=0,
    )
    u_ref[:, 0:128] = tu_ref[128:, :]
    u_ref[:, 128:256] = ntu_ref[256:, :]
    u_ref[:, 256:384] = mm_nt(far_right, x3_ref[...]).T

    sums = []
    for n in range(5):
        cols = slice(n * 256, (n + 1) * 256)
        block = jnp.abs(gram_ref[:, cols] + mm(y2[...], g2[:, cols]))
        for half in range(2):
            own = (2 * n + half) % 5
            part = block[:, half * 128 : (half + 1) * 128]
            rows = [part[i * 128 : (i + 1) * 128] for i in range(5)]
            rows[own] = jnp.where(eye128, 0.0, rows[own])
            total = (rows[0] + rows[1]) + (rows[2] + rows[3]) + rows[4]
            sums.append(jnp.sum(total, axis=0, keepdims=True))
    inv, q0, a1, m20, z20, z30 = [], [], [], [], [], []
    for p in both:
        total = jnp.concatenate(sums[5 * p : 5 * p + 5], axis=1) + diag[p]
        bound = (K - 1.0) + jnp.max(total, axis=1, keepdims=True)
        inv.append(1.0 / bound)
        q0.append((K - 1.0) * inv[p])
        a1.append(1.5 - 0.5 * q0[p])
        m20.append(1.5 - 0.5 * q0[p] * a1[p] * a1[p])
        z20.append(a1[p] * m20[p])
        z30.append(z20[p] * (1.5 - 0.5 * q0[p] * z20[p] * z20[p]))
    s = [(sg_col[p] * inv[p]) * t_mat * sg[p] for p in both]
    s_right = [right3(s[p]) for p in both]
    s2 = [mm(left3(s[p]), s_right[p]) for p in both]
    s34 = [mm(left3(s2[p]), jnp.concatenate([s_right[p], right3(s2[p])], axis=1)) for p in both]
    kz2, z2 = [], []
    for p in both:
        s3, s4 = s34[p][:, 0:NOBS], s34[p][:, NOBS:]
        e0 = -0.5 * (a1[p] * a1[p] - q0[p] * a1[p])
        e1 = -0.5 * (0.25 * q0[p] - a1[p])
        c0 = a1[p] * e0 - 0.5 * m20[p]
        c1 = a1[p] * e1 - 0.5 * e0
        c2 = -0.125 * a1[p] - 0.5 * e1
        kz2.append(c0 * eye + c1 * s[p] + c2 * s2[p] + 0.0625 * s3)
        z2.append(z20[p] * eye + c0 * s[p] + c1 * s2[p] + c2 * s3 + 0.0625 * s4)
    z2_right = [right3(z2[p]) for p in both]
    size = (256, 384)
    start = [
        pl.multiple_of(jnp.where(swap_scalar, 256, 0), 128),
        pl.multiple_of(jnp.where(swap_scalar, 0, 128), 128),
    ]
    v = [
        jnp.concatenate(
            [u_ref[pl.ds(start[p], size[p]), :] * sg[p], jnp.broadcast_to(sgd[p], (8, NOBS))],
            axis=0,
        )
        for p in both
    ]
    w1 = [
        mm(
            left3(v[p]),
            jnp.concatenate([right3(z2[p] + q0[p] * kz2[p]), right3(kz2[p])], axis=1),
        )
        for p in both
    ]
    kv = [w1[p][:, NOBS:] for p in both]
    w2 = [mm(left3(w1[p][:, 0:NOBS]), z2_right[p]) for p in both]
    w3 = [mm(left3(w2[p] + (q0[p] * z20[p]) * kv[p]), z2_right[p]) for p in both]
    hv = [(1.5 - 0.5 * q0[p] * z20[p] * z20[p]) * kv[p] - 0.5 * w3[p] for p in both]
    scale = [jnp.sqrt(q0[p]) for p in both]
    for p in (1, 0):
        n = size[p]
        rows = pl.ds(start[p], n)
        u_col = z30[p] * sgd_col[p] + jnp.sum(hv[p][n : n + 1] * s[p], axis=1, keepdims=True)
        su = jnp.sum(u_col * s[p], axis=0, keepdims=True)
        u = as_row(u_col)
        drift = inv[p] * jnp.sum(
            (z30[p] * u) * v[p][0:n] + su * hv[p][0:n], axis=1, keepdims=True
        )
        part = hv[p][0:n] * (sg[p] * (scale[p] * inv[p]))
        if p == 0:
            cell_row = (
                (lax.broadcasted_iota(jnp.int32, (n, 1), 0) + start[p]) // 8
            ).astype(F32)
            inside = (cell_row >= lower[0]) & (cell_row <= upper[0])
            part = jnp.where(inside, part, c_ref[rows, :])
            drift = jnp.where(inside, drift, d_ref[rows, :])
        c_ref[rows, :] = part
        d_ref[rows, :] = drift
    cell_row = (lax.broadcasted_iota(jnp.int32, (CELLS, 1), 0) // 8).astype(F32)
    inside = (cell_row >= lower[0]) & (cell_row <= upper[0])
    coef = jnp.where(inside, scale[0] * z30[0], scale[1] * z30[1])
    base = mean_ref[...] * (1.0 - coef) + d_ref[...]
    low = lane_iota() < 64
    for i in range(4):
        rows = slice(i * 128, (i + 1) * 128)
        res[rows, :] = (
            coef[rows] * x_ref[rows, :] + base[rows] + mm(left3(c_ref[rows, :]), yt3[...])
        )
        for l in range(4 * i, 4 * i + 4):

            def block(r, k):
                return res[32 * l + 8 * r : 32 * l + 8 * r + 8, k * 128 : (k + 1) * 128]

            for half in range(2):
                for k in range(4):
                    outs = pair_swap(block(2 * half, k), block(2 * half + 1, k))
                    for j, out in enumerate(outs):
                        dest = (2 * (2 * (k % 2) + j) + k // 2) * 16 + l
                        out_ref[dest, 2 * half : 2 * half + 2, :, :] = out.reshape(2, 4, 128)
            ends = [block(r, 4) for r in range(4)]
            for j, out in enumerate(block_transpose(ends, 16)):
                turned = roll(out, 64)
                first_half = jnp.where(low, out, pltpu.roll(turned, 4, 0))
                second_half = jnp.where(low, turned, pltpu.roll(out, 4, 0))
                out_ref[2 * j * 16 + l, 4, :, :] = first_half[0:4]
                out_ref[(2 * j + 1) * 16 + l, 4, :, :] = second_half[0:4]


def unpack_kernel(recv_ref, out_ref):
    for g in range(8):
        cols = slice(g * 128, (g + 1) * 128)
        for b in range(3):
            parts = []
            for w in range(16):
                src = PLACE[16 * g + w]
                if b < 2:
                    parts.append(recv_ref[src, 2 * b : 2 * b + 2, :, :].reshape(8, 128))
                else:
                    part = recv_ref[src, 4, :, :]
                    parts.append(jnp.concatenate([part, roll(part, 64)], axis=0))
            block = jnp.concatenate(parts, axis=0).T
            if b < 2:
                out_ref[0:64, 2 * b, cols] = block[0:64]
                out_ref[0:64, 2 * b + 1, cols] = block[64:128]
            else:
                for r in range(4):
                    out_ref[64:80, r, cols] = block[16 * r : 16 * r + 16]


WHOLE = pl.BlockSpec(memory_space=pltpu.VMEM)
THERE = pl.BlockSpec(memory_space=pltpu.HBM)


def call(kernel, out_shape, *args, scratch=(), name=None, vmem=16, ins=None, outs=None, cost=None):
    return pl.pallas_call(
        kernel,
        out_shape=out_shape,
        in_specs=ins or [WHOLE] * len(args),
        out_specs=outs or jax.tree.map(lambda _: WHOLE, out_shape),
        scratch_shapes=scratch,
        compiler_params=pltpu.CompilerParams(vmem_limit_bytes=vmem * 1024 * 1024),
        cost_estimate=cost,
        name=name,
    )(*args)


def shaped(*shape, dtype=F32):
    return jax.ShapeDtypeStruct(shape, dtype)


def per_device(ensemble, obs_cell, obs_value, obs_var, patch_rows):
    chunks = call(
        pack_kernel,
        shaped(64, 16, 4, 128),
        ensemble,
        obs_cell,
        obs_value,
        obs_var,
        patch_rows,
        scratch=[
            pltpu.VMEM((MEM, 4, 1024), F32),
            pltpu.VMEM((4, MEM, 1024), F32),
            pltpu.VMEM((64, 16, 4, 128), F32),
            pltpu.VMEM((1, 128), jnp.int32),
            pltpu.VMEM((1, 128), F32),
            pltpu.VMEM((1, 128), F32),
            pltpu.VMEM((1, 2), jnp.int32),
            pltpu.SemaphoreType.DMA((10,)),
            pltpu.SemaphoreType.DMA((4,)),
            pltpu.SemaphoreType.DMA((16,)),
        ],
        ins=[THERE] * 5,
        outs=THERE,
        name="pack",
        vmem=58,
    )
    recv = lax.all_to_all(chunks, CHIPS, split_axis=0, concat_axis=0, tiled=True)
    other = call(place_kernel, shaped(65, 16, 384), recv, name="place", vmem=4)
    other = lax.ppermute(other, "core", [(0, 1), (1, 0)])
    part, tail = call(
        forecast_own_kernel,
        (shaped(CELLS, 256), shaped(65, 16, 128)),
        recv,
        scratch=[pltpu.VMEM((66, 16, 256), F32)] * 2,
        name="forecast_own",
        vmem=6,
        cost=pl.CostEstimate(flops=8 << 20, bytes_accessed=8 << 20, transcendentals=0),
    )
    x, obs = call(
        forecast_kernel,
        (shaped(CELLS, K), shaped(136, K)),
        tail,
        other,
        part,
        scratch=[pltpu.VMEM((66, 16, 384), F32)] * 2,
        name="forecast",
        vmem=10,
    )
    far_pairs = [(PLACE[s], PLACE[(s + 1) % 128]) for s in range(1, 128, 2)]
    far = lax.ppermute(obs, ALL, far_pairs + [(b, a) for a, b in far_pairs])
    near = lax.ppermute(obs, "core", [(0, 1), (1, 0)])
    own = call(
        prepare_kernel,
        (
            shaped(CELLS, 3 * K, dtype=BF16),
            shaped(128, 3 * K, dtype=BF16),
            shaped(K, 128, dtype=BF16),
            shaped(128 + CELLS, 128),
            shaped(CELLS, 1),
        ),
        x,
        obs,
        name="prepare",
        vmem=6,
        cost=pl.CostEstimate(flops=2 * K * K * 128 * 3, bytes_accessed=8 << 20, transcendentals=0),
    )
    x3, own3, turned, tu, mean = own
    beside = call(
        beside_kernel,
        (
            shaped(128, 3 * K, dtype=BF16),
            shaped(256 + CELLS, 128),
            shaped(K, 2 * K),
        ),
        obs,
        near,
        x3,
        own3,
        turned,
        scratch=[pltpu.VMEM((K, 512), BF16), pltpu.VMEM((512, 2 * K), BF16)],
        name="beside",
        vmem=10,
        cost=pl.CostEstimate(flops=2 * K * K * 512 * 3, bytes_accessed=8 << 20, transcendentals=0),
    )
    back = call(
        server_kernel,
        shaped(128, 5, 4, 128),
        x,
        obs,
        x3,
        own3,
        tu,
        mean,
        near,
        *beside,
        far,
        scratch=[
            pltpu.VMEM((128, 3 * K), BF16),
            pltpu.VMEM((K, 256), BF16),
            pltpu.VMEM((3 * NOBS, K), BF16),
            pltpu.VMEM((256, 2 * K), BF16),
            pltpu.VMEM((CELLS, NOBS), F32),
            pltpu.VMEM((CELLS, NOBS), F32),
            pltpu.VMEM((CELLS, 1), F32),
            pltpu.VMEM((CELLS, K), F32),
        ],
        name="server",
        vmem=32,
    )
    back = lax.all_to_all(back, ALL, split_axis=0, concat_axis=0, tiled=True)
    return call(unpack_kernel, shaped(MEM, 4, 1024), back, name="unpack", vmem=6)


def solution(mesh):
    split_mesh = Mesh(mesh.devices.reshape(4, 2, 16), ALL)
    in_specs = (P(("y", "core"), "lat", None),) + (P(ALL, None),) * 4
    return jax.shard_map(
        per_device,
        mesh=split_mesh,
        in_specs=in_specs,
        out_specs=P(("y", "core"), "lat", None),
        check_vma=False,
    )
```
